512 devices in a mesh: gx: 32 (over z, core), gy: 16 (over y, x).
Axes of the slice: x: 4, y: 4, z: 16, core: 2. Of those that a mesh axis runs over, the one named last changes fastest.
Arguments:
- density: float32 [4096, 32, 4096], P('gx', None, 'gy'), may hold values from -5 to 5
- absorb: float32 [32, 4096], P(None, 'gy'), as said below
Outputs:
- radiance: float32 [3, 32, 4096], P(None, 'gx', 'gy')
- transmit: float32 [32, 4096], P('gx', 'gy')
The draws below stay inside these ranges and needn't reach their ends.
Inputs may be any that keep to these rules, and one draw needn't show every extreme that they name: `absorb`: each ray's coefficient lies between 0.5 / 4096 and 0.05.
All inputs are finite; a program needn't handle non-finite values.
Results may differ from the reference program's by a relative error of at most 0.0003.
Values sent between devices are 32-bit elements; how exact they have to be, the bound alone decides.
A program may use at most 64 MiB of HBM per device.

```python
import jax
import jax.numpy as jnp
from jax import lax

NZ = 32
NX = 4096
NY = 4096


def draw_absorb(key, part):
    lowest = 0.5 / NX
    highest = 0.05
    spread = jax.random.uniform(key, (NZ, NY), jnp.float32)
    quick = lowest * (highest / lowest) ** spread
    return quick


def block_levels(stream_key, extent, pieces, least, top_value):
    loudness = 1.0
    for dim, parts in pieces:
        heights = jax.random.uniform(jax.random.fold_in(jax.random.fold_in(stream_key, 6), dim), (parts,), jnp.float32, least / len(pieces), top_value / len(pieces))
        loudness = loudness * jnp.repeat(jnp.exp(heights), extent[dim] // parts).reshape((-1,) + (1,) * (len(extent) - 1 - dim))
    return loudness


def centred(stream_key, dims, scale, bound, cuts=(), held_as=jnp.bfloat16):
    values = jax.random.normal(stream_key, dims, jnp.float32) * scale
    if len(cuts) > 0:
        values = block_levels(stream_key, dims, cuts, -0.22, 0.18) * values
    return jnp.clip(values, min=-bound, max=bound).astype(held_as)


def setup_inputs(seed: int = 0) -> dict:
    key_list = jax.random.split(jax.random.key(seed), 3)
    density = centred(key_list[0], (NX, NZ, NY), 1.0, 5.0, ((0, 32), (2, 16)), jnp.float32)
    absorb = draw_absorb(jax.random.fold_in(key_list[2], 71), 0)
    return {"density": density, "absorb": absorb}


SLOPES = (2.0, -1.5, 0.8)
OFFSETS = (0.0, 0.5, -0.3)

def slab_plane(density, position):
    inside = (position >= 0) & (position < density.shape[0])
    clamped = jnp.clip(position, 0, density.shape[0] - 1).astype(jnp.int32)
    picked = lax.dynamic_index_in_dim(density, clamped, 0, keepdims=False)
    return jnp.where(inside, picked, jnp.zeros_like(picked))

def reference(density, absorb):
    depth_count = density.shape[0]

    def advance(position, carry):
        optical, colour = carry
        centre = slab_plane(density, position)
        behind = slab_plane(density, position - 1)
        ahead = slab_plane(density, position + 1)
        padded = jnp.pad(centre, 1)
        step_depth = (ahead - behind) * 0.5
        step_row = (padded[2:, 1:-1] - padded[:-2, 1:-1]) * 0.5
        step_col = (padded[1:-1, 2:] - padded[1:-1, :-2]) * 0.5
        facing = 0.48 * step_depth + 0.64 * step_row + 0.6 * step_col
        length = jnp.sqrt(step_depth * step_depth + step_row * step_row + step_col * step_col + 1.0)
        lighting = 0.25 + 0.75 * jnp.maximum(facing, 0.0) / length
        extinct = absorb * jax.nn.softplus(centre)
        weight = jnp.exp(-optical) * (1.0 - jnp.exp(-extinct)) * lighting
        tinted = jnp.stack([weight * jax.nn.sigmoid(slope * centre + offset) for slope, offset in zip(SLOPES, OFFSETS)])
        return (optical + extinct, colour + tinted)
    start = (jnp.zeros(absorb.shape, density.dtype), jnp.zeros((3,) + absorb.shape, density.dtype))
    optical, colour = lax.fori_loop(0, depth_count, advance, start)
    return (colour, jnp.exp(-optical))
```

```python
import jax
import jax.numpy as jnp
from jax import lax
from jax.sharding import PartitionSpec as P

SLOPES = (2.0, -1.5, 0.8)
OFFSETS = (0.0, 0.5, -0.3)


def extended(value, sides, width):
    for axis, dim in sides:
        size, length = (lax.axis_size(axis), value.shape[dim])
        up = [(i, (i + 1) % size) for i in range(size - 1)]
        down = [(j, i) for i, j in up]
        last = lax.slice_in_dim(value, length - width, length, axis=dim)
        first = lax.slice_in_dim(value, 0, width, axis=dim)
        before = lax.ppermute(last, axis, up)
        after = lax.ppermute(first, axis, down)
        value = jnp.concatenate([before, value, after], axis=dim)
    return value


def local(density, absorb):
    padded = extended(density, (("gx", 0), ("gy", 2)), 1)
    step_depth = (padded[2:, :, 1:-1] - padded[:-2, :, 1:-1]) * 0.5
    step_col = (padded[1:-1, :, 2:] - padded[1:-1, :, :-2]) * 0.5
    row_padded = jnp.pad(density, ((0, 0), (1, 1), (0, 0)))
    step_row = (row_padded[:, 2:] - row_padded[:, :-2]) * 0.5
    facing = 0.48 * step_depth + 0.64 * step_row + 0.6 * step_col
    length = jnp.sqrt(step_depth * step_depth + step_row * step_row + step_col * step_col + 1.0)
    lighting = 0.25 + 0.75 * jnp.maximum(facing, 0.0) / length
    extinct = absorb[None] * jax.nn.softplus(density)
    depth_count = density.shape[0]
    depth_index = jnp.arange(depth_count)
    below_mask = (depth_index[:, None] > depth_index[None, :]).astype(jnp.float32)
    prefix = jnp.dot(
        below_mask, extinct.reshape(depth_count, -1), precision=lax.Precision.HIGHEST
    ).reshape(extinct.shape)
    weight = jnp.exp(-prefix) * (1.0 - jnp.exp(-extinct)) * lighting
    local_colour = jnp.stack(
        [
            jnp.sum(weight * jax.nn.sigmoid(slope * density + offset), 0)
            for slope, offset in zip(SLOPES, OFFSETS)
        ]
    )
    optical = jnp.sum(extinct, 0)
    stacked = jnp.concatenate([local_colour, optical[None]], axis=0)
    gathered = lax.all_to_all(stacked, "gx", 1, 1, tiled=True)
    bricks = gathered.shape[1]
    brick_index = jnp.arange(bricks)
    before_mask = (brick_index[:, None] > brick_index[None, :]).astype(jnp.float32)
    front = jnp.dot(before_mask, gathered[3], precision=lax.Precision.HIGHEST)
    colour = jnp.sum(gathered[:3] * jnp.exp(-front)[None], axis=1, keepdims=True)
    total = jnp.sum(gathered[3], axis=0, keepdims=True)
    return (colour, jnp.exp(-total))


def solution(mesh):
    placed = (P("gx", None, "gy"), P(None, "gy"))
    return jax.shard_map(
        local,
        mesh=mesh,
        in_specs=placed,
        out_specs=(P(None, "gx", "gy"), P("gx", "gy")),
        check_vma=False,
    )
```

```python
import functools

import jax
import jax.numpy as jnp
from jax import lax
from jax.experimental import pallas as pl
from jax.experimental.pallas import tpu as pltpu
from jax.sharding import PartitionSpec as P

SLOPES = (2.0, -1.5, 0.8)
OFFSETS = (0.0, 0.5, -0.3)
MESH_ID = pl.DeviceIdType.MESH


def extended(value, sides, width):
    for axis, dim in sides:
        size, length = (lax.axis_size(axis), value.shape[dim])
        up = [(i, (i + 1) % size) for i in range(size - 1)]
        down = [(j, i) for i, j in up]
        last = lax.slice_in_dim(value, length - width, length, axis=dim)
        first = lax.slice_in_dim(value, 0, width, axis=dim)
        before = lax.ppermute(last, axis, up)
        after = lax.ppermute(first, axis, down)
        value = jnp.concatenate([before, value, after], axis=dim)
    return value


def combine_kernel(n, rows, stacked_ref, colour_ref, transmit_ref, recv, send_sems, recv_sems, local_sem):
    me = lax.axis_index("gx")
    col = lax.axis_index("gy")

    def peer_of(i):
        return lax.rem(me + i, n)

    def link(peer, slot):
        return pltpu.make_async_remote_copy(
            src_ref=stacked_ref.at[peer],
            dst_ref=recv.at[slot],
            send_sem=send_sems.at[peer],
            recv_sem=recv_sems.at[slot],
            device_id=(peer, col),
            device_id_type=MESH_ID,
        )

    barrier = pltpu.get_barrier_semaphore()

    def greet(i, carry):
        pl.semaphore_signal(barrier, inc=1, device_id=(peer_of(i), col), device_id_type=MESH_ID)
        return carry

    lax.fori_loop(1, n, greet, 0)
    pl.semaphore_wait(barrier, n - 1)

    def send(i, carry):
        link(peer_of(i), me).start()
        return carry

    lax.fori_loop(1, n, send, 0)
    own = pltpu.make_async_copy(stacked_ref.at[me], recv.at[me], local_sem)
    own.start()
    own.wait()

    def finish(i, carry):
        peer = peer_of(i)
        link(peer, peer).wait_send()
        link(peer, peer).wait_recv()
        return carry

    lax.fori_loop(1, n, finish, 0)

    cols = recv.shape[-1]
    zero = jnp.zeros((rows, cols), jnp.float32)

    def accumulate(d, carry):
        front, c0, c1, c2 = carry
        block = recv[d]
        seen = jnp.exp(-front)
        return (
            front + block[:, 3, :],
            c0 + block[:, 0, :] * seen,
            c1 + block[:, 1, :] * seen,
            c2 + block[:, 2, :] * seen,
        )

    front, c0, c1, c2 = lax.fori_loop(0, n, accumulate, (zero, zero, zero, zero))
    colour_ref[0] = c0
    colour_ref[1] = c1
    colour_ref[2] = c2
    transmit_ref[...] = jnp.exp(-front)


def combine(stacked, n):
    rows, cols = stacked.shape[1], stacked.shape[3]
    vmem = pltpu.MemorySpace.VMEM
    return pl.pallas_call(
        functools.partial(combine_kernel, n, rows),
        out_shape=(
            jax.ShapeDtypeStruct((3, rows, cols), jnp.float32),
            jax.ShapeDtypeStruct((rows, cols), jnp.float32),
        ),
        in_specs=[pl.BlockSpec(memory_space=vmem)],
        out_specs=(pl.BlockSpec(memory_space=vmem), pl.BlockSpec(memory_space=vmem)),
        scratch_shapes=[
            pltpu.VMEM(stacked.shape, jnp.float32),
            pltpu.SemaphoreType.DMA((n,)),
            pltpu.SemaphoreType.DMA((n,)),
            pltpu.SemaphoreType.DMA,
        ],
        compiler_params=pltpu.CompilerParams(collective_id=0, has_side_effects=True),
    )(stacked)


def local(density, absorb):
    padded = extended(density, (("gx", 0), ("gy", 2)), 1)
    step_depth = (padded[2:, :, 1:-1] - padded[:-2, :, 1:-1]) * 0.5
    step_col = (padded[1:-1, :, 2:] - padded[1:-1, :, :-2]) * 0.5
    row_padded = jnp.pad(density, ((0, 0), (1, 1), (0, 0)))
    step_row = (row_padded[:, 2:] - row_padded[:, :-2]) * 0.5
    facing = 0.48 * step_depth + 0.64 * step_row + 0.6 * step_col
    length = jnp.sqrt(step_depth * step_depth + step_row * step_row + step_col * step_col + 1.0)
    lighting = 0.25 + 0.75 * jnp.maximum(facing, 0.0) / length
    extinct = absorb[None] * jax.nn.softplus(density)
    depth_count = density.shape[0]
    depth_index = jnp.arange(depth_count)
    below_mask = (depth_index[:, None] > depth_index[None, :]).astype(jnp.float32)
    prefix = jnp.dot(
        below_mask, extinct.reshape(depth_count, -1), precision=lax.Precision.HIGHEST
    ).reshape(extinct.shape)
    weight = jnp.exp(-prefix) * (1.0 - jnp.exp(-extinct)) * lighting
    parts = [
        jnp.sum(weight * jax.nn.sigmoid(slope * density + offset), 0)
        for slope, offset in zip(SLOPES, OFFSETS)
    ]
    parts.append(jnp.sum(extinct, 0))
    n = lax.axis_size("gx")
    nz, cols = absorb.shape
    stacked = jnp.stack(parts, axis=1).reshape(n, nz // n, 4, cols)
    return combine(stacked, n)


def solution(mesh):
    placed = (P("gx", None, "gy"), P(None, "gy"))
    return jax.shard_map(
        local,
        mesh=mesh,
        in_specs=placed,
        out_specs=(P(None, "gx", "gy"), P("gx", "gy")),
        check_vma=False,
    )
```

```python
import functools

import jax
import jax.numpy as jnp
from jax import lax
from jax.experimental import pallas as pl
from jax.experimental.pallas import tpu as pltpu
from jax.sharding import PartitionSpec as P

SLOPES = (2.0, -1.5, 0.8)
OFFSETS = (0.0, 0.5, -0.3)
MESH_ID = pl.DeviceIdType.MESH


def extended(value, sides, width):
    for axis, dim in sides:
        size, length = (lax.axis_size(axis), value.shape[dim])
        up = [(i, (i + 1) % size) for i in range(size - 1)]
        down = [(j, i) for i, j in up]
        last = lax.slice_in_dim(value, length - width, length, axis=dim)
        first = lax.slice_in_dim(value, 0, width, axis=dim)
        before = lax.ppermute(last, axis, up)
        after = lax.ppermute(first, axis, down)
        value = jnp.concatenate([before, value, after], axis=dim)
    return value


def combine_kernel(n, rows, stacked_ref, colour_ref, transmit_ref, recv, send_sems, recv_sems, local_sem):
    me = lax.axis_index("gx")
    col = lax.axis_index("gy")

    def peer_of(i):
        return lax.rem(me + i, n)

    def link(peer, slot):
        return pltpu.make_async_remote_copy(
            src_ref=stacked_ref.at[peer],
            dst_ref=recv.at[slot],
            send_sem=send_sems.at[peer],
            recv_sem=recv_sems.at[slot],
            device_id=(peer, col),
            device_id_type=MESH_ID,
        )

    barrier = pltpu.get_barrier_semaphore()

    def greet(i, carry):
        pl.semaphore_signal(barrier, inc=1, device_id=(peer_of(i), col), device_id_type=MESH_ID)
        return carry

    lax.fori_loop(1, n, greet, 0)
    pl.semaphore_wait(barrier, n - 1)

    def send(i, carry):
        link(peer_of(i), me).start()
        return carry

    lax.fori_loop(1, n, send, 0)
    own = pltpu.make_async_copy(stacked_ref.at[me], recv.at[me], local_sem)
    own.start()
    own.wait()

    def finish(i, carry):
        peer = peer_of(i)
        link(peer, peer).wait_send()
        link(peer, peer).wait_recv()
        return carry

    lax.fori_loop(1, n, finish, 0)

    cols = colour_ref.shape[-1]
    span = cols // 128
    zero = jnp.zeros((rows * span, 128), jnp.float32)

    def value(block, k):
        pieces = [block[(r * 4 + k) * span:(r * 4 + k + 1) * span] for r in range(rows)]
        return pieces[0] if rows == 1 else jnp.concatenate(pieces, axis=0)

    def accumulate(d, carry):
        front, c0, c1, c2 = carry
        block = recv[d]
        seen = jnp.exp(-front)
        return (
            front + value(block, 3),
            c0 + value(block, 0) * seen,
            c1 + value(block, 1) * seen,
            c2 + value(block, 2) * seen,
        )

    front, c0, c1, c2 = lax.fori_loop(0, n, accumulate, (zero, zero, zero, zero))
    for k, c in enumerate((c0, c1, c2)):
        colour_ref[k] = c.reshape(rows, cols)
    transmit_ref[...] = jnp.exp(-front).reshape(rows, cols)


def combine(stacked, n):
    rows, cols = stacked.shape[1], stacked.shape[3]
    stacked = stacked.reshape(n, rows * 4 * cols // 128, 128)
    vmem = pltpu.MemorySpace.VMEM
    return pl.pallas_call(
        functools.partial(combine_kernel, n, rows),
        out_shape=(
            jax.ShapeDtypeStruct((3, rows, cols), jnp.float32),
            jax.ShapeDtypeStruct((rows, cols), jnp.float32),
        ),
        in_specs=[pl.BlockSpec(memory_space=vmem)],
        out_specs=(pl.BlockSpec(memory_space=vmem), pl.BlockSpec(memory_space=vmem)),
        scratch_shapes=[
            pltpu.VMEM(stacked.shape, jnp.float32),
            pltpu.SemaphoreType.DMA((n,)),
            pltpu.SemaphoreType.DMA((n,)),
            pltpu.SemaphoreType.DMA,
        ],
        compiler_params=pltpu.CompilerParams(collective_id=0, has_side_effects=True),
    )(stacked)


def local(density, absorb):
    padded = extended(density, (("gx", 0), ("gy", 2)), 1)
    step_depth = (padded[2:, :, 1:-1] - padded[:-2, :, 1:-1]) * 0.5
    step_col = (padded[1:-1, :, 2:] - padded[1:-1, :, :-2]) * 0.5
    row_padded = jnp.pad(density, ((0, 0), (1, 1), (0, 0)))
    step_row = (row_padded[:, 2:] - row_padded[:, :-2]) * 0.5
    facing = 0.48 * step_depth + 0.64 * step_row + 0.6 * step_col
    length = jnp.sqrt(step_depth * step_depth + step_row * step_row + step_col * step_col + 1.0)
    lighting = 0.25 + 0.75 * jnp.maximum(facing, 0.0) / length
    extinct = absorb[None] * jax.nn.softplus(density)
    depth_count = density.shape[0]
    depth_index = jnp.arange(depth_count)
    below_mask = (depth_index[:, None] > depth_index[None, :]).astype(jnp.float32)
    prefix = jnp.dot(
        below_mask, extinct.reshape(depth_count, -1), precision=lax.Precision.HIGHEST
    ).reshape(extinct.shape)
    weight = jnp.exp(-prefix) * (1.0 - jnp.exp(-extinct)) * lighting
    parts = [
        jnp.sum(weight * jax.nn.sigmoid(slope * density + offset), 0)
        for slope, offset in zip(SLOPES, OFFSETS)
    ]
    parts.append(jnp.sum(extinct, 0))
    n = lax.axis_size("gx")
    nz, cols = absorb.shape
    stacked = jnp.stack(parts, axis=1).reshape(n, nz // n, 4, cols)
    return combine(stacked, n)


def solution(mesh):
    placed = (P("gx", None, "gy"), P(None, "gy"))
    return jax.shard_map(
        local,
        mesh=mesh,
        in_specs=placed,
        out_specs=(P(None, "gx", "gy"), P("gx", "gy")),
        check_vma=False,
    )
```

```python
import functools

import jax
import jax.numpy as jnp
from jax import lax
from jax.experimental import pallas as pl
from jax.experimental.pallas import tpu as pltpu
from jax.sharding import PartitionSpec as P

SLOPES = (2.0, -1.5, 0.8)
OFFSETS = (0.0, 0.5, -0.3)
MESH_ID = pl.DeviceIdType.MESH


def combine_kernel(n, rows, stacked_ref, colour_ref, transmit_ref, recv, send_sems, recv_sems, local_sem):
    me = lax.axis_index("gx")
    col = lax.axis_index("gy")

    def peer_of(i):
        return lax.rem(me + i, n)

    def link(peer, slot):
        return pltpu.make_async_remote_copy(
            src_ref=stacked_ref.at[peer],
            dst_ref=recv.at[slot],
            send_sem=send_sems.at[peer],
            recv_sem=recv_sems.at[slot],
            device_id=(peer, col),
            device_id_type=MESH_ID,
        )

    barrier = pltpu.get_barrier_semaphore()

    def greet(i, carry):
        pl.semaphore_signal(barrier, inc=1, device_id=(peer_of(i), col), device_id_type=MESH_ID)
        return carry

    lax.fori_loop(1, n, greet, 0)
    pl.semaphore_wait(barrier, n - 1)

    def send(i, carry):
        link(peer_of(i), me).start()
        return carry

    lax.fori_loop(1, n, send, 0)
    own = pltpu.make_async_copy(stacked_ref.at[me], recv.at[me], local_sem)
    own.start()
    own.wait()

    def finish(i, carry):
        peer = peer_of(i)
        link(peer, peer).wait_send()
        link(peer, peer).wait_recv()
        return carry

    lax.fori_loop(1, n, finish, 0)

    cols = colour_ref.shape[-1]
    span = cols // 128
    zero = jnp.zeros((rows * span, 128), jnp.float32)

    def value(block, k):
        pieces = [block[(r * 4 + k) * span:(r * 4 + k + 1) * span] for r in range(rows)]
        return pieces[0] if rows == 1 else jnp.concatenate(pieces, axis=0)

    def accumulate(d, carry):
        front, c0, c1, c2 = carry
        block = recv[d]
        seen = jnp.exp(-front)
        return (
            front + value(block, 3),
            c0 + value(block, 0) * seen,
            c1 + value(block, 1) * seen,
            c2 + value(block, 2) * seen,
        )

    front, c0, c1, c2 = lax.fori_loop(0, n, accumulate, (zero, zero, zero, zero))
    for k, c in enumerate((c0, c1, c2)):
        colour_ref[k] = c.reshape(rows, cols)
    transmit_ref[...] = jnp.exp(-front).reshape(rows, cols)


def combine(stacked, n):
    rows, cols = stacked.shape[1], stacked.shape[3]
    stacked = stacked.reshape(n, rows * 4 * cols // 128, 128)
    vmem = pltpu.MemorySpace.VMEM
    return pl.pallas_call(
        functools.partial(combine_kernel, n, rows),
        out_shape=(
            jax.ShapeDtypeStruct((3, rows, cols), jnp.float32),
            jax.ShapeDtypeStruct((rows, cols), jnp.float32),
        ),
        in_specs=[pl.BlockSpec(memory_space=vmem)],
        out_specs=(pl.BlockSpec(memory_space=vmem), pl.BlockSpec(memory_space=vmem)),
        scratch_shapes=[
            pltpu.VMEM(stacked.shape, jnp.float32),
            pltpu.SemaphoreType.DMA((n,)),
            pltpu.SemaphoreType.DMA((n,)),
            pltpu.SemaphoreType.DMA,
        ],
        compiler_params=pltpu.CompilerParams(collective_id=0, has_side_effects=True),
    )(stacked)


def march_kernel(last, dens_ref, front_ref, back_ref, halo_ref, absorb_ref, out_ref):
    rows, cols = dens_ref.shape[1], dens_ref.shape[2]
    shape = (rows, 128)
    lane = lax.broadcasted_iota(jnp.int32, shape, 1)
    row = lax.broadcasted_iota(jnp.int32, shape, 0)
    first_lane, last_lane = lane == 0, lane == 127
    top_row, bottom_row = row == 0, row == rows - 1
    halves = cols // 128
    for h in range(halves):
        lanes = slice(h * 128, (h + 1) * 128)
        left_lanes = slice((h - 1) * 128, h * 128) if h > 0 else None
        right_lanes = slice((h + 1) * 128, (h + 2) * 128) if h + 1 < halves else None
        absorb = absorb_ref[:, lanes]

        def plane(ref_plane):
            return ref_plane[:, lanes]

        def step(x, carry):
            seen, c0, c1, c2, optical = carry
            centre_plane = dens_ref.at[x]
            d = centre_plane[:, lanes]
            behind = jnp.where(x == 0, front_ref[:, lanes], dens_ref[jnp.maximum(x - 1, 0), :, lanes])
            ahead = jnp.where(x == last, back_ref[:, lanes], dens_ref[jnp.minimum(x + 1, last), :, lanes])
            halo = halo_ref[x]
            from_left = pltpu.roll(d, 1, 1)
            from_right = pltpu.roll(d, 127, 1)
            if left_lanes is None:
                edge_left = halo
            else:
                edge_left = pltpu.roll(centre_plane[:, left_lanes], 1, 1)
            if right_lanes is None:
                edge_right = halo
            else:
                edge_right = pltpu.roll(centre_plane[:, right_lanes], 127, 1)
            left = jnp.where(first_lane, edge_left, from_left)
            right = jnp.where(last_lane, edge_right, from_right)
            above = jnp.where(top_row, 0.0, pltpu.roll(d, 1, 0))
            below = jnp.where(bottom_row, 0.0, pltpu.roll(d, rows - 1, 0))
            step_depth = (ahead - behind) * 0.5
            step_row = (below - above) * 0.5
            step_col = (right - left) * 0.5
            facing = 0.48 * step_depth + 0.64 * step_row + 0.6 * step_col
            length2 = step_depth * step_depth + step_row * step_row + step_col * step_col + 1.0
            lighting = 0.25 + 0.75 * jnp.maximum(facing, 0.0) * lax.rsqrt(length2)
            soft = jnp.maximum(d, 0.0) + jnp.log1p(jnp.exp(-jnp.abs(d)))
            extinct = absorb * soft
            passed = jnp.exp(-extinct)
            weight = seen * (1.0 - passed) * lighting
            tints = [1.0 / (1.0 + jnp.exp(-(slope * d + offset))) for slope, offset in zip(SLOPES, OFFSETS)]
            return (
                seen * passed,
                c0 + weight * tints[0],
                c1 + weight * tints[1],
                c2 + weight * tints[2],
                optical + extinct,
            )

        zero = jnp.zeros(shape, jnp.float32)
        one = jnp.ones(shape, jnp.float32)
        _, c0, c1, c2, optical = lax.fori_loop(0, last + 1, step, (one, zero, zero, zero, zero))
        for k, value in enumerate((c0, c1, c2, optical)):
            out_ref[k, :, lanes] = value


def march(density, front, back, halo, absorb):
    depth, rows, cols = density.shape
    vmem = pltpu.MemorySpace.VMEM
    return pl.pallas_call(
        functools.partial(march_kernel, depth - 1),
        out_shape=jax.ShapeDtypeStruct((4, rows, cols), jnp.float32),
        in_specs=[pl.BlockSpec(memory_space=vmem)] * 5,
        out_specs=pl.BlockSpec(memory_space=vmem),
    )(density, front, back, halo, absorb)


def shifted(value, axis, forward):
    size = lax.axis_size(axis)
    pairs = [(i, i + 1) for i in range(size - 1)]
    if not forward:
        pairs = [(j, i) for i, j in pairs]
    return lax.ppermute(value, axis, pairs)


def local(density, absorb):
    depth, nz, cols = density.shape
    front = shifted(density[depth - 1], "gx", True)
    back = shifted(density[0], "gx", False)
    left = shifted(density[:, :, cols - 1:], "gy", True)
    right = shifted(density[:, :, :1], "gy", False)
    halo = jnp.concatenate([left, jnp.zeros((depth, nz, 126), jnp.float32), right], axis=2)
    parts = march(density, front, back, halo, absorb)
    n = lax.axis_size("gx")
    stacked = jnp.transpose(parts, (1, 0, 2)).reshape(n, nz // n, 4, cols)
    return combine(stacked, n)


def solution(mesh):
    placed = (P("gx", None, "gy"), P(None, "gy"))
    return jax.shard_map(
        local,
        mesh=mesh,
        in_specs=placed,
        out_specs=(P(None, "gx", "gy"), P("gx", "gy")),
        check_vma=False,
    )
```

```python
import functools

import jax
import jax.numpy as jnp
from jax import lax
from jax.experimental import pallas as pl
from jax.experimental.pallas import tpu as pltpu
from jax.sharding import PartitionSpec as P

SLOPES = (2.0, -1.5, 0.8)
OFFSETS = (0.0, 0.5, -0.3)
MESH_ID = pl.DeviceIdType.MESH


def combine_kernel(n, rows, stacked_ref, colour_ref, transmit_ref, recv, send_sems, recv_sems, local_sem):
    me = lax.axis_index("gx")
    col = lax.axis_index("gy")

    def peer_of(i):
        return lax.rem(me + i, n)

    def link(peer, slot):
        return pltpu.make_async_remote_copy(
            src_ref=stacked_ref.at[peer],
            dst_ref=recv.at[slot],
            send_sem=send_sems.at[peer],
            recv_sem=recv_sems.at[slot],
            device_id=(peer, col),
            device_id_type=MESH_ID,
        )

    barrier = pltpu.get_barrier_semaphore()

    def greet(i, carry):
        pl.semaphore_signal(barrier, inc=1, device_id=(peer_of(i), col), device_id_type=MESH_ID)
        return carry

    lax.fori_loop(1, n, greet, 0)
    pl.semaphore_wait(barrier, n - 1)

    def send(i, carry):
        link(peer_of(i), me).start()
        return carry

    lax.fori_loop(1, n, send, 0)
    own = pltpu.make_async_copy(stacked_ref.at[me], recv.at[me], local_sem)
    own.start()
    own.wait()

    def finish(i, carry):
        peer = peer_of(i)
        link(peer, peer).wait_send()
        link(peer, peer).wait_recv()
        return carry

    lax.fori_loop(1, n, finish, 0)

    cols = colour_ref.shape[-1]
    span = cols // 128
    zero = jnp.zeros((rows * span, 128), jnp.float32)

    def value(block, k):
        pieces = [block[(r * 4 + k) * span:(r * 4 + k + 1) * span] for r in range(rows)]
        return pieces[0] if rows == 1 else jnp.concatenate(pieces, axis=0)

    def accumulate(d, carry):
        front, c0, c1, c2 = carry
        block = recv[d]
        seen = jnp.exp(-front)
        return (
            front + value(block, 3),
            c0 + value(block, 0) * seen,
            c1 + value(block, 1) * seen,
            c2 + value(block, 2) * seen,
        )

    front, c0, c1, c2 = lax.fori_loop(0, n, accumulate, (zero, zero, zero, zero))
    for k, c in enumerate((c0, c1, c2)):
        colour_ref[k] = c.reshape(rows, cols)
    transmit_ref[...] = jnp.exp(-front).reshape(rows, cols)


def combine(stacked, n):
    rows, cols = stacked.shape[1], stacked.shape[3]
    stacked = stacked.reshape(n, rows * 4 * cols // 128, 128)
    vmem = pltpu.MemorySpace.VMEM
    return pl.pallas_call(
        functools.partial(combine_kernel, n, rows),
        out_shape=(
            jax.ShapeDtypeStruct((3, rows, cols), jnp.float32),
            jax.ShapeDtypeStruct((rows, cols), jnp.float32),
        ),
        in_specs=[pl.BlockSpec(memory_space=vmem)],
        out_specs=(pl.BlockSpec(memory_space=vmem), pl.BlockSpec(memory_space=vmem)),
        scratch_shapes=[
            pltpu.VMEM(stacked.shape, jnp.float32),
            pltpu.SemaphoreType.DMA((n,)),
            pltpu.SemaphoreType.DMA((n,)),
            pltpu.SemaphoreType.DMA,
        ],
        compiler_params=pltpu.CompilerParams(collective_id=0, has_side_effects=True),
    )(stacked)


def march_kernel(last, dens_ref, front_ref, back_ref, left_ref, right_ref, absorb_ref, out_ref):
    rows, cols = dens_ref.shape[1], dens_ref.shape[2]
    shape = (rows, 128)
    lane = lax.broadcasted_iota(jnp.int32, shape, 1)
    row = lax.broadcasted_iota(jnp.int32, shape, 0)
    first_lane, last_lane = lane == 0, lane == 127
    top_row, bottom_row = row == 0, row == rows - 1
    halves = cols // 128
    for h in range(halves):
        lanes = slice(h * 128, (h + 1) * 128)
        left_lanes = slice((h - 1) * 128, h * 128) if h > 0 else None
        right_lanes = slice((h + 1) * 128, (h + 2) * 128) if h + 1 < halves else None
        absorb = absorb_ref[:, lanes]

        def plane(ref_plane):
            return ref_plane[:, lanes]

        def step(x, carry):
            seen, c0, c1, c2, optical = carry
            centre_plane = dens_ref.at[x]
            d = centre_plane[:, lanes]
            behind = jnp.where(x == 0, front_ref[:, lanes], dens_ref[jnp.maximum(x - 1, 0), :, lanes])
            ahead = jnp.where(x == last, back_ref[:, lanes], dens_ref[jnp.minimum(x + 1, last), :, lanes])
            span = left_ref.shape[1]
            halo_left = pltpu.roll(left_ref[...], lax.rem(span - x, span), 1)
            halo_right = pltpu.roll(right_ref[...], lax.rem(span + 127 - x, span), 1)
            from_left = pltpu.roll(d, 1, 1)
            from_right = pltpu.roll(d, 127, 1)
            if left_lanes is None:
                edge_left = halo_left
            else:
                edge_left = pltpu.roll(centre_plane[:, left_lanes], 1, 1)
            if right_lanes is None:
                edge_right = halo_right
            else:
                edge_right = pltpu.roll(centre_plane[:, right_lanes], 127, 1)
            left = jnp.where(first_lane, edge_left, from_left)
            right = jnp.where(last_lane, edge_right, from_right)
            above = jnp.where(top_row, 0.0, pltpu.roll(d, 1, 0))
            below = jnp.where(bottom_row, 0.0, pltpu.roll(d, rows - 1, 0))
            step_depth = (ahead - behind) * 0.5
            step_row = (below - above) * 0.5
            step_col = (right - left) * 0.5
            facing = 0.48 * step_depth + 0.64 * step_row + 0.6 * step_col
            length2 = step_depth * step_depth + step_row * step_row + step_col * step_col + 1.0
            lighting = 0.25 + 0.75 * jnp.maximum(facing, 0.0) * lax.rsqrt(length2)
            soft = jnp.maximum(d, 0.0) + jnp.log1p(jnp.exp(-jnp.abs(d)))
            extinct = absorb * soft
            passed = jnp.exp(-extinct)
            weight = seen * (1.0 - passed) * lighting
            tints = [1.0 / (1.0 + jnp.exp(-(slope * d + offset))) for slope, offset in zip(SLOPES, OFFSETS)]
            return (
                seen * passed,
                c0 + weight * tints[0],
                c1 + weight * tints[1],
                c2 + weight * tints[2],
                optical + extinct,
            )

        zero = jnp.zeros(shape, jnp.float32)
        one = jnp.ones(shape, jnp.float32)
        _, c0, c1, c2, optical = lax.fori_loop(0, last + 1, step, (one, zero, zero, zero, zero))
        for k, value in enumerate((c0, c1, c2, optical)):
            out_ref[k, :, lanes] = value


def march(density, front, back, left, right, absorb):
    depth, rows, cols = density.shape
    vmem = pltpu.MemorySpace.VMEM
    return pl.pallas_call(
        functools.partial(march_kernel, depth - 1),
        out_shape=jax.ShapeDtypeStruct((4, rows, cols), jnp.float32),
        in_specs=[pl.BlockSpec(memory_space=vmem)] * 6,
        out_specs=pl.BlockSpec(memory_space=vmem),
    )(density, front, back, left, right, absorb)


def shifted(value, axis, forward):
    size = lax.axis_size(axis)
    pairs = [(i, i + 1) for i in range(size - 1)]
    if not forward:
        pairs = [(j, i) for i, j in pairs]
    return lax.ppermute(value, axis, pairs)


def local(density, absorb):
    depth, nz, cols = density.shape
    front = shifted(density[depth - 1], "gx", True)
    back = shifted(density[0], "gx", False)
    left = shifted(jnp.transpose(density[:, :, cols - 1]), "gy", True)
    right = shifted(jnp.transpose(density[:, :, 0]), "gy", False)
    parts = march(density, front, back, left, right, absorb)
    n = lax.axis_size("gx")
    stacked = jnp.transpose(parts, (1, 0, 2)).reshape(n, nz // n, 4, cols)
    return combine(stacked, n)


def solution(mesh):
    placed = (P("gx", None, "gy"), P(None, "gy"))
    return jax.shard_map(
        local,
        mesh=mesh,
        in_specs=placed,
        out_specs=(P(None, "gx", "gy"), P("gx", "gy")),
        check_vma=False,
    )
```

```python
import functools

import jax
import jax.numpy as jnp
from jax import lax
from jax.experimental import pallas as pl
from jax.experimental.pallas import tpu as pltpu
from jax.sharding import PartitionSpec as P

SLOPES = (2.0, -1.5, 0.8)
OFFSETS = (0.0, 0.5, -0.3)
HALF_SLOPES = tuple(0.5 * v for v in SLOPES)
HALF_OFFSETS = tuple(0.5 * v for v in OFFSETS)
LOG2_E = 1.4426950408889634
MESH_ID = pl.DeviceIdType.MESH


def combine_kernel(n, rows, stacked_ref, colour_ref, transmit_ref, recv, send_sems, recv_sems, local_sem):
    me = lax.axis_index("gx")
    col = lax.axis_index("gy")

    def peer_of(i):
        return lax.rem(me + i, n)

    def link(peer, slot):
        return pltpu.make_async_remote_copy(
            src_ref=stacked_ref.at[peer],
            dst_ref=recv.at[slot],
            send_sem=send_sems.at[peer],
            recv_sem=recv_sems.at[slot],
            device_id=(peer, col),
            device_id_type=MESH_ID,
        )

    barrier = pltpu.get_barrier_semaphore()

    def greet(i, carry):
        pl.semaphore_signal(barrier, inc=1, device_id=(peer_of(i), col), device_id_type=MESH_ID)
        return carry

    lax.fori_loop(1, n, greet, 0)
    pl.semaphore_wait(barrier, n - 1)

    def send(i, carry):
        link(peer_of(i), me).start()
        return carry

    lax.fori_loop(1, n, send, 0)
    own = pltpu.make_async_copy(stacked_ref.at[me], recv.at[me], local_sem)
    own.start()
    own.wait()

    def finish(i, carry):
        peer = peer_of(i)
        link(peer, peer).wait_send()
        link(peer, peer).wait_recv()
        return carry

    lax.fori_loop(1, n, finish, 0)

    cols = colour_ref.shape[-1]
    span = cols // 128
    zero = jnp.zeros((rows * span, 128), jnp.float32)

    def value(block, k):
        pieces = [block[(r * 4 + k) * span:(r * 4 + k + 1) * span] for r in range(rows)]
        return pieces[0] if rows == 1 else jnp.concatenate(pieces, axis=0)

    def accumulate(d, carry):
        front, c0, c1, c2 = carry
        block = recv[d]
        seen = jnp.exp(-front)
        return (
            front + value(block, 3),
            c0 + value(block, 0) * seen,
            c1 + value(block, 1) * seen,
            c2 + value(block, 2) * seen,
        )

    front, c0, c1, c2 = lax.fori_loop(0, n, accumulate, (zero, zero, zero, zero))
    for k, c in enumerate((c0, c1, c2)):
        colour_ref[k] = c.reshape(rows, cols)
    transmit_ref[...] = jnp.exp(-front).reshape(rows, cols)


def combine(stacked, n):
    rows, cols = stacked.shape[1], stacked.shape[3]
    stacked = stacked.reshape(n, rows * 4 * cols // 128, 128)
    vmem = pltpu.MemorySpace.VMEM
    return pl.pallas_call(
        functools.partial(combine_kernel, n, rows),
        out_shape=(
            jax.ShapeDtypeStruct((3, rows, cols), jnp.float32),
            jax.ShapeDtypeStruct((rows, cols), jnp.float32),
        ),
        in_specs=[pl.BlockSpec(memory_space=vmem)],
        out_specs=(pl.BlockSpec(memory_space=vmem), pl.BlockSpec(memory_space=vmem)),
        scratch_shapes=[
            pltpu.VMEM(stacked.shape, jnp.float32),
            pltpu.SemaphoreType.DMA((n,)),
            pltpu.SemaphoreType.DMA((n,)),
            pltpu.SemaphoreType.DMA,
        ],
        compiler_params=pltpu.CompilerParams(collective_id=0, has_side_effects=True),
    )(stacked)


def march_kernel(last, dens_ref, front_ref, back_ref, left_ref, right_ref, absorb_ref, out_ref):
    rows, cols = dens_ref.shape[1], dens_ref.shape[2]
    shape = (rows, 128)
    lane = lax.broadcasted_iota(jnp.int32, shape, 1)
    row = lax.broadcasted_iota(jnp.int32, shape, 0)
    first_lane, last_lane = lane == 0, lane == 127
    top_row, bottom_row = row == 0, row == rows - 1
    halves = cols // 128
    for h in range(halves):
        lanes = slice(h * 128, (h + 1) * 128)
        left_lanes = slice((h - 1) * 128, h * 128) if h > 0 else None
        right_lanes = slice((h + 1) * 128, (h + 2) * 128) if h + 1 < halves else None
        absorb = absorb_ref[:, lanes]
        fade = absorb * (-LOG2_E)

        def plane(ref_plane):
            return ref_plane[:, lanes]

        def step(x, carry):
            seen, total, t0, t1, t2, softsum = carry
            centre_plane = dens_ref.at[x]
            d = centre_plane[:, lanes]
            behind = jnp.where(x == 0, front_ref[:, lanes], dens_ref[jnp.maximum(x - 1, 0), :, lanes])
            ahead = jnp.where(x == last, back_ref[:, lanes], dens_ref[jnp.minimum(x + 1, last), :, lanes])
            span = left_ref.shape[1]
            halo_left = pltpu.roll(left_ref[...], lax.rem(span - x, span), 1)
            halo_right = pltpu.roll(right_ref[...], lax.rem(span + 127 - x, span), 1)
            from_left = pltpu.roll(d, 1, 1)
            from_right = pltpu.roll(d, 127, 1)
            if left_lanes is None:
                edge_left = halo_left
            else:
                edge_left = pltpu.roll(centre_plane[:, left_lanes], 1, 1)
            if right_lanes is None:
                edge_right = halo_right
            else:
                edge_right = pltpu.roll(centre_plane[:, right_lanes], 127, 1)
            left = jnp.where(first_lane, edge_left, from_left)
            right = jnp.where(last_lane, edge_right, from_right)
            above = jnp.where(top_row, 0.0, pltpu.roll(d, 1, 0))
            below = jnp.where(bottom_row, 0.0, pltpu.roll(d, rows - 1, 0))
            step_depth = ahead - behind
            step_row = below - above
            step_col = right - left
            facing = 0.18 * step_depth + 0.24 * step_row + 0.225 * step_col
            length2 = 0.25 * (step_depth * step_depth + step_row * step_row + step_col * step_col) + 1.0
            lighting = 0.25 + jnp.maximum(facing, 0.0) * lax.rsqrt(length2)
            soft = jnp.log(1.0 + jnp.exp(d))
            passed = jnp.exp2(fade * soft)
            seen_after = seen * passed
            weight = (seen - seen_after) * lighting
            return (
                seen_after,
                total + weight,
                t0 + weight * jnp.tanh(HALF_SLOPES[0] * d + HALF_OFFSETS[0]),
                t1 + weight * jnp.tanh(HALF_SLOPES[1] * d + HALF_OFFSETS[1]),
                t2 + weight * jnp.tanh(HALF_SLOPES[2] * d + HALF_OFFSETS[2]),
                softsum + soft,
            )

        zero = jnp.zeros(shape, jnp.float32)
        one = jnp.ones(shape, jnp.float32)
        _, total, t0, t1, t2, softsum = lax.fori_loop(
            0, last + 1, step, (one, zero, zero, zero, zero, zero)
        )
        for k, value in enumerate((t0, t1, t2)):
            out_ref[k, :, lanes] = 0.5 * (total + value)
        out_ref[3, :, lanes] = absorb * softsum


def march(density, front, back, left, right, absorb):
    depth, rows, cols = density.shape
    vmem = pltpu.MemorySpace.VMEM
    return pl.pallas_call(
        functools.partial(march_kernel, depth - 1),
        out_shape=jax.ShapeDtypeStruct((4, rows, cols), jnp.float32),
        in_specs=[pl.BlockSpec(memory_space=vmem)] * 6,
        out_specs=pl.BlockSpec(memory_space=vmem),
    )(density, front, back, left, right, absorb)


def shifted(value, axis, forward):
    size = lax.axis_size(axis)
    pairs = [(i, i + 1) for i in range(size - 1)]
    if not forward:
        pairs = [(j, i) for i, j in pairs]
    return lax.ppermute(value, axis, pairs)


def local(density, absorb):
    depth, nz, cols = density.shape
    front = shifted(density[depth - 1], "gx", True)
    back = shifted(density[0], "gx", False)
    left = shifted(jnp.transpose(density[:, :, cols - 1]), "gy", True)
    right = shifted(jnp.transpose(density[:, :, 0]), "gy", False)
    parts = march(density, front, back, left, right, absorb)
    n = lax.axis_size("gx")
    stacked = jnp.transpose(parts, (1, 0, 2)).reshape(n, nz // n, 4, cols)
    return combine(stacked, n)


def solution(mesh):
    placed = (P("gx", None, "gy"), P(None, "gy"))
    return jax.shard_map(
        local,
        mesh=mesh,
        in_specs=placed,
        out_specs=(P(None, "gx", "gy"), P("gx", "gy")),
        check_vma=False,
    )
```

```python
import functools

import jax
import jax.numpy as jnp
from jax import lax
from jax.experimental import pallas as pl
from jax.experimental.pallas import tpu as pltpu
from jax.sharding import PartitionSpec as P

SLOPES = (2.0, -1.5, 0.8)
OFFSETS = (0.0, 0.5, -0.3)
HALF_SLOPES = tuple(0.5 * v for v in SLOPES)
HALF_OFFSETS = tuple(0.5 * v for v in OFFSETS)
LOG2_E = 1.4426950408889634
MESH_ID = pl.DeviceIdType.MESH


def combine_kernel(n, rows, stacked_ref, colour_ref, transmit_ref, recv, send_sems, recv_sems, local_sem):
    me = lax.axis_index("gx")
    col = lax.axis_index("gy")

    def peer_of(i):
        return lax.rem(me + i, n)

    def link(peer, slot):
        return pltpu.make_async_remote_copy(
            src_ref=stacked_ref.at[peer],
            dst_ref=recv.at[slot],
            send_sem=send_sems.at[peer],
            recv_sem=recv_sems.at[slot],
            device_id=(peer, col),
            device_id_type=MESH_ID,
        )

    barrier = pltpu.get_barrier_semaphore()

    def greet(i, carry):
        pl.semaphore_signal(barrier, inc=1, device_id=(peer_of(i), col), device_id_type=MESH_ID)
        return carry

    lax.fori_loop(1, n, greet, 0)
    pl.semaphore_wait(barrier, n - 1)

    def send(i, carry):
        link(peer_of(i), me).start()
        return carry

    lax.fori_loop(1, n, send, 0)
    own = pltpu.make_async_copy(stacked_ref.at[me], recv.at[me], local_sem)
    own.start()
    own.wait()

    def finish(i, carry):
        peer = peer_of(i)
        link(peer, peer).wait_send()
        link(peer, peer).wait_recv()
        return carry

    lax.fori_loop(1, n, finish, 0)

    cols = colour_ref.shape[-1]
    span = cols // 128
    zero = jnp.zeros((rows * span, 128), jnp.float32)

    def value(block, k):
        pieces = [block[(r * 4 + k) * span:(r * 4 + k + 1) * span] for r in range(rows)]
        return pieces[0] if rows == 1 else jnp.concatenate(pieces, axis=0)

    def accumulate(d, carry):
        front, c0, c1, c2 = carry
        block = recv[d]
        seen = jnp.exp(-front)
        return (
            front + value(block, 3),
            c0 + value(block, 0) * seen,
            c1 + value(block, 1) * seen,
            c2 + value(block, 2) * seen,
        )

    front, c0, c1, c2 = lax.fori_loop(0, n, accumulate, (zero, zero, zero, zero))
    for k, c in enumerate((c0, c1, c2)):
        colour_ref[k] = c.reshape(rows, cols)
    transmit_ref[...] = jnp.exp(-front).reshape(rows, cols)


def combine(stacked, n):
    rows, cols = stacked.shape[1], stacked.shape[3]
    stacked = stacked.reshape(n, rows * 4 * cols // 128, 128)
    vmem = pltpu.MemorySpace.VMEM
    return pl.pallas_call(
        functools.partial(combine_kernel, n, rows),
        out_shape=(
            jax.ShapeDtypeStruct((3, rows, cols), jnp.float32),
            jax.ShapeDtypeStruct((rows, cols), jnp.float32),
        ),
        in_specs=[pl.BlockSpec(memory_space=vmem)],
        out_specs=(pl.BlockSpec(memory_space=vmem), pl.BlockSpec(memory_space=vmem)),
        scratch_shapes=[
            pltpu.VMEM(stacked.shape, jnp.float32),
            pltpu.SemaphoreType.DMA((n,)),
            pltpu.SemaphoreType.DMA((n,)),
            pltpu.SemaphoreType.DMA,
        ],
        compiler_params=pltpu.CompilerParams(collective_id=0, has_side_effects=True),
    )(stacked)


def march_kernel(last, dens_ref, front_ref, back_ref, left_ref, right_ref, absorb_ref, out_ref):
    rows, cols = dens_ref.shape[1], dens_ref.shape[2]
    shape = (rows, 128)
    lane = lax.broadcasted_iota(jnp.int32, shape, 1)
    row = lax.broadcasted_iota(jnp.int32, shape, 0)
    first_lane, last_lane = lane == 0, lane == 127
    top_row, bottom_row = row == 0, row == rows - 1
    halves = cols // 128
    for h in range(halves):
        lanes = slice(h * 128, (h + 1) * 128)
        left_lanes = slice((h - 1) * 128, h * 128) if h > 0 else None
        right_lanes = slice((h + 1) * 128, (h + 2) * 128) if h + 1 < halves else None
        absorb = absorb_ref[:, lanes]
        fade = absorb * (-LOG2_E)

        def plane(ref_plane):
            return ref_plane[:, lanes]

        def step(x, carry):
            seen, total, t0, t1, t2, softsum = carry
            centre_plane = dens_ref.at[x]
            d = centre_plane[:, lanes]
            behind = jnp.where(x == 0, front_ref[:, lanes], dens_ref[jnp.maximum(x - 1, 0), :, lanes])
            ahead = jnp.where(x == last, back_ref[:, lanes], dens_ref[jnp.minimum(x + 1, last), :, lanes])
            span = left_ref.shape[1]
            halo_left = pltpu.roll(left_ref[...], lax.rem(span - x, span), 1)
            halo_right = pltpu.roll(right_ref[...], lax.rem(span + 127 - x, span), 1)
            from_left = pltpu.roll(d, 1, 1)
            from_right = pltpu.roll(d, 127, 1)
            if left_lanes is None:
                edge_left = halo_left
            else:
                edge_left = pltpu.roll(centre_plane[:, left_lanes], 1, 1)
            if right_lanes is None:
                edge_right = halo_right
            else:
                edge_right = pltpu.roll(centre_plane[:, right_lanes], 127, 1)
            left = jnp.where(first_lane, edge_left, from_left)
            right = jnp.where(last_lane, edge_right, from_right)
            above = jnp.where(top_row, 0.0, pltpu.roll(d, 1, 0))
            below = jnp.where(bottom_row, 0.0, pltpu.roll(d, rows - 1, 0))
            step_depth = ahead - behind
            step_row = below - above
            step_col = right - left
            facing = 0.18 * step_depth + 0.24 * step_row + 0.225 * step_col
            length2 = 0.25 * (step_depth * step_depth + step_row * step_row + step_col * step_col) + 1.0
            lighting = 0.25 + jnp.maximum(facing, 0.0) * lax.rsqrt(length2)
            soft = jnp.log(1.0 + jnp.exp(d))
            passed = jnp.exp2(fade * soft)
            seen_after = seen * passed
            weight = (seen - seen_after) * lighting
            return (
                seen_after,
                total + weight,
                t0 + weight * jnp.tanh(HALF_SLOPES[0] * d + HALF_OFFSETS[0]),
                t1 + weight * jnp.tanh(HALF_SLOPES[1] * d + HALF_OFFSETS[1]),
                t2 + weight * jnp.tanh(HALF_SLOPES[2] * d + HALF_OFFSETS[2]),
                softsum + soft,
            )

        zero = jnp.zeros(shape, jnp.float32)
        one = jnp.ones(shape, jnp.float32)
        _, total, t0, t1, t2, softsum = lax.fori_loop(
            0, last + 1, step, (one, zero, zero, zero, zero, zero), unroll=4
        )
        for k, value in enumerate((t0, t1, t2)):
            out_ref[k, :, lanes] = 0.5 * (total + value)
        out_ref[3, :, lanes] = absorb * softsum


def march(density, front, back, left, right, absorb):
    depth, rows, cols = density.shape
    vmem = pltpu.MemorySpace.VMEM
    return pl.pallas_call(
        functools.partial(march_kernel, depth - 1),
        out_shape=jax.ShapeDtypeStruct((4, rows, cols), jnp.float32),
        in_specs=[pl.BlockSpec(memory_space=vmem)] * 6,
        out_specs=pl.BlockSpec(memory_space=vmem),
    )(density, front, back, left, right, absorb)


def shifted(value, axis, forward):
    size = lax.axis_size(axis)
    pairs = [(i, i + 1) for i in range(size - 1)]
    if not forward:
        pairs = [(j, i) for i, j in pairs]
    return lax.ppermute(value, axis, pairs)


def local(density, absorb):
    depth, nz, cols = density.shape
    front = shifted(density[depth - 1], "gx", True)
    back = shifted(density[0], "gx", False)
    left = shifted(jnp.transpose(density[:, :, cols - 1]), "gy", True)
    right = shifted(jnp.transpose(density[:, :, 0]), "gy", False)
    parts = march(density, front, back, left, right, absorb)
    n = lax.axis_size("gx")
    stacked = jnp.transpose(parts, (1, 0, 2)).reshape(n, nz // n, 4, cols)
    return combine(stacked, n)


def solution(mesh):
    placed = (P("gx", None, "gy"), P(None, "gy"))
    return jax.shard_map(
        local,
        mesh=mesh,
        in_specs=placed,
        out_specs=(P(None, "gx", "gy"), P("gx", "gy")),
        check_vma=False,
    )
```

```python
import functools

import jax
import jax.numpy as jnp
from jax import lax
from jax.experimental import pallas as pl
from jax.experimental.pallas import tpu as pltpu
from jax.sharding import PartitionSpec as P

SLOPES = (2.0, -1.5, 0.8)
OFFSETS = (0.0, 0.5, -0.3)
HALF_SLOPES = tuple(0.5 * v for v in SLOPES)
HALF_OFFSETS = tuple(0.5 * v for v in OFFSETS)
LOG2_E = 1.4426950408889634
MESH_ID = pl.DeviceIdType.MESH


def combine_kernel(n, rows, stacked_ref, colour_ref, transmit_ref, recv, send_sems, recv_sems, local_sem):
    me = lax.axis_index("gx")
    col = lax.axis_index("gy")

    def peer_of(i):
        return lax.rem(me + i, n)

    def link(peer, slot):
        return pltpu.make_async_remote_copy(
            src_ref=stacked_ref.at[peer],
            dst_ref=recv.at[slot],
            send_sem=send_sems.at[peer],
            recv_sem=recv_sems.at[slot],
            device_id=(peer, col),
            device_id_type=MESH_ID,
        )

    barrier = pltpu.get_barrier_semaphore()

    def greet(i, carry):
        pl.semaphore_signal(barrier, inc=1, device_id=(peer_of(i), col), device_id_type=MESH_ID)
        return carry

    lax.fori_loop(1, n, greet, 0)
    pl.semaphore_wait(barrier, n - 1)

    def send(i, carry):
        link(peer_of(i), me).start()
        return carry

    lax.fori_loop(1, n, send, 0)
    own = pltpu.make_async_copy(stacked_ref.at[me], recv.at[me], local_sem)
    own.start()
    own.wait()

    def finish(i, carry):
        peer = peer_of(i)
        link(peer, peer).wait_send()
        link(peer, peer).wait_recv()
        return carry

    lax.fori_loop(1, n, finish, 0)

    cols = colour_ref.shape[-1]
    span = cols // 128
    zero = jnp.zeros((rows * span, 128), jnp.float32)

    def value(block, k):
        pieces = [block[(r * 4 + k) * span:(r * 4 + k + 1) * span] for r in range(rows)]
        return pieces[0] if rows == 1 else jnp.concatenate(pieces, axis=0)

    def accumulate(d, carry):
        front, c0, c1, c2 = carry
        block = recv[d]
        seen = jnp.exp(-front)
        return (
            front + value(block, 3),
            c0 + value(block, 0) * seen,
            c1 + value(block, 1) * seen,
            c2 + value(block, 2) * seen,
        )

    front, c0, c1, c2 = lax.fori_loop(0, n, accumulate, (zero, zero, zero, zero))
    for k, c in enumerate((c0, c1, c2)):
        colour_ref[k] = c.reshape(rows, cols)
    transmit_ref[...] = jnp.exp(-front).reshape(rows, cols)


def combine(stacked, n):
    rows, cols = stacked.shape[1], stacked.shape[3]
    stacked = stacked.reshape(n, rows * 4 * cols // 128, 128)
    vmem = pltpu.MemorySpace.VMEM
    return pl.pallas_call(
        functools.partial(combine_kernel, n, rows),
        out_shape=(
            jax.ShapeDtypeStruct((3, rows, cols), jnp.float32),
            jax.ShapeDtypeStruct((rows, cols), jnp.float32),
        ),
        in_specs=[pl.BlockSpec(memory_space=vmem)],
        out_specs=(pl.BlockSpec(memory_space=vmem), pl.BlockSpec(memory_space=vmem)),
        scratch_shapes=[
            pltpu.VMEM(stacked.shape, jnp.float32),
            pltpu.SemaphoreType.DMA((n,)),
            pltpu.SemaphoreType.DMA((n,)),
            pltpu.SemaphoreType.DMA,
        ],
        compiler_params=pltpu.CompilerParams(collective_id=0, has_side_effects=True),
    )(stacked)


def march_kernel(last, dens_ref, front_ref, back_ref, left_ref, right_ref, absorb_ref, out_ref):
    rows, cols = dens_ref.shape[1], dens_ref.shape[2]
    shape = (rows, 128)
    lane = lax.broadcasted_iota(jnp.int32, shape, 1)
    row = lax.broadcasted_iota(jnp.int32, shape, 0)
    first_lane, last_lane = lane == 0, lane == 127
    top_row, bottom_row = row == 0, row == rows - 1
    halves = cols // 128
    for h in range(halves):
        lanes = slice(h * 128, (h + 1) * 128)
        left_lanes = slice((h - 1) * 128, h * 128) if h > 0 else None
        right_lanes = slice((h + 1) * 128, (h + 2) * 128) if h + 1 < halves else None
        absorb = absorb_ref[:, lanes]
        fade = absorb * (-LOG2_E)

        def plane(ref_plane):
            return ref_plane[:, lanes]

        def step(x, carry):
            seen, total, t0, t1, t2, softsum = carry
            centre_plane = dens_ref.at[x]
            d = centre_plane[:, lanes]
            behind = jnp.where(x == 0, front_ref[:, lanes], dens_ref[jnp.maximum(x - 1, 0), :, lanes])
            ahead = jnp.where(x == last, back_ref[:, lanes], dens_ref[jnp.minimum(x + 1, last), :, lanes])
            span = left_ref.shape[1]
            halo_left = pltpu.roll(left_ref[...], lax.rem(span - x, span), 1)
            halo_right = pltpu.roll(right_ref[...], lax.rem(span + 127 - x, span), 1)
            from_left = pltpu.roll(d, 1, 1)
            from_right = pltpu.roll(d, 127, 1)
            if left_lanes is None:
                edge_left = halo_left
            else:
                edge_left = pltpu.roll(centre_plane[:, left_lanes], 1, 1)
            if right_lanes is None:
                edge_right = halo_right
            else:
                edge_right = pltpu.roll(centre_plane[:, right_lanes], 127, 1)
            left = jnp.where(first_lane, edge_left, from_left)
            right = jnp.where(last_lane, edge_right, from_right)
            above = jnp.where(top_row, 0.0, pltpu.roll(d, 1, 0))
            below = jnp.where(bottom_row, 0.0, pltpu.roll(d, rows - 1, 0))
            step_depth = ahead - behind
            step_row = below - above
            step_col = right - left
            facing = 0.18 * step_depth + 0.24 * step_row + 0.225 * step_col
            length2 = 0.25 * (step_depth * step_depth + step_row * step_row + step_col * step_col) + 1.0
            lighting = 0.25 + jnp.maximum(facing, 0.0) * lax.rsqrt(length2)
            soft = jnp.log(1.0 + jnp.exp(d))
            passed = jnp.exp2(fade * soft)
            seen_after = seen * passed
            weight = (seen - seen_after) * lighting
            return (
                seen_after,
                total + weight,
                t0 + weight * jnp.tanh(HALF_SLOPES[0] * d + HALF_OFFSETS[0]),
                t1 + weight * jnp.tanh(HALF_SLOPES[1] * d + HALF_OFFSETS[1]),
                t2 + weight * jnp.tanh(HALF_SLOPES[2] * d + HALF_OFFSETS[2]),
                softsum + soft,
            )

        zero = jnp.zeros(shape, jnp.float32)
        one = jnp.ones(shape, jnp.float32)
        _, total, t0, t1, t2, softsum = lax.fori_loop(
            0, last + 1, step, (one, zero, zero, zero, zero, zero), unroll=4
        )
        for k, value in enumerate((t0, t1, t2)):
            out_ref[k, :, lanes] = 0.5 * (total + value)
        out_ref[3, :, lanes] = absorb * softsum


def march(density, front, back, left, right, absorb):
    depth, rows, cols = density.shape
    vmem = pltpu.MemorySpace.VMEM
    return pl.pallas_call(
        functools.partial(march_kernel, depth - 1),
        out_shape=jax.ShapeDtypeStruct((4, rows, cols), jnp.float32),
        in_specs=[pl.BlockSpec(memory_space=vmem)] * 6,
        out_specs=pl.BlockSpec(memory_space=vmem),
    )(density, front, back, left, right, absorb)


def edge_kernel(dens_ref, first_ref, last_ref):
    depth, rows, cols = dens_ref.shape
    lane = lax.broadcasted_iota(jnp.int32, (rows, depth), 1)

    def step(x, carry):
        first, last = carry
        here = lane == x
        low = dens_ref[x, :, 0:128]
        high = dens_ref[x, :, cols - 128:cols]
        first = jnp.where(here, jnp.broadcast_to(low[:, 0:1], (rows, depth)), first)
        last = jnp.where(here, jnp.broadcast_to(high[:, 127:128], (rows, depth)), last)
        return first, last

    zero = jnp.zeros((rows, depth), jnp.float32)
    first, last = lax.fori_loop(0, depth, step, (zero, zero), unroll=8)
    first_ref[...] = first
    last_ref[...] = last


def edges(density):
    depth, rows, cols = density.shape
    vmem = pltpu.MemorySpace.VMEM
    plane = jax.ShapeDtypeStruct((rows, depth), jnp.float32)
    return pl.pallas_call(
        edge_kernel,
        out_shape=(plane, plane),
        in_specs=[pl.BlockSpec(memory_space=vmem)],
        out_specs=(pl.BlockSpec(memory_space=vmem), pl.BlockSpec(memory_space=vmem)),
    )(density)


def shifted(value, axis, forward):
    size = lax.axis_size(axis)
    pairs = [(i, i + 1) for i in range(size - 1)]
    if not forward:
        pairs = [(j, i) for i, j in pairs]
    return lax.ppermute(value, axis, pairs)


def local(density, absorb):
    depth, nz, cols = density.shape
    front = shifted(density[depth - 1], "gx", True)
    back = shifted(density[0], "gx", False)
    first_col, last_col = edges(density)
    left = shifted(last_col, "gy", True)
    right = shifted(first_col, "gy", False)
    parts = march(density, front, back, left, right, absorb)
    n = lax.axis_size("gx")
    stacked = jnp.transpose(parts, (1, 0, 2)).reshape(n, nz // n, 4, cols)
    return combine(stacked, n)


def solution(mesh):
    placed = (P("gx", None, "gy"), P(None, "gy"))
    return jax.shard_map(
        local,
        mesh=mesh,
        in_specs=placed,
        out_specs=(P(None, "gx", "gy"), P("gx", "gy")),
        check_vma=False,
    )
```

```python
import functools

import jax
import jax.numpy as jnp
from jax import lax
from jax.experimental import pallas as pl
from jax.experimental.pallas import tpu as pltpu
from jax.sharding import PartitionSpec as P

SLOPES = (2.0, -1.5, 0.8)
OFFSETS = (0.0, 0.5, -0.3)
HALF_SLOPES = tuple(0.5 * v for v in SLOPES)
HALF_OFFSETS = tuple(0.5 * v for v in OFFSETS)
LOG2_E = 1.4426950408889634
MESH_ID = pl.DeviceIdType.MESH


def march_kernel(last, n, dens_ref, front_ref, back_ref, left_ref, right_ref, absorb_ref,
                 colour_ref, transmit_ref, out_ref, part, recv, send_sems, recv_sems, local_sem):
    rows, cols = dens_ref.shape[1], dens_ref.shape[2]
    shape = (rows, 128)
    lane = lax.broadcasted_iota(jnp.int32, shape, 1)
    row = lax.broadcasted_iota(jnp.int32, shape, 0)
    first_lane, last_lane = lane == 0, lane == 127
    top_row, bottom_row = row == 0, row == rows - 1
    halves = cols // 128
    me = lax.axis_index("gx")
    col = lax.axis_index("gy")
    barrier = pltpu.get_barrier_semaphore()

    def greet(i, carry):
        pl.semaphore_signal(barrier, inc=1, device_id=(lax.rem(me + i, n), col), device_id_type=MESH_ID)
        return carry

    lax.fori_loop(1, n, greet, 0)
    for h in range(halves):
        lanes = slice(h * 128, (h + 1) * 128)
        left_lanes = slice((h - 1) * 128, h * 128) if h > 0 else None
        right_lanes = slice((h + 1) * 128, (h + 2) * 128) if h + 1 < halves else None
        absorb = absorb_ref[:, lanes]
        fade = absorb * (-LOG2_E)

        def plane(ref_plane):
            return ref_plane[:, lanes]

        def step(x, carry):
            seen, total, t0, t1, t2, softsum = carry
            centre_plane = dens_ref.at[x]
            d = centre_plane[:, lanes]
            behind = jnp.where(x == 0, front_ref[:, lanes], dens_ref[jnp.maximum(x - 1, 0), :, lanes])
            ahead = jnp.where(x == last, back_ref[:, lanes], dens_ref[jnp.minimum(x + 1, last), :, lanes])
            span = left_ref.shape[1]
            halo_left = pltpu.roll(left_ref[...], lax.rem(span - x, span), 1)
            halo_right = pltpu.roll(right_ref[...], lax.rem(span + 127 - x, span), 1)
            from_left = pltpu.roll(d, 1, 1)
            from_right = pltpu.roll(d, 127, 1)
            if left_lanes is None:
                edge_left = halo_left
            else:
                edge_left = pltpu.roll(centre_plane[:, left_lanes], 1, 1)
            if right_lanes is None:
                edge_right = halo_right
            else:
                edge_right = pltpu.roll(centre_plane[:, right_lanes], 127, 1)
            left = jnp.where(first_lane, edge_left, from_left)
            right = jnp.where(last_lane, edge_right, from_right)
            above = jnp.where(top_row, 0.0, pltpu.roll(d, 1, 0))
            below = jnp.where(bottom_row, 0.0, pltpu.roll(d, rows - 1, 0))
            step_depth = ahead - behind
            step_row = below - above
            step_col = right - left
            facing = 0.18 * step_depth + 0.24 * step_row + 0.225 * step_col
            length2 = 0.25 * (step_depth * step_depth + step_row * step_row + step_col * step_col) + 1.0
            lighting = 0.25 + jnp.maximum(facing, 0.0) * lax.rsqrt(length2)
            soft = jnp.log(1.0 + jnp.exp(d))
            passed = jnp.exp2(fade * soft)
            seen_after = seen * passed
            weight = (seen - seen_after) * lighting
            return (
                seen_after,
                total + weight,
                t0 + weight * jnp.tanh(HALF_SLOPES[0] * d + HALF_OFFSETS[0]),
                t1 + weight * jnp.tanh(HALF_SLOPES[1] * d + HALF_OFFSETS[1]),
                t2 + weight * jnp.tanh(HALF_SLOPES[2] * d + HALF_OFFSETS[2]),
                softsum + soft,
            )

        zero = jnp.zeros(shape, jnp.float32)
        one = jnp.ones(shape, jnp.float32)
        _, total, t0, t1, t2, softsum = lax.fori_loop(
            0, last + 1, step, (one, zero, zero, zero, zero, zero), unroll=4
        )
        for k, value in enumerate((t0, t1, t2)):
            out_ref[k, :, lanes] = 0.5 * (total + value)
        out_ref[3, :, lanes] = absorb * softsum

    share = rows // n
    for z in range(rows):
        for k in range(4):
            for h in range(halves):
                r = ((z % share) * 4 + k) * halves + h
                part[z // share, r:r + 1, :] = out_ref[k, z:z + 1, h * 128:(h + 1) * 128]
    exchange_and_combine(n, share, halves, me, col, barrier, part, recv, send_sems, recv_sems,
                         local_sem, colour_ref, transmit_ref)


def exchange_and_combine(n, share, halves, me, col, barrier, part, recv, send_sems, recv_sems,
                         local_sem, colour_ref, transmit_ref):
    def link(peer, slot):
        return pltpu.make_async_remote_copy(
            src_ref=part.at[peer],
            dst_ref=recv.at[slot],
            send_sem=send_sems.at[peer],
            recv_sem=recv_sems.at[slot],
            device_id=(peer, col),
            device_id_type=MESH_ID,
        )

    pl.semaphore_wait(barrier, n - 1)

    def send(i, carry):
        link(lax.rem(me + i, n), me).start()
        return carry

    lax.fori_loop(1, n, send, 0)
    own = pltpu.make_async_copy(part.at[me], recv.at[me], local_sem)
    own.start()
    own.wait()

    def finish(i, carry):
        peer = lax.rem(me + i, n)
        link(peer, peer).wait_send()
        link(peer, peer).wait_recv()
        return carry

    lax.fori_loop(1, n, finish, 0)
    cols = colour_ref.shape[-1]
    zero = jnp.zeros((share * halves, 128), jnp.float32)

    def value(block, k):
        pieces = [block[(r * 4 + k) * halves:(r * 4 + k + 1) * halves] for r in range(share)]
        return pieces[0] if share == 1 else jnp.concatenate(pieces, axis=0)

    def accumulate(d, carry):
        front, c0, c1, c2 = carry
        block = recv[d]
        seen = jnp.exp(-front)
        return (
            front + value(block, 3),
            c0 + value(block, 0) * seen,
            c1 + value(block, 1) * seen,
            c2 + value(block, 2) * seen,
        )

    front, c0, c1, c2 = lax.fori_loop(0, n, accumulate, (zero, zero, zero, zero))
    for k, c in enumerate((c0, c1, c2)):
        colour_ref[k] = c.reshape(share, cols)
    transmit_ref[...] = jnp.exp(-front).reshape(share, cols)


def march(density, front, back, left, right, absorb, n):
    depth, rows, cols = density.shape
    share = rows // n
    tiles = (n, share * 4 * cols // 128, 128)
    vmem = pltpu.MemorySpace.VMEM
    return pl.pallas_call(
        functools.partial(march_kernel, depth - 1, n),
        out_shape=(
            jax.ShapeDtypeStruct((3, share, cols), jnp.float32),
            jax.ShapeDtypeStruct((share, cols), jnp.float32),
        ),
        in_specs=[pl.BlockSpec(memory_space=vmem)] * 6,
        out_specs=(pl.BlockSpec(memory_space=vmem), pl.BlockSpec(memory_space=vmem)),
        scratch_shapes=[
            pltpu.VMEM((4, rows, cols), jnp.float32),
            pltpu.VMEM(tiles, jnp.float32),
            pltpu.VMEM(tiles, jnp.float32),
            pltpu.SemaphoreType.DMA((n,)),
            pltpu.SemaphoreType.DMA((n,)),
            pltpu.SemaphoreType.DMA,
        ],
        compiler_params=pltpu.CompilerParams(collective_id=0, has_side_effects=True),
    )(density, front, back, left, right, absorb)


def edge_kernel(dens_ref, first_ref, last_ref):
    depth, rows, cols = dens_ref.shape
    lane = lax.broadcasted_iota(jnp.int32, (rows, depth), 1)

    def step(x, carry):
        first, last = carry
        here = lane == x
        low = dens_ref[x, :, 0:128]
        high = dens_ref[x, :, cols - 128:cols]
        first = jnp.where(here, jnp.broadcast_to(low[:, 0:1], (rows, depth)), first)
        last = jnp.where(here, jnp.broadcast_to(high[:, 127:128], (rows, depth)), last)
        return first, last

    zero = jnp.zeros((rows, depth), jnp.float32)
    first, last = lax.fori_loop(0, depth, step, (zero, zero), unroll=8)
    first_ref[...] = first
    last_ref[...] = last


def edges(density):
    depth, rows, cols = density.shape
    vmem = pltpu.MemorySpace.VMEM
    plane = jax.ShapeDtypeStruct((rows, depth), jnp.float32)
    return pl.pallas_call(
        edge_kernel,
        out_shape=(plane, plane),
        in_specs=[pl.BlockSpec(memory_space=vmem)],
        out_specs=(pl.BlockSpec(memory_space=vmem), pl.BlockSpec(memory_space=vmem)),
    )(density)


def shifted(value, axis, forward):
    size = lax.axis_size(axis)
    pairs = [(i, i + 1) for i in range(size - 1)]
    if not forward:
        pairs = [(j, i) for i, j in pairs]
    return lax.ppermute(value, axis, pairs)


def local(density, absorb):
    depth, nz, cols = density.shape
    front = shifted(density[depth - 1], "gx", True)
    back = shifted(density[0], "gx", False)
    first_col, last_col = edges(density)
    left = shifted(last_col, "gy", True)
    right = shifted(first_col, "gy", False)
    return march(density, front, back, left, right, absorb, lax.axis_size("gx"))


def solution(mesh):
    placed = (P("gx", None, "gy"), P(None, "gy"))
    return jax.shard_map(
        local,
        mesh=mesh,
        in_specs=placed,
        out_specs=(P(None, "gx", "gy"), P("gx", "gy")),
        check_vma=False,
    )
```

```python
import functools

import jax
import jax.numpy as jnp
from jax import lax
from jax.experimental import pallas as pl
from jax.experimental.pallas import tpu as pltpu
from jax.sharding import PartitionSpec as P

SLOPES = (2.0, -1.5, 0.8)
OFFSETS = (0.0, 0.5, -0.3)
HALF_SLOPES = tuple(0.5 * v for v in SLOPES)
HALF_OFFSETS = tuple(0.5 * v for v in OFFSETS)
LOG2_E = 1.4426950408889634
MESH_ID = pl.DeviceIdType.MESH


def march_kernel(last, n, dens_ref, front_ref, back_ref, left_ref, right_ref, absorb_ref,
                 colour_ref, transmit_ref, out_ref, part, recv, send_sems, recv_sems, local_sem):
    rows, cols = dens_ref.shape[1], dens_ref.shape[2]
    shape = (rows, 128)
    lane = lax.broadcasted_iota(jnp.int32, shape, 1)
    row = lax.broadcasted_iota(jnp.int32, shape, 0)
    first_lane, last_lane = lane == 0, lane == 127
    top_row, bottom_row = row == 0, row == rows - 1
    halves = cols // 128
    me = lax.axis_index("gx")
    col = lax.axis_index("gy")
    barrier = pltpu.get_barrier_semaphore()

    def greet(i, carry):
        pl.semaphore_signal(barrier, inc=1, device_id=(lax.rem(me + i, n), col), device_id_type=MESH_ID)
        return carry

    lax.fori_loop(1, n, greet, 0)
    for h in range(halves):
        lanes = slice(h * 128, (h + 1) * 128)
        left_lanes = slice((h - 1) * 128, h * 128) if h > 0 else None
        right_lanes = slice((h + 1) * 128, (h + 2) * 128) if h + 1 < halves else None
        absorb = absorb_ref[:, lanes]
        fade = absorb * (-LOG2_E)

        def plane(ref_plane):
            return ref_plane[:, lanes]

        def step(x, carry):
            seen, total, t0, t1, t2, softsum = carry
            centre_plane = dens_ref.at[x]
            d = centre_plane[:, lanes]
            behind = jnp.where(x == 0, front_ref[:, lanes], dens_ref[jnp.maximum(x - 1, 0), :, lanes])
            ahead = jnp.where(x == last, back_ref[:, lanes], dens_ref[jnp.minimum(x + 1, last), :, lanes])
            span = left_ref.shape[1]
            halo_left = pltpu.roll(left_ref[...], lax.rem(span - x, span), 1)
            halo_right = pltpu.roll(right_ref[...], lax.rem(span + 127 - x, span), 1)
            from_left = pltpu.roll(d, 1, 1)
            from_right = pltpu.roll(d, 127, 1)
            if left_lanes is None:
                edge_left = halo_left
            else:
                edge_left = pltpu.roll(centre_plane[:, left_lanes], 1, 1)
            if right_lanes is None:
                edge_right = halo_right
            else:
                edge_right = pltpu.roll(centre_plane[:, right_lanes], 127, 1)
            left = jnp.where(first_lane, edge_left, from_left)
            right = jnp.where(last_lane, edge_right, from_right)
            above = jnp.where(top_row, 0.0, pltpu.roll(d, 1, 0))
            below = jnp.where(bottom_row, 0.0, pltpu.roll(d, rows - 1, 0))
            step_depth = ahead - behind
            step_row = below - above
            step_col = right - left
            facing = 0.18 * step_depth + 0.24 * step_row + 0.225 * step_col
            length2 = 0.25 * (step_depth * step_depth + step_row * step_row + step_col * step_col) + 1.0
            lighting = 0.25 + jnp.maximum(facing, 0.0) * lax.rsqrt(length2)
            soft = jnp.log(1.0 + jnp.exp(d))
            passed = jnp.exp2(fade * soft)
            seen_after = seen * passed
            weight = (seen - seen_after) * lighting
            return (
                seen_after,
                total + weight,
                t0 + weight * jnp.tanh(HALF_SLOPES[0] * d + HALF_OFFSETS[0]),
                t1 + weight * jnp.tanh(HALF_SLOPES[1] * d + HALF_OFFSETS[1]),
                t2 + weight * jnp.tanh(HALF_SLOPES[2] * d + HALF_OFFSETS[2]),
                softsum + soft,
            )

        zero = jnp.zeros(shape, jnp.float32)
        one = jnp.ones(shape, jnp.float32)
        _, total, t0, t1, t2, softsum = lax.fori_loop(
            0, last + 1, step, (one, zero, zero, zero, zero, zero), unroll=4
        )
        for k, value in enumerate((t0, t1, t2)):
            out_ref[k, :, lanes] = 0.5 * (total + value)
        out_ref[3, :, lanes] = absorb * softsum

    share = rows // n
    for z in range(rows):
        for k in range(4):
            for h in range(halves):
                r = ((z % share) * 4 + k) * halves + h
                part[z // share, r:r + 1, :] = out_ref[k, z:z + 1, h * 128:(h + 1) * 128]
    exchange_and_combine(n, share, halves, me, col, barrier, part, recv, send_sems, recv_sems,
                         local_sem, colour_ref, transmit_ref)


def exchange_and_combine(n, share, halves, me, col, barrier, part, recv, send_sems, recv_sems,
                         local_sem, colour_ref, transmit_ref):
    def link(peer, slot):
        return pltpu.make_async_remote_copy(
            src_ref=part.at[peer],
            dst_ref=recv.at[slot],
            send_sem=send_sems.at[peer],
            recv_sem=recv_sems.at[slot],
            device_id=(peer, col),
            device_id_type=MESH_ID,
        )

    pl.semaphore_wait(barrier, n - 1)

    def send(i, carry):
        link(lax.rem(me + i, n), me).start()
        return carry

    lax.fori_loop(1, n, send, 0)
    own = pltpu.make_async_copy(part.at[me], recv.at[me], local_sem)
    own.start()
    own.wait()

    def finish(i, carry):
        peer = lax.rem(me + i, n)
        link(peer, peer).wait_send()
        link(peer, peer).wait_recv()
        return carry

    lax.fori_loop(1, n, finish, 0)
    cols = colour_ref.shape[-1]
    zero = jnp.zeros((share * halves, 128), jnp.float32)

    def value(block, k):
        pieces = [block[(r * 4 + k) * halves:(r * 4 + k + 1) * halves] for r in range(share)]
        return pieces[0] if share == 1 else jnp.concatenate(pieces, axis=0)

    def accumulate(d, carry):
        front, c0, c1, c2 = carry
        block = recv[d]
        seen = jnp.exp(-front)
        return (
            front + value(block, 3),
            c0 + value(block, 0) * seen,
            c1 + value(block, 1) * seen,
            c2 + value(block, 2) * seen,
        )

    front, c0, c1, c2 = lax.fori_loop(0, n, accumulate, (zero, zero, zero, zero))
    for k, c in enumerate((c0, c1, c2)):
        colour_ref[k] = c.reshape(share, cols)
    transmit_ref[...] = jnp.exp(-front).reshape(share, cols)


def march(density, front, back, left, right, absorb, n):
    depth, rows, cols = density.shape
    share = rows // n
    tiles = (n, share * 4 * cols // 128, 128)
    vmem = pltpu.MemorySpace.VMEM
    return pl.pallas_call(
        functools.partial(march_kernel, depth - 1, n),
        out_shape=(
            jax.ShapeDtypeStruct((3, share, cols), jnp.float32),
            jax.ShapeDtypeStruct((share, cols), jnp.float32),
        ),
        in_specs=[pl.BlockSpec(memory_space=vmem)] * 6,
        out_specs=(pl.BlockSpec(memory_space=vmem), pl.BlockSpec(memory_space=vmem)),
        scratch_shapes=[
            pltpu.VMEM((4, rows, cols), jnp.float32),
            pltpu.VMEM(tiles, jnp.float32),
            pltpu.VMEM(tiles, jnp.float32),
            pltpu.SemaphoreType.DMA((n,)),
            pltpu.SemaphoreType.DMA((n,)),
            pltpu.SemaphoreType.DMA,
        ],
        compiler_params=pltpu.CompilerParams(collective_id=0, has_side_effects=True),
    )(density, front, back, left, right, absorb)


def edge_kernel(chunk, dens_ref, first_ref, last_ref):
    _, rows, cols = dens_ref.shape
    depth = first_ref.shape[1]
    lane = lax.broadcasted_iota(jnp.int32, (rows, depth), 1)
    start = pl.program_id(0) * chunk

    @pl.when(pl.program_id(0) == 0)
    def _():
        first_ref[...] = jnp.zeros((rows, depth), jnp.float32)
        last_ref[...] = jnp.zeros((rows, depth), jnp.float32)

    def step(t, carry):
        first, last = carry
        here = lane == start + t
        low = dens_ref[t, :, 0:128]
        high = dens_ref[t, :, cols - 128:cols]
        first = jnp.where(here, jnp.broadcast_to(low[:, 0:1], (rows, depth)), first)
        last = jnp.where(here, jnp.broadcast_to(high[:, 127:128], (rows, depth)), last)
        return first, last

    first, last = lax.fori_loop(0, chunk, step, (first_ref[...], last_ref[...]), unroll=8)
    first_ref[...] = first
    last_ref[...] = last


def edges(density):
    depth, rows, cols = density.shape
    chunk = 16 if depth % 16 == 0 else depth
    plane = jax.ShapeDtypeStruct((rows, depth), jnp.float32)
    resident = pl.BlockSpec((rows, depth), lambda i: (0, 0))
    return pl.pallas_call(
        functools.partial(edge_kernel, chunk),
        out_shape=(plane, plane),
        grid=(depth // chunk,),
        in_specs=[pl.BlockSpec((chunk, rows, cols), lambda i: (i, 0, 0))],
        out_specs=(resident, resident),
    )(density)


def shifted(value, axis, forward):
    size = lax.axis_size(axis)
    pairs = [(i, i + 1) for i in range(size - 1)]
    if not forward:
        pairs = [(j, i) for i, j in pairs]
    return lax.ppermute(value, axis, pairs)


def local(density, absorb):
    depth, nz, cols = density.shape
    front = shifted(density[depth - 1], "gx", True)
    back = shifted(density[0], "gx", False)
    first_col, last_col = edges(density)
    left = shifted(last_col, "gy", True)
    right = shifted(first_col, "gy", False)
    return march(density, front, back, left, right, absorb, lax.axis_size("gx"))


def solution(mesh):
    placed = (P("gx", None, "gy"), P(None, "gy"))
    return jax.shard_map(
        local,
        mesh=mesh,
        in_specs=placed,
        out_specs=(P(None, "gx", "gy"), P("gx", "gy")),
        check_vma=False,
    )
```

```python
import functools

import jax
import jax.numpy as jnp
from jax import lax
from jax.experimental import pallas as pl
from jax.experimental.pallas import tpu as pltpu
from jax.sharding import PartitionSpec as P

SLOPES = (2.0, -1.5, 0.8)
OFFSETS = (0.0, 0.5, -0.3)
HALF_SLOPES = tuple(0.5 * v for v in SLOPES)
HALF_OFFSETS = tuple(0.5 * v for v in OFFSETS)
LOG2_E = 1.4426950408889634
MESH_ID = pl.DeviceIdType.MESH


def march_kernel(last, n, dens_ref, front_ref, back_ref, left_ref, right_ref, absorb_ref,
                 colour_ref, transmit_ref, out_ref, part, recv, send_sems, recv_sems, local_sem):
    rows, cols = dens_ref.shape[1], dens_ref.shape[2]
    shape = (rows, 128)
    lane = lax.broadcasted_iota(jnp.int32, shape, 1)
    row = lax.broadcasted_iota(jnp.int32, shape, 0)
    first_lane, last_lane = lane == 0, lane == 127
    top_row, bottom_row = row == 0, row == rows - 1
    halves = cols // 128
    me = lax.axis_index("gx")
    col = lax.axis_index("gy")
    barrier = pltpu.get_barrier_semaphore()

    def greet(i, carry):
        pl.semaphore_signal(barrier, inc=1, device_id=(lax.rem(me + i, n), col), device_id_type=MESH_ID)
        return carry

    lax.fori_loop(1, n, greet, 0)
    for h in range(halves):
        lanes = slice(h * 128, (h + 1) * 128)
        left_lanes = slice((h - 1) * 128, h * 128) if h > 0 else None
        right_lanes = slice((h + 1) * 128, (h + 2) * 128) if h + 1 < halves else None
        absorb = absorb_ref[:, lanes]
        fade = absorb * (-LOG2_E)

        def plane(ref_plane):
            return ref_plane[:, lanes]

        def step(x, carry):
            seen, total, t0, t1, t2, softsum = carry
            centre_plane = dens_ref.at[x]
            d = centre_plane[:, lanes]
            behind = jnp.where(x == 0, front_ref[:, lanes], dens_ref[jnp.maximum(x - 1, 0), :, lanes])
            ahead = jnp.where(x == last, back_ref[:, lanes], dens_ref[jnp.minimum(x + 1, last), :, lanes])
            span = left_ref.shape[1]
            halo_left = pltpu.roll(left_ref[...], lax.rem(span - x, span), 1)
            halo_right = pltpu.roll(right_ref[...], lax.rem(span + 127 - x, span), 1)
            from_left = pltpu.roll(d, 1, 1)
            from_right = pltpu.roll(d, 127, 1)
            if left_lanes is None:
                edge_left = halo_left
            else:
                edge_left = pltpu.roll(centre_plane[:, left_lanes], 1, 1)
            if right_lanes is None:
                edge_right = halo_right
            else:
                edge_right = pltpu.roll(centre_plane[:, right_lanes], 127, 1)
            left = jnp.where(first_lane, edge_left, from_left)
            right = jnp.where(last_lane, edge_right, from_right)
            above = jnp.where(top_row, 0.0, pltpu.roll(d, 1, 0))
            below = jnp.where(bottom_row, 0.0, pltpu.roll(d, rows - 1, 0))
            step_depth = ahead - behind
            step_row = below - above
            step_col = right - left
            facing = 0.18 * step_depth + 0.24 * step_row + 0.225 * step_col
            length2 = 0.25 * (step_depth * step_depth + step_row * step_row + step_col * step_col) + 1.0
            lighting = 0.25 + jnp.maximum(facing, 0.0) * lax.rsqrt(length2)
            soft = jnp.log(1.0 + jnp.exp(d))
            passed = jnp.exp2(fade * soft)
            seen_after = seen * passed
            weight = (seen - seen_after) * lighting
            return (
                seen_after,
                total + weight,
                t0 + weight * jnp.tanh(HALF_SLOPES[0] * d + HALF_OFFSETS[0]),
                t1 + weight * jnp.tanh(HALF_SLOPES[1] * d + HALF_OFFSETS[1]),
                t2 + weight * jnp.tanh(HALF_SLOPES[2] * d + HALF_OFFSETS[2]),
                softsum + soft,
            )

        zero = jnp.zeros(shape, jnp.float32)
        one = jnp.ones(shape, jnp.float32)
        _, total, t0, t1, t2, softsum = lax.fori_loop(
            0, last + 1, step, (one, zero, zero, zero, zero, zero), unroll=4
        )
        for k, value in enumerate((t0, t1, t2)):
            out_ref[k, :, lanes] = 0.5 * (total + value)
        out_ref[3, :, lanes] = absorb * softsum

    share = rows // n
    for z in range(rows):
        for k in range(4):
            for h in range(halves):
                r = ((z % share) * 4 + k) * halves + h
                part[z // share, r:r + 1, :] = out_ref[k, z:z + 1, h * 128:(h + 1) * 128]
    exchange_and_combine(n, share, halves, me, col, barrier, part, recv, send_sems, recv_sems,
                         local_sem, colour_ref, transmit_ref)


def exchange_and_combine(n, share, halves, me, col, barrier, part, recv, send_sems, recv_sems,
                         local_sem, colour_ref, transmit_ref):
    def link(peer, slot):
        return pltpu.make_async_remote_copy(
            src_ref=part.at[peer],
            dst_ref=recv.at[slot],
            send_sem=send_sems.at[peer],
            recv_sem=recv_sems.at[slot],
            device_id=(peer, col),
            device_id_type=MESH_ID,
        )

    pl.semaphore_wait(barrier, n - 1)

    def send(i, carry):
        link(lax.rem(me + i, n), me).start()
        return carry

    lax.fori_loop(1, n, send, 0)
    own = pltpu.make_async_copy(part.at[me], recv.at[me], local_sem)
    own.start()
    own.wait()

    def finish(i, carry):
        peer = lax.rem(me + i, n)
        link(peer, peer).wait_send()
        link(peer, peer).wait_recv()
        return carry

    lax.fori_loop(1, n, finish, 0)
    cols = colour_ref.shape[-1]
    zero = jnp.zeros((share * halves, 128), jnp.float32)

    def value(block, k):
        pieces = [block[(r * 4 + k) * halves:(r * 4 + k + 1) * halves] for r in range(share)]
        return pieces[0] if share == 1 else jnp.concatenate(pieces, axis=0)

    def accumulate(d, carry):
        front, c0, c1, c2 = carry
        block = recv[d]
        seen = jnp.exp(-front)
        return (
            front + value(block, 3),
            c0 + value(block, 0) * seen,
            c1 + value(block, 1) * seen,
            c2 + value(block, 2) * seen,
        )

    front, c0, c1, c2 = lax.fori_loop(0, n, accumulate, (zero, zero, zero, zero))
    for k, c in enumerate((c0, c1, c2)):
        colour_ref[k] = c.reshape(share, cols)
    transmit_ref[...] = jnp.exp(-front).reshape(share, cols)


def march(density, front, back, left, right, absorb, n):
    depth, rows, cols = density.shape
    share = rows // n
    tiles = (n, share * 4 * cols // 128, 128)
    vmem = pltpu.MemorySpace.VMEM
    return pl.pallas_call(
        functools.partial(march_kernel, depth - 1, n),
        out_shape=(
            jax.ShapeDtypeStruct((3, share, cols), jnp.float32),
            jax.ShapeDtypeStruct((share, cols), jnp.float32),
        ),
        in_specs=[pl.BlockSpec(memory_space=vmem)] * 6,
        out_specs=(pl.BlockSpec(memory_space=vmem), pl.BlockSpec(memory_space=vmem)),
        scratch_shapes=[
            pltpu.VMEM((4, rows, cols), jnp.float32),
            pltpu.VMEM(tiles, jnp.float32),
            pltpu.VMEM(tiles, jnp.float32),
            pltpu.SemaphoreType.DMA((n,)),
            pltpu.SemaphoreType.DMA((n,)),
            pltpu.SemaphoreType.DMA,
        ],
        compiler_params=pltpu.CompilerParams(collective_id=0, has_side_effects=True),
    )(density, front, back, left, right, absorb)


def edge_kernel(dens_ref, first_ref, last_ref):
    depth, rows, cols = dens_ref.shape
    for z in range(rows):
        low = jnp.transpose(dens_ref[:, z, 0:128])
        high = jnp.transpose(dens_ref[:, z, cols - 128:cols])
        first_ref[z:z + 1, :] = low[0:1, :]
        last_ref[z:z + 1, :] = high[127:128, :]


def edges(density):
    depth, rows, cols = density.shape
    vmem = pltpu.MemorySpace.VMEM
    plane = jax.ShapeDtypeStruct((rows, depth), jnp.float32)
    return pl.pallas_call(
        edge_kernel,
        out_shape=(plane, plane),
        in_specs=[pl.BlockSpec(memory_space=vmem)],
        out_specs=(pl.BlockSpec(memory_space=vmem), pl.BlockSpec(memory_space=vmem)),
    )(density)


def shifted(value, axis, forward):
    size = lax.axis_size(axis)
    pairs = [(i, i + 1) for i in range(size - 1)]
    if not forward:
        pairs = [(j, i) for i, j in pairs]
    return lax.ppermute(value, axis, pairs)


def local(density, absorb):
    depth, nz, cols = density.shape
    front = shifted(density[depth - 1], "gx", True)
    back = shifted(density[0], "gx", False)
    first_col, last_col = edges(density)
    left = shifted(last_col, "gy", True)
    right = shifted(first_col, "gy", False)
    return march(density, front, back, left, right, absorb, lax.axis_size("gx"))


def solution(mesh):
    placed = (P("gx", None, "gy"), P(None, "gy"))
    return jax.shard_map(
        local,
        mesh=mesh,
        in_specs=placed,
        out_specs=(P(None, "gx", "gy"), P("gx", "gy")),
        check_vma=False,
    )
```

```python
import functools

import jax
import jax.numpy as jnp
from jax import lax
from jax.experimental import pallas as pl
from jax.experimental.pallas import tpu as pltpu
from jax.sharding import PartitionSpec as P

SLOPES = (2.0, -1.5, 0.8)
OFFSETS = (0.0, 0.5, -0.3)
HALF_SLOPES = tuple(0.5 * v for v in SLOPES)
HALF_OFFSETS = tuple(0.5 * v for v in OFFSETS)
LOG2_E = 1.4426950408889634
MESH_ID = pl.DeviceIdType.MESH


def march_kernel(last, n, dens_ref, front_ref, back_ref, left_ref, right_ref, absorb_ref,
                 colour_ref, transmit_ref, out_ref, part, mixed, recv_pair, recv,
                 send_pair, got_pair, send_sems, recv_sems, local_sem):
    rows, cols = dens_ref.shape[1], dens_ref.shape[2]
    shape = (rows, 128)
    lane = lax.broadcasted_iota(jnp.int32, shape, 1)
    row = lax.broadcasted_iota(jnp.int32, shape, 0)
    first_lane, last_lane = lane == 0, lane == 127
    top_row, bottom_row = row == 0, row == rows - 1
    halves = cols // 128
    me = lax.axis_index("gx")
    col = lax.axis_index("gy")
    barrier = pltpu.get_barrier_semaphore()

    pairs = n // 2
    parity = lax.rem(me, 2)
    chip = me // 2
    sems = (send_pair, got_pair, send_sems, recv_sems, local_sem)

    def greet(i, carry):
        peer = 2 * lax.rem(chip + i, pairs) + parity
        pl.semaphore_signal(barrier, inc=1, device_id=(peer, col), device_id_type=MESH_ID)
        return carry

    pl.semaphore_signal(barrier, inc=1, device_id=(me + 1 - 2 * parity, col), device_id_type=MESH_ID)
    lax.fori_loop(1, pairs, greet, 0)
    for h in range(halves):
        lanes = slice(h * 128, (h + 1) * 128)
        left_lanes = slice((h - 1) * 128, h * 128) if h > 0 else None
        right_lanes = slice((h + 1) * 128, (h + 2) * 128) if h + 1 < halves else None
        absorb = absorb_ref[:, lanes]
        fade = absorb * (-LOG2_E)

        def plane(ref_plane):
            return ref_plane[:, lanes]

        def step(x, carry):
            seen, total, t0, t1, t2, softsum = carry
            centre_plane = dens_ref.at[x]
            d = centre_plane[:, lanes]
            behind = jnp.where(x == 0, front_ref[:, lanes], dens_ref[jnp.maximum(x - 1, 0), :, lanes])
            ahead = jnp.where(x == last, back_ref[:, lanes], dens_ref[jnp.minimum(x + 1, last), :, lanes])
            span = left_ref.shape[1]
            halo_left = pltpu.roll(left_ref[...], lax.rem(span - x, span), 1)
            halo_right = pltpu.roll(right_ref[...], lax.rem(span + 127 - x, span), 1)
            from_left = pltpu.roll(d, 1, 1)
            from_right = pltpu.roll(d, 127, 1)
            if left_lanes is None:
                edge_left = halo_left
            else:
                edge_left = pltpu.roll(centre_plane[:, left_lanes], 1, 1)
            if right_lanes is None:
                edge_right = halo_right
            else:
                edge_right = pltpu.roll(centre_plane[:, right_lanes], 127, 1)
            left = jnp.where(first_lane, edge_left, from_left)
            right = jnp.where(last_lane, edge_right, from_right)
            above = jnp.where(top_row, 0.0, pltpu.roll(d, 1, 0))
            below = jnp.where(bottom_row, 0.0, pltpu.roll(d, rows - 1, 0))
            step_depth = ahead - behind
            step_row = below - above
            step_col = right - left
            facing = 0.18 * step_depth + 0.24 * step_row + 0.225 * step_col
            length2 = 0.25 * (step_depth * step_depth + step_row * step_row + step_col * step_col) + 1.0
            lighting = 0.25 + jnp.maximum(facing, 0.0) * lax.rsqrt(length2)
            soft = jnp.log(1.0 + jnp.exp(d))
            passed = jnp.exp2(fade * soft)
            seen_after = seen * passed
            weight = (seen - seen_after) * lighting
            return (
                seen_after,
                total + weight,
                t0 + weight * jnp.tanh(HALF_SLOPES[0] * d + HALF_OFFSETS[0]),
                t1 + weight * jnp.tanh(HALF_SLOPES[1] * d + HALF_OFFSETS[1]),
                t2 + weight * jnp.tanh(HALF_SLOPES[2] * d + HALF_OFFSETS[2]),
                softsum + soft,
            )

        zero = jnp.zeros(shape, jnp.float32)
        one = jnp.ones(shape, jnp.float32)
        _, total, t0, t1, t2, softsum = lax.fori_loop(
            0, last + 1, step, (one, zero, zero, zero, zero, zero), unroll=4
        )
        for k, value in enumerate((t0, t1, t2)):
            out_ref[k, :, lanes] = 0.5 * (total + value)
        out_ref[3, :, lanes] = absorb * softsum

    share = rows // n
    pairs = n // 2
    for z in range(rows):
        owner = z // share
        slot = (owner % 2) * pairs + owner // 2
        for k in range(4):
            for h in range(halves):
                r = ((z % share) * 4 + k) * halves + h
                part[slot, r:r + 1, :] = out_ref[k, z:z + 1, h * 128:(h + 1) * 128]
    exchange_and_combine(n, share, halves, me, col, barrier, part, mixed, recv_pair, recv,
                         sems, colour_ref, transmit_ref)


def merge(front, back, share, halves):
    def rows_of(k):
        return [(r * 4 + k) * halves + h for r in range(share) for h in range(halves)]

    seen = jnp.exp(-jnp.concatenate([front[i:i + 1] for i in rows_of(3)], axis=0))
    pieces = [None] * (share * 4 * halves)
    for k in range(4):
        idx = rows_of(k)
        f = jnp.concatenate([front[i:i + 1] for i in idx], axis=0)
        b = jnp.concatenate([back[i:i + 1] for i in idx], axis=0)
        merged = f + b if k == 3 else f + seen * b
        for j, i in enumerate(idx):
            pieces[i] = merged[j:j + 1]
    return jnp.concatenate(pieces, axis=0)


def exchange_and_combine(n, share, halves, me, col, barrier, part, mixed, recv_pair, recv,
                         sems, colour_ref, transmit_ref):
    pairs = n // 2
    parity = lax.rem(me, 2)
    partner = me + 1 - 2 * parity
    chip = me // 2
    send_pair, got_pair, send_sems, recv_sems, local_sem = sems
    pl.semaphore_wait(barrier, pairs)

    swap = pltpu.make_async_remote_copy(
        src_ref=part.at[pl.ds((1 - parity) * pairs, pairs)],
        dst_ref=recv_pair,
        send_sem=send_pair,
        recv_sem=got_pair,
        device_id=(partner, col),
        device_id_type=MESH_ID,
    )
    swap.start()
    swap.wait()

    def combine_pair(j, carry):
        mine = part[parity * pairs + j]
        theirs = recv_pair[j]
        first = parity == 0
        front = jnp.where(first, mine, theirs)
        back = jnp.where(first, theirs, mine)
        mixed[j] = merge(front, back, share, halves)
        return carry

    lax.fori_loop(0, pairs, combine_pair, 0)

    def link(j, slot):
        return pltpu.make_async_remote_copy(
            src_ref=mixed.at[j],
            dst_ref=recv.at[slot],
            send_sem=send_sems.at[j],
            recv_sem=recv_sems.at[slot],
            device_id=(2 * j + parity, col),
            device_id_type=MESH_ID,
        )

    def send(i, carry):
        link(lax.rem(chip + i, pairs), chip).start()
        return carry

    lax.fori_loop(1, pairs, send, 0)
    own = pltpu.make_async_copy(mixed.at[chip], recv.at[chip], local_sem)
    own.start()
    own.wait()

    def finish(i, carry):
        j = lax.rem(chip + i, pairs)
        link(j, j).wait_send()
        link(j, j).wait_recv()
        return carry

    lax.fori_loop(1, pairs, finish, 0)
    cols = colour_ref.shape[-1]
    zero = jnp.zeros((share * halves, 128), jnp.float32)

    def value(block, k):
        pieces = [block[(r * 4 + k) * halves:(r * 4 + k + 1) * halves] for r in range(share)]
        return pieces[0] if share == 1 else jnp.concatenate(pieces, axis=0)

    def accumulate(d, carry):
        front, c0, c1, c2 = carry
        block = recv[d]
        seen = jnp.exp(-front)
        return (
            front + value(block, 3),
            c0 + value(block, 0) * seen,
            c1 + value(block, 1) * seen,
            c2 + value(block, 2) * seen,
        )

    front, c0, c1, c2 = lax.fori_loop(0, pairs, accumulate, (zero, zero, zero, zero))
    for k, c in enumerate((c0, c1, c2)):
        colour_ref[k] = c.reshape(share, cols)
    transmit_ref[...] = jnp.exp(-front).reshape(share, cols)


def march(density, front, back, left, right, absorb, n):
    depth, rows, cols = density.shape
    share = rows // n
    tiles = (n, share * 4 * cols // 128, 128)
    half_tiles = (n // 2,) + tiles[1:]
    vmem = pltpu.MemorySpace.VMEM
    return pl.pallas_call(
        functools.partial(march_kernel, depth - 1, n),
        out_shape=(
            jax.ShapeDtypeStruct((3, share, cols), jnp.float32),
            jax.ShapeDtypeStruct((share, cols), jnp.float32),
        ),
        in_specs=[pl.BlockSpec(memory_space=vmem)] * 6,
        out_specs=(pl.BlockSpec(memory_space=vmem), pl.BlockSpec(memory_space=vmem)),
        scratch_shapes=[
            pltpu.VMEM((4, rows, cols), jnp.float32),
            pltpu.VMEM(tiles, jnp.float32),
            pltpu.VMEM(half_tiles, jnp.float32),
            pltpu.VMEM(half_tiles, jnp.float32),
            pltpu.VMEM(half_tiles, jnp.float32),
            pltpu.SemaphoreType.DMA,
            pltpu.SemaphoreType.DMA,
            pltpu.SemaphoreType.DMA((n // 2,)),
            pltpu.SemaphoreType.DMA((n // 2,)),
            pltpu.SemaphoreType.DMA,
        ],
        compiler_params=pltpu.CompilerParams(collective_id=0, has_side_effects=True),
    )(density, front, back, left, right, absorb)


def edge_kernel(dens_ref, first_ref, last_ref):
    depth, rows, cols = dens_ref.shape
    for z in range(rows):
        low = jnp.transpose(dens_ref[:, z, 0:128])
        high = jnp.transpose(dens_ref[:, z, cols - 128:cols])
        first_ref[z:z + 1, :] = low[0:1, :]
        last_ref[z:z + 1, :] = high[127:128, :]


def edges(density):
    depth, rows, cols = density.shape
    vmem = pltpu.MemorySpace.VMEM
    plane = jax.ShapeDtypeStruct((rows, depth), jnp.float32)
    return pl.pallas_call(
        edge_kernel,
        out_shape=(plane, plane),
        in_specs=[pl.BlockSpec(memory_space=vmem)],
        out_specs=(pl.BlockSpec(memory_space=vmem), pl.BlockSpec(memory_space=vmem)),
    )(density)


def shifted(value, axis, forward):
    size = lax.axis_size(axis)
    pairs = [(i, i + 1) for i in range(size - 1)]
    if not forward:
        pairs = [(j, i) for i, j in pairs]
    return lax.ppermute(value, axis, pairs)


def local(density, absorb):
    depth, nz, cols = density.shape
    front = shifted(density[depth - 1], "gx", True)
    back = shifted(density[0], "gx", False)
    first_col, last_col = edges(density)
    left = shifted(last_col, "gy", True)
    right = shifted(first_col, "gy", False)
    return march(density, front, back, left, right, absorb, lax.axis_size("gx"))


def solution(mesh):
    placed = (P("gx", None, "gy"), P(None, "gy"))
    return jax.shard_map(
        local,
        mesh=mesh,
        in_specs=placed,
        out_specs=(P(None, "gx", "gy"), P("gx", "gy")),
        check_vma=False,
    )
```

```python
import functools

import jax
import jax.numpy as jnp
from jax import lax
from jax.experimental import pallas as pl
from jax.experimental.pallas import tpu as pltpu
from jax.sharding import PartitionSpec as P

SLOPES = (2.0, -1.5, 0.8)
OFFSETS = (0.0, 0.5, -0.3)
HALF_SLOPES = tuple(0.5 * v for v in SLOPES)
HALF_OFFSETS = tuple(0.5 * v for v in OFFSETS)
LOG2_E = 1.4426950408889634
MESH_ID = pl.DeviceIdType.MESH


def march_kernel(last, n, dens_ref, front_ref, back_ref, left_ref, right_ref, absorb_ref,
                 colour_ref, transmit_ref, out_ref, part, mixed, recv_pair, recv,
                 send_pair, got_pair, send_sems, recv_sems, local_sem):
    rows, cols = dens_ref.shape[1], dens_ref.shape[2]
    shape = (rows, 128)
    lane = lax.broadcasted_iota(jnp.int32, shape, 1)
    row = lax.broadcasted_iota(jnp.int32, shape, 0)
    first_lane, last_lane = lane == 0, lane == 127
    top_row, bottom_row = row == 0, row == rows - 1
    halves = cols // 128
    me = lax.axis_index("gx")
    col = lax.axis_index("gy")
    barrier = pltpu.get_barrier_semaphore()

    pairs = n // 2
    parity = lax.rem(me, 2)
    chip = me // 2
    sems = (send_pair, got_pair, send_sems, recv_sems, local_sem)

    def greet(i, carry):
        peer = 2 * lax.rem(chip + i, pairs) + parity
        pl.semaphore_signal(barrier, inc=1, device_id=(peer, col), device_id_type=MESH_ID)
        return carry

    pl.semaphore_signal(barrier, inc=1, device_id=(me + 1 - 2 * parity, col), device_id_type=MESH_ID)
    lax.fori_loop(1, pairs, greet, 0)
    for h in range(halves):
        lanes = slice(h * 128, (h + 1) * 128)
        left_lanes = slice((h - 1) * 128, h * 128) if h > 0 else None
        right_lanes = slice((h + 1) * 128, (h + 2) * 128) if h + 1 < halves else None
        absorb = absorb_ref[:, lanes]
        fade = absorb * (-LOG2_E)

        def plane(ref_plane):
            return ref_plane[:, lanes]

        def step(x, carry):
            seen, total, t0, t1, t2, softsum = carry
            centre_plane = dens_ref.at[x]
            d = centre_plane[:, lanes]
            behind = jnp.where(x == 0, front_ref[:, lanes], dens_ref[jnp.maximum(x - 1, 0), :, lanes])
            ahead = jnp.where(x == last, back_ref[:, lanes], dens_ref[jnp.minimum(x + 1, last), :, lanes])
            span = left_ref.shape[1]
            halo_left = pltpu.roll(left_ref[...], lax.rem(span - x, span), 1)
            halo_right = pltpu.roll(right_ref[...], lax.rem(span + 127 - x, span), 1)
            from_left = pltpu.roll(d, 1, 1)
            from_right = pltpu.roll(d, 127, 1)
            if left_lanes is None:
                edge_left = halo_left
            else:
                edge_left = pltpu.roll(centre_plane[:, left_lanes], 1, 1)
            if right_lanes is None:
                edge_right = halo_right
            else:
                edge_right = pltpu.roll(centre_plane[:, right_lanes], 127, 1)
            left = jnp.where(first_lane, edge_left, from_left)
            right = jnp.where(last_lane, edge_right, from_right)
            above = jnp.where(top_row, 0.0, pltpu.roll(d, 1, 0))
            below = jnp.where(bottom_row, 0.0, pltpu.roll(d, rows - 1, 0))
            step_depth = ahead - behind
            step_row = below - above
            step_col = right - left
            facing = 0.18 * step_depth + 0.24 * step_row + 0.225 * step_col
            length2 = 0.25 * (step_depth * step_depth + step_row * step_row + step_col * step_col) + 1.0
            lighting = 0.25 + jnp.maximum(facing, 0.0) * lax.rsqrt(length2)
            soft = jnp.log(1.0 + jnp.exp(d))
            passed = jnp.exp2(fade * soft)
            seen_after = seen * passed
            weight = (seen - seen_after) * lighting
            return (
                seen_after,
                total + weight,
                t0 + weight * jnp.tanh(HALF_SLOPES[0] * d + HALF_OFFSETS[0]),
                t1 + weight * jnp.tanh(HALF_SLOPES[1] * d + HALF_OFFSETS[1]),
                t2 + weight * jnp.tanh(HALF_SLOPES[2] * d + HALF_OFFSETS[2]),
                softsum + soft,
            )

        zero = jnp.zeros(shape, jnp.float32)
        one = jnp.ones(shape, jnp.float32)
        _, total, t0, t1, t2, softsum = lax.fori_loop(
            0, last + 1, step, (one, zero, zero, zero, zero, zero), unroll=8
        )
        for k, value in enumerate((t0, t1, t2)):
            out_ref[k, :, lanes] = 0.5 * (total + value)
        out_ref[3, :, lanes] = absorb * softsum

    share = rows // n
    pairs = n // 2
    for z in range(rows):
        owner = z // share
        slot = (owner % 2) * pairs + owner // 2
        for k in range(4):
            for h in range(halves):
                r = ((z % share) * 4 + k) * halves + h
                part[slot, r:r + 1, :] = out_ref[k, z:z + 1, h * 128:(h + 1) * 128]
    exchange_and_combine(n, share, halves, me, col, barrier, part, mixed, recv_pair, recv,
                         sems, colour_ref, transmit_ref)


def merge(front, back, share, halves):
    def rows_of(k):
        return [(r * 4 + k) * halves + h for r in range(share) for h in range(halves)]

    seen = jnp.exp(-jnp.concatenate([front[i:i + 1] for i in rows_of(3)], axis=0))
    pieces = [None] * (share * 4 * halves)
    for k in range(4):
        idx = rows_of(k)
        f = jnp.concatenate([front[i:i + 1] for i in idx], axis=0)
        b = jnp.concatenate([back[i:i + 1] for i in idx], axis=0)
        merged = f + b if k == 3 else f + seen * b
        for j, i in enumerate(idx):
            pieces[i] = merged[j:j + 1]
    return jnp.concatenate(pieces, axis=0)


def exchange_and_combine(n, share, halves, me, col, barrier, part, mixed, recv_pair, recv,
                         sems, colour_ref, transmit_ref):
    pairs = n // 2
    parity = lax.rem(me, 2)
    partner = me + 1 - 2 * parity
    chip = me // 2
    send_pair, got_pair, send_sems, recv_sems, local_sem = sems
    pl.semaphore_wait(barrier, pairs)

    swap = pltpu.make_async_remote_copy(
        src_ref=part.at[pl.ds((1 - parity) * pairs, pairs)],
        dst_ref=recv_pair,
        send_sem=send_pair,
        recv_sem=got_pair,
        device_id=(partner, col),
        device_id_type=MESH_ID,
    )
    swap.start()
    swap.wait()

    def combine_pair(j, carry):
        mine = part[parity * pairs + j]
        theirs = recv_pair[j]
        first = parity == 0
        front = jnp.where(first, mine, theirs)
        back = jnp.where(first, theirs, mine)
        mixed[j] = merge(front, back, share, halves)
        return carry

    lax.fori_loop(0, pairs, combine_pair, 0)

    def link(j, slot):
        return pltpu.make_async_remote_copy(
            src_ref=mixed.at[j],
            dst_ref=recv.at[slot],
            send_sem=send_sems.at[j],
            recv_sem=recv_sems.at[slot],
            device_id=(2 * j + parity, col),
            device_id_type=MESH_ID,
        )

    def send(i, carry):
        link(lax.rem(chip + i, pairs), chip).start()
        return carry

    lax.fori_loop(1, pairs, send, 0)
    own = pltpu.make_async_copy(mixed.at[chip], recv.at[chip], local_sem)
    own.start()
    own.wait()

    def finish(i, carry):
        j = lax.rem(chip + i, pairs)
        link(j, j).wait_send()
        link(j, j).wait_recv()
        return carry

    lax.fori_loop(1, pairs, finish, 0)
    cols = colour_ref.shape[-1]
    zero = jnp.zeros((share * halves, 128), jnp.float32)

    def value(block, k):
        pieces = [block[(r * 4 + k) * halves:(r * 4 + k + 1) * halves] for r in range(share)]
        return pieces[0] if share == 1 else jnp.concatenate(pieces, axis=0)

    def accumulate(d, carry):
        front, c0, c1, c2 = carry
        block = recv[d]
        seen = jnp.exp(-front)
        return (
            front + value(block, 3),
            c0 + value(block, 0) * seen,
            c1 + value(block, 1) * seen,
            c2 + value(block, 2) * seen,
        )

    front, c0, c1, c2 = lax.fori_loop(0, pairs, accumulate, (zero, zero, zero, zero))
    for k, c in enumerate((c0, c1, c2)):
        colour_ref[k] = c.reshape(share, cols)
    transmit_ref[...] = jnp.exp(-front).reshape(share, cols)


def march(density, front, back, left, right, absorb, n):
    depth, rows, cols = density.shape
    share = rows // n
    tiles = (n, share * 4 * cols // 128, 128)
    half_tiles = (n // 2,) + tiles[1:]
    vmem = pltpu.MemorySpace.VMEM
    return pl.pallas_call(
        functools.partial(march_kernel, depth - 1, n),
        out_shape=(
            jax.ShapeDtypeStruct((3, share, cols), jnp.float32),
            jax.ShapeDtypeStruct((share, cols), jnp.float32),
        ),
        in_specs=[pl.BlockSpec(memory_space=vmem)] * 6,
        out_specs=(pl.BlockSpec(memory_space=vmem), pl.BlockSpec(memory_space=vmem)),
        scratch_shapes=[
            pltpu.VMEM((4, rows, cols), jnp.float32),
            pltpu.VMEM(tiles, jnp.float32),
            pltpu.VMEM(half_tiles, jnp.float32),
            pltpu.VMEM(half_tiles, jnp.float32),
            pltpu.VMEM(half_tiles, jnp.float32),
            pltpu.SemaphoreType.DMA,
            pltpu.SemaphoreType.DMA,
            pltpu.SemaphoreType.DMA((n // 2,)),
            pltpu.SemaphoreType.DMA((n // 2,)),
            pltpu.SemaphoreType.DMA,
        ],
        compiler_params=pltpu.CompilerParams(collective_id=0, has_side_effects=True),
    )(density, front, back, left, right, absorb)


def edge_kernel(dens_ref, first_ref, last_ref):
    depth, rows, cols = dens_ref.shape
    for z in range(rows):
        low = jnp.transpose(dens_ref[:, z, 0:128])
        high = jnp.transpose(dens_ref[:, z, cols - 128:cols])
        first_ref[z:z + 1, :] = low[0:1, :]
        last_ref[z:z + 1, :] = high[127:128, :]


def edges(density):
    depth, rows, cols = density.shape
    vmem = pltpu.MemorySpace.VMEM
    plane = jax.ShapeDtypeStruct((rows, depth), jnp.float32)
    return pl.pallas_call(
        edge_kernel,
        out_shape=(plane, plane),
        in_specs=[pl.BlockSpec(memory_space=vmem)],
        out_specs=(pl.BlockSpec(memory_space=vmem), pl.BlockSpec(memory_space=vmem)),
    )(density)


def shifted(value, axis, forward):
    size = lax.axis_size(axis)
    pairs = [(i, i + 1) for i in range(size - 1)]
    if not forward:
        pairs = [(j, i) for i, j in pairs]
    return lax.ppermute(value, axis, pairs)


def local(density, absorb):
    depth, nz, cols = density.shape
    front = shifted(density[depth - 1], "gx", True)
    back = shifted(density[0], "gx", False)
    first_col, last_col = edges(density)
    left = shifted(last_col, "gy", True)
    right = shifted(first_col, "gy", False)
    return march(density, front, back, left, right, absorb, lax.axis_size("gx"))


def solution(mesh):
    placed = (P("gx", None, "gy"), P(None, "gy"))
    return jax.shard_map(
        local,
        mesh=mesh,
        in_specs=placed,
        out_specs=(P(None, "gx", "gy"), P("gx", "gy")),
        check_vma=False,
    )
```

```python
import functools

import jax
import jax.numpy as jnp
from jax import lax
from jax.experimental import pallas as pl
from jax.experimental.pallas import tpu as pltpu
from jax.sharding import PartitionSpec as P

SLOPES = (2.0, -1.5, 0.8)
OFFSETS = (0.0, 0.5, -0.3)
HALF_SLOPES = tuple(0.5 * v for v in SLOPES)
HALF_OFFSETS = tuple(0.5 * v for v in OFFSETS)
LOG2_E = 1.4426950408889634
MESH_ID = pl.DeviceIdType.MESH


def march_kernel(last, n, dens_ref, front_ref, back_ref, left_ref, right_ref, absorb_ref,
                 colour_ref, transmit_ref, out_ref, part, mixed, recv_pair, recv,
                 send_pair, got_pair, send_sems, recv_sems, local_sem):
    rows, cols = dens_ref.shape[1], dens_ref.shape[2]
    shape = (rows, 128)
    lane = lax.broadcasted_iota(jnp.int32, shape, 1)
    row = lax.broadcasted_iota(jnp.int32, shape, 0)
    first_lane, last_lane = lane == 0, lane == 127
    top_row, bottom_row = row == 0, row == rows - 1
    halves = cols // 128
    me = lax.axis_index("gx")
    col = lax.axis_index("gy")
    barrier = pltpu.get_barrier_semaphore()

    pairs = n // 2
    parity = lax.rem(me, 2)
    chip = me // 2
    sems = (send_pair, got_pair, send_sems, recv_sems, local_sem)

    def greet(i, carry):
        peer = 2 * lax.rem(chip + i, pairs) + parity
        pl.semaphore_signal(barrier, inc=1, device_id=(peer, col), device_id_type=MESH_ID)
        return carry

    pl.semaphore_signal(barrier, inc=1, device_id=(me + 1 - 2 * parity, col), device_id_type=MESH_ID)
    lax.fori_loop(1, pairs, greet, 0)
    for h in range(halves):
        lanes = slice(h * 128, (h + 1) * 128)
        left_lanes = slice((h - 1) * 128, h * 128) if h > 0 else None
        right_lanes = slice((h + 1) * 128, (h + 2) * 128) if h + 1 < halves else None
        absorb = absorb_ref[:, lanes]
        fade = absorb * (-LOG2_E)

        def plane(ref_plane):
            return ref_plane[:, lanes]

        def step(x, carry):
            seen, total, t0, t1, t2, softsum = carry
            centre_plane = dens_ref.at[x]
            d = centre_plane[:, lanes]
            behind = jnp.where(x == 0, front_ref[:, lanes], dens_ref[jnp.maximum(x - 1, 0), :, lanes])
            ahead = jnp.where(x == last, back_ref[:, lanes], dens_ref[jnp.minimum(x + 1, last), :, lanes])
            span = left_ref.shape[1]
            halo_left = pltpu.roll(left_ref[...], lax.rem(span - x, span), 1)
            halo_right = pltpu.roll(right_ref[...], lax.rem(span + 127 - x, span), 1)
            from_left = pltpu.roll(d, 1, 1)
            from_right = pltpu.roll(d, 127, 1)
            if left_lanes is None:
                edge_left = halo_left
            else:
                edge_left = pltpu.roll(centre_plane[:, left_lanes], 1, 1)
            if right_lanes is None:
                edge_right = halo_right
            else:
                edge_right = pltpu.roll(centre_plane[:, right_lanes], 127, 1)
            left = jnp.where(first_lane, edge_left, from_left)
            right = jnp.where(last_lane, edge_right, from_right)
            above = jnp.where(top_row, 0.0, pltpu.roll(d, 1, 0))
            below = jnp.where(bottom_row, 0.0, pltpu.roll(d, rows - 1, 0))
            step_depth = ahead - behind
            step_row = below - above
            step_col = right - left
            facing = 0.18 * step_depth + 0.24 * step_row + 0.225 * step_col
            length2 = 0.25 * (step_depth * step_depth + step_row * step_row + step_col * step_col) + 1.0
            lighting = 0.25 + jnp.maximum(facing, 0.0) * lax.rsqrt(length2)
            soft = jnp.log(1.0 + jnp.exp(d))
            passed = jnp.exp2(fade * soft)
            seen_after = seen * passed
            weight = (seen - seen_after) * lighting
            return (
                seen_after,
                total + weight,
                t0 + weight * jnp.tanh(HALF_SLOPES[0] * d + HALF_OFFSETS[0]),
                t1 + weight * jnp.tanh(HALF_SLOPES[1] * d + HALF_OFFSETS[1]),
                t2 + weight * jnp.tanh(HALF_SLOPES[2] * d + HALF_OFFSETS[2]),
                softsum + soft,
            )

        zero = jnp.zeros(shape, jnp.float32)
        one = jnp.ones(shape, jnp.float32)
        _, total, t0, t1, t2, softsum = lax.fori_loop(
            0, last + 1, step, (one, zero, zero, zero, zero, zero), unroll=16
        )
        for k, value in enumerate((t0, t1, t2)):
            out_ref[k, :, lanes] = 0.5 * (total + value)
        out_ref[3, :, lanes] = absorb * softsum

    share = rows // n
    pairs = n // 2
    for z in range(rows):
        owner = z // share
        slot = (owner % 2) * pairs + owner // 2
        for k in range(4):
            for h in range(halves):
                r = ((z % share) * 4 + k) * halves + h
                part[slot, r:r + 1, :] = out_ref[k, z:z + 1, h * 128:(h + 1) * 128]
    exchange_and_combine(n, share, halves, me, col, barrier, part, mixed, recv_pair, recv,
                         sems, colour_ref, transmit_ref)


def merge(front, back, share, halves):
    def rows_of(k):
        return [(r * 4 + k) * halves + h for r in range(share) for h in range(halves)]

    seen = jnp.exp(-jnp.concatenate([front[i:i + 1] for i in rows_of(3)], axis=0))
    pieces = [None] * (share * 4 * halves)
    for k in range(4):
        idx = rows_of(k)
        f = jnp.concatenate([front[i:i + 1] for i in idx], axis=0)
        b = jnp.concatenate([back[i:i + 1] for i in idx], axis=0)
        merged = f + b if k == 3 else f + seen * b
        for j, i in enumerate(idx):
            pieces[i] = merged[j:j + 1]
    return jnp.concatenate(pieces, axis=0)


def exchange_and_combine(n, share, halves, me, col, barrier, part, mixed, recv_pair, recv,
                         sems, colour_ref, transmit_ref):
    pairs = n // 2
    parity = lax.rem(me, 2)
    partner = me + 1 - 2 * parity
    chip = me // 2
    send_pair, got_pair, send_sems, recv_sems, local_sem = sems
    pl.semaphore_wait(barrier, pairs)

    swap = pltpu.make_async_remote_copy(
        src_ref=part.at[pl.ds((1 - parity) * pairs, pairs)],
        dst_ref=recv_pair,
        send_sem=send_pair,
        recv_sem=got_pair,
        device_id=(partner, col),
        device_id_type=MESH_ID,
    )
    swap.start()
    swap.wait()

    def combine_pair(j, carry):
        mine = part[parity * pairs + j]
        theirs = recv_pair[j]
        first = parity == 0
        front = jnp.where(first, mine, theirs)
        back = jnp.where(first, theirs, mine)
        mixed[j] = merge(front, back, share, halves)
        return carry

    lax.fori_loop(0, pairs, combine_pair, 0)

    def link(j, slot):
        return pltpu.make_async_remote_copy(
            src_ref=mixed.at[j],
            dst_ref=recv.at[slot],
            send_sem=send_sems.at[j],
            recv_sem=recv_sems.at[slot],
            device_id=(2 * j + parity, col),
            device_id_type=MESH_ID,
        )

    def send(i, carry):
        link(lax.rem(chip + i, pairs), chip).start()
        return carry

    lax.fori_loop(1, pairs, send, 0)
    own = pltpu.make_async_copy(mixed.at[chip], recv.at[chip], local_sem)
    own.start()
    own.wait()

    def finish(i, carry):
        j = lax.rem(chip + i, pairs)
        link(j, j).wait_send()
        link(j, j).wait_recv()
        return carry

    lax.fori_loop(1, pairs, finish, 0)
    cols = colour_ref.shape[-1]
    zero = jnp.zeros((share * halves, 128), jnp.float32)

    def value(block, k):
        pieces = [block[(r * 4 + k) * halves:(r * 4 + k + 1) * halves] for r in range(share)]
        return pieces[0] if share == 1 else jnp.concatenate(pieces, axis=0)

    def accumulate(d, carry):
        front, c0, c1, c2 = carry
        block = recv[d]
        seen = jnp.exp(-front)
        return (
            front + value(block, 3),
            c0 + value(block, 0) * seen,
            c1 + value(block, 1) * seen,
            c2 + value(block, 2) * seen,
        )

    front, c0, c1, c2 = lax.fori_loop(0, pairs, accumulate, (zero, zero, zero, zero))
    for k, c in enumerate((c0, c1, c2)):
        colour_ref[k] = c.reshape(share, cols)
    transmit_ref[...] = jnp.exp(-front).reshape(share, cols)


def march(density, front, back, left, right, absorb, n):
    depth, rows, cols = density.shape
    share = rows // n
    tiles = (n, share * 4 * cols // 128, 128)
    half_tiles = (n // 2,) + tiles[1:]
    vmem = pltpu.MemorySpace.VMEM
    return pl.pallas_call(
        functools.partial(march_kernel, depth - 1, n),
        out_shape=(
            jax.ShapeDtypeStruct((3, share, cols), jnp.float32),
            jax.ShapeDtypeStruct((share, cols), jnp.float32),
        ),
        in_specs=[pl.BlockSpec(memory_space=vmem)] * 6,
        out_specs=(pl.BlockSpec(memory_space=vmem), pl.BlockSpec(memory_space=vmem)),
        scratch_shapes=[
            pltpu.VMEM((4, rows, cols), jnp.float32),
            pltpu.VMEM(tiles, jnp.float32),
            pltpu.VMEM(half_tiles, jnp.float32),
            pltpu.VMEM(half_tiles, jnp.float32),
            pltpu.VMEM(half_tiles, jnp.float32),
            pltpu.SemaphoreType.DMA,
            pltpu.SemaphoreType.DMA,
            pltpu.SemaphoreType.DMA((n // 2,)),
            pltpu.SemaphoreType.DMA((n // 2,)),
            pltpu.SemaphoreType.DMA,
        ],
        compiler_params=pltpu.CompilerParams(collective_id=0, has_side_effects=True),
    )(density, front, back, left, right, absorb)


def edge_kernel(dens_ref, first_ref, last_ref):
    depth, rows, cols = dens_ref.shape
    for z in range(rows):
        low = jnp.transpose(dens_ref[:, z, 0:128])
        high = jnp.transpose(dens_ref[:, z, cols - 128:cols])
        first_ref[z:z + 1, :] = low[0:1, :]
        last_ref[z:z + 1, :] = high[127:128, :]


def edges(density):
    depth, rows, cols = density.shape
    vmem = pltpu.MemorySpace.VMEM
    plane = jax.ShapeDtypeStruct((rows, depth), jnp.float32)
    return pl.pallas_call(
        edge_kernel,
        out_shape=(plane, plane),
        in_specs=[pl.BlockSpec(memory_space=vmem)],
        out_specs=(pl.BlockSpec(memory_space=vmem), pl.BlockSpec(memory_space=vmem)),
    )(density)


def shifted(value, axis, forward):
    size = lax.axis_size(axis)
    pairs = [(i, i + 1) for i in range(size - 1)]
    if not forward:
        pairs = [(j, i) for i, j in pairs]
    return lax.ppermute(value, axis, pairs)


def local(density, absorb):
    depth, nz, cols = density.shape
    front = shifted(density[depth - 1], "gx", True)
    back = shifted(density[0], "gx", False)
    first_col, last_col = edges(density)
    left = shifted(last_col, "gy", True)
    right = shifted(first_col, "gy", False)
    return march(density, front, back, left, right, absorb, lax.axis_size("gx"))


def solution(mesh):
    placed = (P("gx", None, "gy"), P(None, "gy"))
    return jax.shard_map(
        local,
        mesh=mesh,
        in_specs=placed,
        out_specs=(P(None, "gx", "gy"), P("gx", "gy")),
        check_vma=False,
    )
```

```python
import functools

import jax
import jax.numpy as jnp
from jax import lax
from jax.experimental import pallas as pl
from jax.experimental.pallas import tpu as pltpu
from jax.sharding import PartitionSpec as P

SLOPES = (2.0, -1.5, 0.8)
OFFSETS = (0.0, 0.5, -0.3)
HALF_SLOPES = tuple(0.5 * v for v in SLOPES)
HALF_OFFSETS = tuple(0.5 * v for v in OFFSETS)
LOG2_E = 1.4426950408889634
MESH_ID = pl.DeviceIdType.MESH


def march_kernel(last, n, dens_ref, front_ref, back_ref, left_ref, right_ref, absorb_ref,
                 colour_ref, transmit_ref, out_ref, part, mixed, recv_pair, recv,
                 send_pair, got_pair, send_sems, recv_sems, local_sem):
    rows, cols = dens_ref.shape[1], dens_ref.shape[2]
    shape = (rows, 128)
    lane = lax.broadcasted_iota(jnp.int32, shape, 1)
    row = lax.broadcasted_iota(jnp.int32, shape, 0)
    first_lane, last_lane = lane == 0, lane == 127
    top_row, bottom_row = row == 0, row == rows - 1
    halves = cols // 128
    me = lax.axis_index("gx")
    col = lax.axis_index("gy")
    barrier = pltpu.get_barrier_semaphore()

    pairs = n // 2
    parity = lax.rem(me, 2)
    chip = me // 2
    sems = (send_pair, got_pair, send_sems, recv_sems, local_sem)

    def greet(i, carry):
        peer = 2 * lax.rem(chip + i, pairs) + parity
        pl.semaphore_signal(barrier, inc=1, device_id=(peer, col), device_id_type=MESH_ID)
        return carry

    pl.semaphore_signal(barrier, inc=1, device_id=(me + 1 - 2 * parity, col), device_id_type=MESH_ID)
    lax.fori_loop(1, pairs, greet, 0)
    for h in range(halves):
        lanes = slice(h * 128, (h + 1) * 128)
        left_lanes = slice((h - 1) * 128, h * 128) if h > 0 else None
        right_lanes = slice((h + 1) * 128, (h + 2) * 128) if h + 1 < halves else None
        absorb = absorb_ref[:, lanes]
        fade = absorb * (-LOG2_E)

        def plane(ref_plane):
            return ref_plane[:, lanes]

        def step(x, carry):
            seen, total, t0, t1, t2, softsum = carry
            centre_plane = dens_ref.at[x]
            d = centre_plane[:, lanes]
            behind = jnp.where(x == 0, front_ref[:, lanes], dens_ref[jnp.maximum(x - 1, 0), :, lanes])
            ahead = jnp.where(x == last, back_ref[:, lanes], dens_ref[jnp.minimum(x + 1, last), :, lanes])
            span = left_ref.shape[1]
            halo_left = pltpu.roll(left_ref[...], lax.rem(span - x, span), 1)
            halo_right = pltpu.roll(right_ref[...], lax.rem(span + 127 - x, span), 1)
            from_left = pltpu.roll(d, 1, 1)
            from_right = pltpu.roll(d, 127, 1)
            if left_lanes is None:
                edge_left = halo_left
            else:
                edge_left = pltpu.roll(centre_plane[:, left_lanes], 1, 1)
            if right_lanes is None:
                edge_right = halo_right
            else:
                edge_right = pltpu.roll(centre_plane[:, right_lanes], 127, 1)
            left = jnp.where(first_lane, edge_left, from_left)
            right = jnp.where(last_lane, edge_right, from_right)
            above = jnp.where(top_row, 0.0, pltpu.roll(d, 1, 0))
            below = jnp.where(bottom_row, 0.0, pltpu.roll(d, rows - 1, 0))
            step_depth = ahead - behind
            step_row = below - above
            step_col = right - left
            facing = 0.18 * step_depth + 0.24 * step_row + 0.225 * step_col
            length2 = 0.25 * (step_depth * step_depth + step_row * step_row + step_col * step_col) + 1.0
            lighting = 0.25 + jnp.maximum(facing, 0.0) * lax.rsqrt(length2)
            soft = jnp.log(1.0 + jnp.exp(d))
            passed = jnp.exp2(fade * soft)
            seen_after = seen * passed
            weight = (seen - seen_after) * lighting
            return (
                seen_after,
                total + weight,
                t0 + weight * jnp.tanh(HALF_SLOPES[0] * d + HALF_OFFSETS[0]),
                t1 + weight * jnp.tanh(HALF_SLOPES[1] * d + HALF_OFFSETS[1]),
                t2 + weight * jnp.tanh(HALF_SLOPES[2] * d + HALF_OFFSETS[2]),
                softsum + soft,
            )

        zero = jnp.zeros(shape, jnp.float32)
        one = jnp.ones(shape, jnp.float32)
        _, total, t0, t1, t2, softsum = lax.fori_loop(
            0, last + 1, step, (one, zero, zero, zero, zero, zero), unroll=16
        )
        for k, value in enumerate((t0, t1, t2)):
            out_ref[k, :, lanes] = 0.5 * (total + value)
        out_ref[3, :, lanes] = absorb * softsum

    share = rows // n
    pairs = n // 2
    for z in range(rows):
        owner = z // share
        slot = (owner % 2) * pairs + owner // 2
        for k in range(4):
            for h in range(halves):
                r = ((z % share) * 4 + k) * halves + h
                part[slot, r:r + 1, :] = out_ref[k, z:z + 1, h * 128:(h + 1) * 128]
    exchange_and_combine(n, share, halves, me, col, barrier, part, mixed, recv_pair, recv,
                         sems, colour_ref, transmit_ref)


def merge(front, back, share, halves):
    def rows_of(k):
        return [(r * 4 + k) * halves + h for r in range(share) for h in range(halves)]

    seen = jnp.exp(-jnp.concatenate([front[i:i + 1] for i in rows_of(3)], axis=0))
    pieces = [None] * (share * 4 * halves)
    for k in range(4):
        idx = rows_of(k)
        f = jnp.concatenate([front[i:i + 1] for i in idx], axis=0)
        b = jnp.concatenate([back[i:i + 1] for i in idx], axis=0)
        merged = f + b if k == 3 else f + seen * b
        for j, i in enumerate(idx):
            pieces[i] = merged[j:j + 1]
    return jnp.concatenate(pieces, axis=0)


def exchange_and_combine(n, share, halves, me, col, barrier, part, mixed, recv_pair, recv,
                         sems, colour_ref, transmit_ref):
    pairs = n // 2
    parity = lax.rem(me, 2)
    partner = me + 1 - 2 * parity
    chip = me // 2
    send_pair, got_pair, send_sems, recv_sems, local_sem = sems
    pl.semaphore_wait(barrier, pairs)

    swap = pltpu.make_async_remote_copy(
        src_ref=part.at[pl.ds((1 - parity) * pairs, pairs)],
        dst_ref=recv_pair,
        send_sem=send_pair,
        recv_sem=got_pair,
        device_id=(partner, col),
        device_id_type=MESH_ID,
    )
    swap.start()
    swap.wait()

    def combine_pair(j, carry):
        mine = part[parity * pairs + j]
        theirs = recv_pair[j]
        first = parity == 0
        front = jnp.where(first, mine, theirs)
        back = jnp.where(first, theirs, mine)
        mixed[j] = merge(front, back, share, halves)
        return carry

    lax.fori_loop(0, pairs, combine_pair, 0)

    def link(j, slot):
        return pltpu.make_async_remote_copy(
            src_ref=mixed.at[j],
            dst_ref=recv.at[slot],
            send_sem=send_sems.at[j],
            recv_sem=recv_sems.at[slot],
            device_id=(2 * j + parity, col),
            device_id_type=MESH_ID,
        )

    def send(i, carry):
        link(lax.rem(chip + i, pairs), chip).start()
        return carry

    lax.fori_loop(1, pairs, send, 0)
    own = pltpu.make_async_copy(mixed.at[chip], recv.at[chip], local_sem)
    own.start()
    own.wait()

    def finish(i, carry):
        j = lax.rem(chip + i, pairs)
        link(j, j).wait_send()
        link(j, j).wait_recv()
        return carry

    lax.fori_loop(1, pairs, finish, 0)
    cols = colour_ref.shape[-1]
    zero = jnp.zeros((share * halves, 128), jnp.float32)

    def value(block, k):
        pieces = [block[(r * 4 + k) * halves:(r * 4 + k + 1) * halves] for r in range(share)]
        return pieces[0] if share == 1 else jnp.concatenate(pieces, axis=0)

    def accumulate(d, carry):
        front, c0, c1, c2 = carry
        block = recv[d]
        seen = jnp.exp(-front)
        return (
            front + value(block, 3),
            c0 + value(block, 0) * seen,
            c1 + value(block, 1) * seen,
            c2 + value(block, 2) * seen,
        )

    front, c0, c1, c2 = lax.fori_loop(0, pairs, accumulate, (zero, zero, zero, zero))
    for k, c in enumerate((c0, c1, c2)):
        colour_ref[k] = c.reshape(share, cols)
    transmit_ref[...] = jnp.exp(-front).reshape(share, cols)


def march(density, front, back, left, right, absorb, n):
    depth, rows, cols = density.shape
    share = rows // n
    tiles = (n, share * 4 * cols // 128, 128)
    half_tiles = (n // 2,) + tiles[1:]
    vmem = pltpu.MemorySpace.VMEM
    return pl.pallas_call(
        functools.partial(march_kernel, depth - 1, n),
        out_shape=(
            jax.ShapeDtypeStruct((3, share, cols), jnp.float32),
            jax.ShapeDtypeStruct((share, cols), jnp.float32),
        ),
        in_specs=[pl.BlockSpec(memory_space=vmem)] * 6,
        out_specs=(pl.BlockSpec(memory_space=vmem), pl.BlockSpec(memory_space=vmem)),
        scratch_shapes=[
            pltpu.VMEM((4, rows, cols), jnp.float32),
            pltpu.VMEM(tiles, jnp.float32),
            pltpu.VMEM(half_tiles, jnp.float32),
            pltpu.VMEM(half_tiles, jnp.float32),
            pltpu.VMEM(half_tiles, jnp.float32),
            pltpu.SemaphoreType.DMA,
            pltpu.SemaphoreType.DMA,
            pltpu.SemaphoreType.DMA((n // 2,)),
            pltpu.SemaphoreType.DMA((n // 2,)),
            pltpu.SemaphoreType.DMA,
        ],
        compiler_params=pltpu.CompilerParams(collective_id=0, has_side_effects=True),
    )(density, front, back, left, right, absorb)


def halo_kernel(dens_ref, front_ref, back_ref, left_ref, right_ref,
                first_col, last_col, lands, send_sems, recv_sems):
    depth, rows, cols = dens_ref.shape
    nx, ny = lax.axis_size("gx"), lax.axis_size("gy")
    gx, gy = lax.axis_index("gx"), lax.axis_index("gy")
    ahead_x, behind_x = lax.rem(gx + 1, nx), lax.rem(gx + nx - 1, nx)
    ahead_y, behind_y = lax.rem(gy + 1, ny), lax.rem(gy + ny - 1, ny)
    barrier = pltpu.get_barrier_semaphore()
    for peer in ((ahead_x, gy), (behind_x, gy), (gx, ahead_y), (gx, behind_y)):
        pl.semaphore_signal(barrier, inc=1, device_id=peer, device_id_type=MESH_ID)
    for z in range(rows):
        low = jnp.transpose(dens_ref[:, z, 0:128])
        high = jnp.transpose(dens_ref[:, z, cols - 128:cols])
        first_col[z:z + 1, :] = low[0:1, :]
        last_col[z:z + 1, :] = high[127:128, :]
    pl.semaphore_wait(barrier, 4)
    front_land, back_land, left_land, right_land = lands
    copies = [
        (dens_ref.at[depth - 1], front_land, (ahead_x, gy)),
        (dens_ref.at[0], back_land, (behind_x, gy)),
        (last_col, left_land, (gx, ahead_y)),
        (first_col, right_land, (gx, behind_y)),
    ]
    started = []
    for i, (src, dst, peer) in enumerate(copies):
        copy = pltpu.make_async_remote_copy(
            src_ref=src, dst_ref=dst, send_sem=send_sems.at[i], recv_sem=recv_sems.at[i],
            device_id=peer, device_id_type=MESH_ID,
        )
        copy.start()
        started.append(copy)
    for copy in started:
        copy.wait()
    front_ref[...] = jnp.where(gx == 0, 0.0, front_land[...])
    back_ref[...] = jnp.where(gx == nx - 1, 0.0, back_land[...])
    left_ref[...] = jnp.where(gy == 0, 0.0, left_land[...])
    right_ref[...] = jnp.where(gy == ny - 1, 0.0, right_land[...])


def halos(density):
    depth, rows, cols = density.shape
    vmem = pltpu.MemorySpace.VMEM
    plane = jax.ShapeDtypeStruct((rows, cols), jnp.float32)
    column = jax.ShapeDtypeStruct((rows, depth), jnp.float32)
    return pl.pallas_call(
        halo_kernel,
        out_shape=(plane, plane, column, column),
        in_specs=[pl.BlockSpec(memory_space=vmem)],
        out_specs=tuple(pl.BlockSpec(memory_space=vmem) for _ in range(4)),
        scratch_shapes=[
            pltpu.VMEM((rows, depth), jnp.float32),
            pltpu.VMEM((rows, depth), jnp.float32),
            (
                pltpu.VMEM((rows, cols), jnp.float32),
                pltpu.VMEM((rows, cols), jnp.float32),
                pltpu.VMEM((rows, depth), jnp.float32),
                pltpu.VMEM((rows, depth), jnp.float32),
            ),
            pltpu.SemaphoreType.DMA((4,)),
            pltpu.SemaphoreType.DMA((4,)),
        ],
        compiler_params=pltpu.CompilerParams(collective_id=1, has_side_effects=True),
    )(density)


def local(density, absorb):
    front, back, left, right = halos(density)
    return march(density, front, back, left, right, absorb, lax.axis_size("gx"))


def solution(mesh):
    placed = (P("gx", None, "gy"), P(None, "gy"))
    return jax.shard_map(
        local,
        mesh=mesh,
        in_specs=placed,
        out_specs=(P(None, "gx", "gy"), P("gx", "gy")),
        check_vma=False,
    )
```

```python
import functools

import jax
import jax.numpy as jnp
from jax import lax
from jax.experimental import pallas as pl
from jax.experimental.pallas import tpu as pltpu
from jax.sharding import PartitionSpec as P

SLOPES = (2.0, -1.5, 0.8)
OFFSETS = (0.0, 0.5, -0.3)
HALF_SLOPES = tuple(0.5 * v for v in SLOPES)
HALF_OFFSETS = tuple(0.5 * v for v in OFFSETS)
LOG2_E = 1.4426950408889634
MESH_ID = pl.DeviceIdType.MESH


def march_kernel(last, n, dens_ref, front_ref, back_ref, left_ref, right_ref, absorb_ref,
                 colour_ref, out_ref, part, mixed, recv_pair, recv,
                 send_pair, got_pair, send_sems, recv_sems, local_sem):
    rows, cols = dens_ref.shape[1], dens_ref.shape[2]
    shape = (rows, 128)
    lane = lax.broadcasted_iota(jnp.int32, shape, 1)
    row = lax.broadcasted_iota(jnp.int32, shape, 0)
    first_lane, last_lane = lane == 0, lane == 127
    top_row, bottom_row = row == 0, row == rows - 1
    halves = cols // 128
    me = lax.axis_index("gx")
    col = lax.axis_index("gy")
    barrier = pltpu.get_barrier_semaphore()

    pairs = n // 2
    parity = lax.rem(me, 2)
    chip = me // 2
    sems = (send_pair, got_pair, send_sems, recv_sems, local_sem)

    def greet(i, carry):
        peer = 2 * lax.rem(chip + i, pairs) + parity
        pl.semaphore_signal(barrier, inc=1, device_id=(peer, col), device_id_type=MESH_ID)
        return carry

    pl.semaphore_signal(barrier, inc=1, device_id=(me + 1 - 2 * parity, col), device_id_type=MESH_ID)
    lax.fori_loop(1, pairs, greet, 0)
    for h in range(halves):
        lanes = slice(h * 128, (h + 1) * 128)
        left_lanes = slice((h - 1) * 128, h * 128) if h > 0 else None
        right_lanes = slice((h + 1) * 128, (h + 2) * 128) if h + 1 < halves else None
        absorb = absorb_ref[:, lanes]
        fade = absorb * (-LOG2_E)

        def plane(ref_plane):
            return ref_plane[:, lanes]

        def step(x, carry):
            seen, total, t0, t1, t2, softsum = carry
            centre_plane = dens_ref.at[x]
            d = centre_plane[:, lanes]
            behind = jnp.where(x == 0, front_ref[:, lanes], dens_ref[jnp.maximum(x - 1, 0), :, lanes])
            ahead = jnp.where(x == last, back_ref[:, lanes], dens_ref[jnp.minimum(x + 1, last), :, lanes])
            span = left_ref.shape[1]
            halo_left = pltpu.roll(left_ref[...], lax.rem(span - x, span), 1)
            halo_right = pltpu.roll(right_ref[...], lax.rem(span + 127 - x, span), 1)
            from_left = pltpu.roll(d, 1, 1)
            from_right = pltpu.roll(d, 127, 1)
            if left_lanes is None:
                edge_left = halo_left
            else:
                edge_left = pltpu.roll(centre_plane[:, left_lanes], 1, 1)
            if right_lanes is None:
                edge_right = halo_right
            else:
                edge_right = pltpu.roll(centre_plane[:, right_lanes], 127, 1)
            left = jnp.where(first_lane, edge_left, from_left)
            right = jnp.where(last_lane, edge_right, from_right)
            above = jnp.where(top_row, 0.0, pltpu.roll(d, 1, 0))
            below = jnp.where(bottom_row, 0.0, pltpu.roll(d, rows - 1, 0))
            step_depth = ahead - behind
            step_row = below - above
            step_col = right - left
            facing = 0.18 * step_depth + 0.24 * step_row + 0.225 * step_col
            length2 = 0.25 * (step_depth * step_depth + step_row * step_row + step_col * step_col) + 1.0
            lighting = 0.25 + jnp.maximum(facing, 0.0) * lax.rsqrt(length2)
            soft = jnp.log(1.0 + jnp.exp(d))
            passed = jnp.exp2(fade * soft)
            seen_after = seen * passed
            weight = (seen - seen_after) * lighting
            return (
                seen_after,
                total + weight,
                t0 + weight * jnp.tanh(HALF_SLOPES[0] * d + HALF_OFFSETS[0]),
                t1 + weight * jnp.tanh(HALF_SLOPES[1] * d + HALF_OFFSETS[1]),
                t2 + weight * jnp.tanh(HALF_SLOPES[2] * d + HALF_OFFSETS[2]),
                softsum + soft,
            )

        zero = jnp.zeros(shape, jnp.float32)
        one = jnp.ones(shape, jnp.float32)
        _, total, t0, t1, t2, softsum = lax.fori_loop(
            0, last + 1, step, (one, zero, zero, zero, zero, zero), unroll=16
        )
        for k, value in enumerate((t0, t1, t2)):
            out_ref[k, :, lanes] = 0.5 * (total + value)
        out_ref[3, :, lanes] = absorb * softsum

    share = rows // n
    pairs = n // 2
    for z in range(rows):
        owner = z // share
        slot = (owner % 2) * pairs + owner // 2
        for k in range(4):
            for h in range(halves):
                r = ((z % share) * 4 + k) * halves + h
                part[slot, r:r + 1, :] = out_ref[k, z:z + 1, h * 128:(h + 1) * 128]
    exchange_and_combine(n, share, halves, me, col, barrier, part, mixed, recv_pair, recv,
                         sems, colour_ref)


def merge(front, back, share, halves):
    def rows_of(k):
        return [(r * 4 + k) * halves + h for r in range(share) for h in range(halves)]

    seen = jnp.exp(-jnp.concatenate([front[i:i + 1] for i in rows_of(3)], axis=0))
    pieces = [None] * (share * 4 * halves)
    for k in range(4):
        idx = rows_of(k)
        f = jnp.concatenate([front[i:i + 1] for i in idx], axis=0)
        b = jnp.concatenate([back[i:i + 1] for i in idx], axis=0)
        merged = f + b if k == 3 else f + seen * b
        for j, i in enumerate(idx):
            pieces[i] = merged[j:j + 1]
    return jnp.concatenate(pieces, axis=0)


def exchange_and_combine(n, share, halves, me, col, barrier, part, mixed, recv_pair, recv,
                         sems, colour_ref):
    pairs = n // 2
    parity = lax.rem(me, 2)
    partner = me + 1 - 2 * parity
    chip = me // 2
    send_pair, got_pair, send_sems, recv_sems, local_sem = sems
    pl.semaphore_wait(barrier, pairs)

    swap = pltpu.make_async_remote_copy(
        src_ref=part.at[pl.ds((1 - parity) * pairs, pairs)],
        dst_ref=recv_pair,
        send_sem=send_pair,
        recv_sem=got_pair,
        device_id=(partner, col),
        device_id_type=MESH_ID,
    )
    swap.start()
    swap.wait()

    def combine_pair(j, carry):
        mine = part[parity * pairs + j]
        theirs = recv_pair[j]
        first = parity == 0
        front = jnp.where(first, mine, theirs)
        back = jnp.where(first, theirs, mine)
        mixed[j] = merge(front, back, share, halves)
        return carry

    lax.fori_loop(0, pairs, combine_pair, 0)

    def link(j, slot):
        return pltpu.make_async_remote_copy(
            src_ref=mixed.at[j],
            dst_ref=recv.at[slot],
            send_sem=send_sems.at[j],
            recv_sem=recv_sems.at[slot],
            device_id=(2 * j + parity, col),
            device_id_type=MESH_ID,
        )

    def send(i, carry):
        link(lax.rem(chip + i, pairs), chip).start()
        return carry

    lax.fori_loop(1, pairs, send, 0)
    own = pltpu.make_async_copy(mixed.at[chip], recv.at[chip], local_sem)
    own.start()
    own.wait()

    def finish(i, carry):
        j = lax.rem(chip + i, pairs)
        link(j, j).wait_send()
        link(j, j).wait_recv()
        return carry

    lax.fori_loop(1, pairs, finish, 0)
    colour_ref[...] = recv[...]


def finish_kernel(share, halves, recv_ref, colour_ref, transmit_ref):
    pairs = recv_ref.shape[0]
    cols = colour_ref.shape[-1]
    zero = jnp.zeros((share * halves, 128), jnp.float32)

    def value(block, k):
        pieces = [block[(r * 4 + k) * halves:(r * 4 + k + 1) * halves] for r in range(share)]
        return pieces[0] if share == 1 else jnp.concatenate(pieces, axis=0)

    def accumulate(d, carry):
        front, c0, c1, c2 = carry
        block = recv_ref[d]
        seen = jnp.exp(-front)
        return (
            front + value(block, 3),
            c0 + value(block, 0) * seen,
            c1 + value(block, 1) * seen,
            c2 + value(block, 2) * seen,
        )

    front, c0, c1, c2 = lax.fori_loop(0, pairs, accumulate, (zero, zero, zero, zero))
    for k, c in enumerate((c0, c1, c2)):
        colour_ref[k] = c.reshape(share, cols)
    transmit_ref[...] = jnp.exp(-front).reshape(share, cols)


def finish(gathered, share, cols):
    vmem = pltpu.MemorySpace.VMEM
    return pl.pallas_call(
        functools.partial(finish_kernel, share, cols // 128),
        out_shape=(
            jax.ShapeDtypeStruct((3, share, cols), jnp.float32),
            jax.ShapeDtypeStruct((share, cols), jnp.float32),
        ),
        in_specs=[pl.BlockSpec(memory_space=vmem)],
        out_specs=(pl.BlockSpec(memory_space=vmem), pl.BlockSpec(memory_space=vmem)),
    )(gathered)


def march(density, front, back, left, right, absorb, n):
    depth, rows, cols = density.shape
    share = rows // n
    tiles = (n, share * 4 * cols // 128, 128)
    half_tiles = (n // 2,) + tiles[1:]
    vmem = pltpu.MemorySpace.VMEM
    return pl.pallas_call(
        functools.partial(march_kernel, depth - 1, n),
        out_shape=jax.ShapeDtypeStruct(half_tiles, jnp.float32),
        in_specs=[pl.BlockSpec(memory_space=vmem)] * 6,
        out_specs=pl.BlockSpec(memory_space=vmem),
        scratch_shapes=[
            pltpu.VMEM((4, rows, cols), jnp.float32),
            pltpu.VMEM(tiles, jnp.float32),
            pltpu.VMEM(half_tiles, jnp.float32),
            pltpu.VMEM(half_tiles, jnp.float32),
            pltpu.VMEM(half_tiles, jnp.float32),
            pltpu.SemaphoreType.DMA,
            pltpu.SemaphoreType.DMA,
            pltpu.SemaphoreType.DMA((n // 2,)),
            pltpu.SemaphoreType.DMA((n // 2,)),
            pltpu.SemaphoreType.DMA,
        ],
        compiler_params=pltpu.CompilerParams(collective_id=0, has_side_effects=True),
    )(density, front, back, left, right, absorb)


def halo_kernel(dens_ref, front_ref, back_ref, left_ref, right_ref,
                first_col, last_col, lands, send_sems, recv_sems):
    depth, rows, cols = dens_ref.shape
    nx, ny = lax.axis_size("gx"), lax.axis_size("gy")
    gx, gy = lax.axis_index("gx"), lax.axis_index("gy")
    ahead_x, behind_x = lax.rem(gx + 1, nx), lax.rem(gx + nx - 1, nx)
    ahead_y, behind_y = lax.rem(gy + 1, ny), lax.rem(gy + ny - 1, ny)
    barrier = pltpu.get_barrier_semaphore()
    for peer in ((ahead_x, gy), (behind_x, gy), (gx, ahead_y), (gx, behind_y)):
        pl.semaphore_signal(barrier, inc=1, device_id=peer, device_id_type=MESH_ID)
    for z in range(rows):
        low = jnp.transpose(dens_ref[:, z, 0:128])
        high = jnp.transpose(dens_ref[:, z, cols - 128:cols])
        first_col[z:z + 1, :] = low[0:1, :]
        last_col[z:z + 1, :] = high[127:128, :]
    pl.semaphore_wait(barrier, 4)
    front_land, back_land, left_land, right_land = lands
    copies = [
        (dens_ref.at[depth - 1], front_land, (ahead_x, gy)),
        (dens_ref.at[0], back_land, (behind_x, gy)),
        (last_col, left_land, (gx, ahead_y)),
        (first_col, right_land, (gx, behind_y)),
    ]
    started = []
    for i, (src, dst, peer) in enumerate(copies):
        copy = pltpu.make_async_remote_copy(
            src_ref=src, dst_ref=dst, send_sem=send_sems.at[i], recv_sem=recv_sems.at[i],
            device_id=peer, device_id_type=MESH_ID,
        )
        copy.start()
        started.append(copy)
    for copy in started:
        copy.wait()
    front_ref[...] = jnp.where(gx == 0, 0.0, front_land[...])
    back_ref[...] = jnp.where(gx == nx - 1, 0.0, back_land[...])
    left_ref[...] = jnp.where(gy == 0, 0.0, left_land[...])
    right_ref[...] = jnp.where(gy == ny - 1, 0.0, right_land[...])


def halos(density):
    depth, rows, cols = density.shape
    vmem = pltpu.MemorySpace.VMEM
    plane = jax.ShapeDtypeStruct((rows, cols), jnp.float32)
    column = jax.ShapeDtypeStruct((rows, depth), jnp.float32)
    return pl.pallas_call(
        halo_kernel,
        out_shape=(plane, plane, column, column),
        in_specs=[pl.BlockSpec(memory_space=vmem)],
        out_specs=tuple(pl.BlockSpec(memory_space=vmem) for _ in range(4)),
        scratch_shapes=[
            pltpu.VMEM((rows, depth), jnp.float32),
            pltpu.VMEM((rows, depth), jnp.float32),
            (
                pltpu.VMEM((rows, cols), jnp.float32),
                pltpu.VMEM((rows, cols), jnp.float32),
                pltpu.VMEM((rows, depth), jnp.float32),
                pltpu.VMEM((rows, depth), jnp.float32),
            ),
            pltpu.SemaphoreType.DMA((4,)),
            pltpu.SemaphoreType.DMA((4,)),
        ],
        compiler_params=pltpu.CompilerParams(collective_id=1, has_side_effects=True),
    )(density)


def local(density, absorb):
    front, back, left, right = halos(density)
    n = lax.axis_size("gx")
    gathered = march(density, front, back, left, right, absorb, n)
    return finish(gathered, density.shape[1] // n, density.shape[2])


def solution(mesh):
    placed = (P("gx", None, "gy"), P(None, "gy"))
    return jax.shard_map(
        local,
        mesh=mesh,
        in_specs=placed,
        out_specs=(P(None, "gx", "gy"), P("gx", "gy")),
        check_vma=False,
    )
```

```python
import functools

import jax
import jax.numpy as jnp
from jax import lax
from jax.experimental import pallas as pl
from jax.experimental.pallas import tpu as pltpu
from jax.sharding import PartitionSpec as P

SLOPES = (2.0, -1.5, 0.8)
OFFSETS = (0.0, 0.5, -0.3)
HALF_SLOPES = tuple(0.5 * v for v in SLOPES)
HALF_OFFSETS = tuple(0.5 * v for v in OFFSETS)
LOG2_E = 1.4426950408889634
MESH_ID = pl.DeviceIdType.MESH


def march_kernel(last, n, dens_ref, front_ref, back_ref, left_ref, right_ref, absorb_ref,
                 colour_ref, out_ref, part, mixed, recv_pair, recv,
                 send_pair, got_pair, send_sems, recv_sems, local_sem):
    rows, cols = dens_ref.shape[1], dens_ref.shape[2]
    shape = (rows, 128)
    lane = lax.broadcasted_iota(jnp.int32, shape, 1)
    row = lax.broadcasted_iota(jnp.int32, shape, 0)
    first_lane, last_lane = lane == 0, lane == 127
    top_row, bottom_row = row == 0, row == rows - 1
    halves = cols // 128
    me = lax.axis_index("gx")
    col = lax.axis_index("gy")
    barrier = pltpu.get_barrier_semaphore()

    pairs = n // 2
    parity = lax.rem(me, 2)
    chip = me // 2
    sems = (send_pair, got_pair, send_sems, recv_sems, local_sem)

    def greet(i, carry):
        peer = 2 * lax.rem(chip + i, pairs) + parity
        pl.semaphore_signal(barrier, inc=1, device_id=(peer, col), device_id_type=MESH_ID)
        return carry

    pl.semaphore_signal(barrier, inc=1, device_id=(me + 1 - 2 * parity, col), device_id_type=MESH_ID)
    lax.fori_loop(1, pairs, greet, 0)
    for h in range(halves):
        lanes = slice(h * 128, (h + 1) * 128)
        left_lanes = slice((h - 1) * 128, h * 128) if h > 0 else None
        right_lanes = slice((h + 1) * 128, (h + 2) * 128) if h + 1 < halves else None
        absorb = absorb_ref[:, lanes]
        fade = absorb * (-LOG2_E)

        def plane(ref_plane):
            return ref_plane[:, lanes]

        def step(x, carry):
            seen, total, t0, t1, t2, softsum = carry
            centre_plane = dens_ref.at[x]
            d = centre_plane[:, lanes]
            behind = jnp.where(x == 0, front_ref[:, lanes], dens_ref[jnp.maximum(x - 1, 0), :, lanes])
            ahead = jnp.where(x == last, back_ref[:, lanes], dens_ref[jnp.minimum(x + 1, last), :, lanes])
            span = left_ref.shape[1]
            halo_left = pltpu.roll(left_ref[...], lax.rem(span - x, span), 1)
            halo_right = pltpu.roll(right_ref[...], lax.rem(span + 127 - x, span), 1)
            from_left = pltpu.roll(d, 1, 1)
            from_right = pltpu.roll(d, 127, 1)
            if left_lanes is None:
                edge_left = halo_left
            else:
                edge_left = pltpu.roll(centre_plane[:, left_lanes], 1, 1)
            if right_lanes is None:
                edge_right = halo_right
            else:
                edge_right = pltpu.roll(centre_plane[:, right_lanes], 127, 1)
            left = jnp.where(first_lane, edge_left, from_left)
            right = jnp.where(last_lane, edge_right, from_right)
            above = jnp.where(top_row, 0.0, pltpu.roll(d, 1, 0))
            below = jnp.where(bottom_row, 0.0, pltpu.roll(d, rows - 1, 0))
            step_depth = ahead - behind
            step_row = below - above
            step_col = right - left
            facing = 0.18 * step_depth + 0.24 * step_row + 0.225 * step_col
            length2 = 0.25 * (step_depth * step_depth + step_row * step_row + step_col * step_col) + 1.0
            lighting = 0.25 + jnp.maximum(facing, 0.0) * lax.rsqrt(length2)
            soft = jnp.log(1.0 + jnp.exp(d))
            passed = jnp.exp2(fade * soft)
            seen_after = seen * passed
            weight = (seen - seen_after) * lighting
            return (
                seen_after,
                total + weight,
                t0 + weight * jnp.tanh(HALF_SLOPES[0] * d + HALF_OFFSETS[0]),
                t1 + weight * jnp.tanh(HALF_SLOPES[1] * d + HALF_OFFSETS[1]),
                t2 + weight * jnp.tanh(HALF_SLOPES[2] * d + HALF_OFFSETS[2]),
                softsum + soft,
            )

        zero = jnp.zeros(shape, jnp.float32)
        one = jnp.ones(shape, jnp.float32)
        _, total, t0, t1, t2, softsum = lax.fori_loop(
            0, last + 1, step, (one, zero, zero, zero, zero, zero), unroll=16
        )
        for k, value in enumerate((t0, t1, t2)):
            out_ref[k, :, lanes] = 0.5 * (total + value)
        out_ref[3, :, lanes] = absorb * softsum

    share = rows // n
    pairs = n // 2
    for z in range(rows):
        owner = z // share
        slot = (owner % 2) * pairs + owner // 2
        for k in range(4):
            for h in range(halves):
                r = ((z % share) * 4 + k) * halves + h
                part[slot, r:r + 1, :] = out_ref[k, z:z + 1, h * 128:(h + 1) * 128]
    exchange_and_combine(n, share, halves, me, col, barrier, part, mixed, recv_pair, recv,
                         sems, colour_ref)


def merge(front, back, share, halves):
    def rows_of(k):
        return [(r * 4 + k) * halves + h for r in range(share) for h in range(halves)]

    seen = jnp.exp(-jnp.concatenate([front[i:i + 1] for i in rows_of(3)], axis=0))
    pieces = [None] * (share * 4 * halves)
    for k in range(4):
        idx = rows_of(k)
        f = jnp.concatenate([front[i:i + 1] for i in idx], axis=0)
        b = jnp.concatenate([back[i:i + 1] for i in idx], axis=0)
        merged = f + b if k == 3 else f + seen * b
        for j, i in enumerate(idx):
            pieces[i] = merged[j:j + 1]
    return jnp.concatenate(pieces, axis=0)


def exchange_and_combine(n, share, halves, me, col, barrier, part, mixed, recv_pair, recv,
                         sems, colour_ref):
    pairs = n // 2
    parity = lax.rem(me, 2)
    partner = me + 1 - 2 * parity
    chip = me // 2
    send_pair, got_pair, send_sems, recv_sems, local_sem = sems
    pl.semaphore_wait(barrier, pairs)

    swap = pltpu.make_async_remote_copy(
        src_ref=part.at[pl.ds((1 - parity) * pairs, pairs)],
        dst_ref=recv_pair,
        send_sem=send_pair,
        recv_sem=got_pair,
        device_id=(partner, col),
        device_id_type=MESH_ID,
    )
    swap.start()
    swap.wait()

    def combine_pair(j, carry):
        mine = part[parity * pairs + j]
        theirs = recv_pair[j]
        first = parity == 0
        front = jnp.where(first, mine, theirs)
        back = jnp.where(first, theirs, mine)
        mixed[j] = merge(front, back, share, halves)
        return carry

    lax.fori_loop(0, pairs, combine_pair, 0)

    def link(j, slot):
        return pltpu.make_async_remote_copy(
            src_ref=mixed.at[j],
            dst_ref=recv.at[slot],
            send_sem=send_sems.at[j],
            recv_sem=recv_sems.at[slot],
            device_id=(2 * j + parity, col),
            device_id_type=MESH_ID,
        )

    def send(i, carry):
        link(lax.rem(chip + i, pairs), chip).start()
        return carry

    lax.fori_loop(1, pairs, send, 0)
    own = pltpu.make_async_copy(mixed.at[chip], recv.at[chip], local_sem)
    own.start()
    own.wait()

    def finish(i, carry):
        j = lax.rem(chip + i, pairs)
        link(j, j).wait_send()
        link(j, j).wait_recv()
        return carry

    lax.fori_loop(1, pairs, finish, 0)
    colour_ref[...] = recv[...]


def finish_kernel(share, halves, recv_ref, colour_ref, transmit_ref):
    pairs = recv_ref.shape[0]
    cols = colour_ref.shape[-1]
    zero = jnp.zeros((share * halves, 128), jnp.float32)

    def value(block, k):
        pieces = [block[(r * 4 + k) * halves:(r * 4 + k + 1) * halves] for r in range(share)]
        return pieces[0] if share == 1 else jnp.concatenate(pieces, axis=0)

    def accumulate(d, carry):
        front, c0, c1, c2 = carry
        block = recv_ref[d]
        seen = jnp.exp(-front)
        return (
            front + value(block, 3),
            c0 + value(block, 0) * seen,
            c1 + value(block, 1) * seen,
            c2 + value(block, 2) * seen,
        )

    front, c0, c1, c2 = lax.fori_loop(0, pairs, accumulate, (zero, zero, zero, zero))
    for k, c in enumerate((c0, c1, c2)):
        colour_ref[k] = c.reshape(share, cols)
    transmit_ref[...] = jnp.exp(-front).reshape(share, cols)


def finish(gathered, share, cols):
    vmem = pltpu.MemorySpace.VMEM
    return pl.pallas_call(
        functools.partial(finish_kernel, share, cols // 128),
        out_shape=(
            jax.ShapeDtypeStruct((3, share, cols), jnp.float32),
            jax.ShapeDtypeStruct((share, cols), jnp.float32),
        ),
        in_specs=[pl.BlockSpec(memory_space=vmem)],
        out_specs=(pl.BlockSpec(memory_space=vmem), pl.BlockSpec(memory_space=vmem)),
    )(gathered)


def march(density, front, back, left, right, absorb, n):
    depth, rows, cols = density.shape
    share = rows // n
    tiles = (n, share * 4 * cols // 128, 128)
    half_tiles = (n // 2,) + tiles[1:]
    vmem = pltpu.MemorySpace.VMEM
    return pl.pallas_call(
        functools.partial(march_kernel, depth - 1, n),
        out_shape=jax.ShapeDtypeStruct(half_tiles, jnp.float32),
        in_specs=[pl.BlockSpec(memory_space=vmem)] * 6,
        out_specs=pl.BlockSpec(memory_space=vmem),
        scratch_shapes=[
            pltpu.VMEM((4, rows, cols), jnp.float32),
            pltpu.VMEM(tiles, jnp.float32),
            pltpu.VMEM(half_tiles, jnp.float32),
            pltpu.VMEM(half_tiles, jnp.float32),
            pltpu.VMEM(half_tiles, jnp.float32),
            pltpu.SemaphoreType.DMA,
            pltpu.SemaphoreType.DMA,
            pltpu.SemaphoreType.DMA((n // 2,)),
            pltpu.SemaphoreType.DMA((n // 2,)),
            pltpu.SemaphoreType.DMA,
        ],
        compiler_params=pltpu.CompilerParams(collective_id=0, has_side_effects=True),
    )(density, front, back, left, right, absorb)


def halo_kernel(dens_hbm, front_ref, back_ref, left_ref, right_ref,
                dens_ref, first_col, last_col, lands, send_sems, recv_sems, load_sem):
    depth, rows, cols = dens_ref.shape
    nx, ny = lax.axis_size("gx"), lax.axis_size("gy")
    gx, gy = lax.axis_index("gx"), lax.axis_index("gy")
    ahead_x, behind_x = lax.rem(gx + 1, nx), lax.rem(gx + nx - 1, nx)
    ahead_y, behind_y = lax.rem(gy + 1, ny), lax.rem(gy + ny - 1, ny)
    barrier = pltpu.get_barrier_semaphore()
    for peer in ((ahead_x, gy), (behind_x, gy), (gx, ahead_y), (gx, behind_y)):
        pl.semaphore_signal(barrier, inc=1, device_id=peer, device_id_type=MESH_ID)
    load = pltpu.make_async_copy(dens_hbm, dens_ref, load_sem)
    load.start()
    load.wait()
    for z in range(rows):
        low = jnp.transpose(dens_ref[:, z, 0:128])
        high = jnp.transpose(dens_ref[:, z, cols - 128:cols])
        first_col[z:z + 1, :] = low[0:1, :]
        last_col[z:z + 1, :] = high[127:128, :]
    pl.semaphore_wait(barrier, 4)
    front_land, back_land, left_land, right_land = lands
    copies = [
        (dens_hbm.at[depth - 1], front_land, (ahead_x, gy)),
        (dens_hbm.at[0], back_land, (behind_x, gy)),
        (last_col, left_land, (gx, ahead_y)),
        (first_col, right_land, (gx, behind_y)),
    ]
    started = []
    for i, (src, dst, peer) in enumerate(copies):
        copy = pltpu.make_async_remote_copy(
            src_ref=src, dst_ref=dst, send_sem=send_sems.at[i], recv_sem=recv_sems.at[i],
            device_id=peer, device_id_type=MESH_ID,
        )
        copy.start()
        started.append(copy)
    for copy in started:
        copy.wait()
    front_ref[...] = jnp.where(gx == 0, 0.0, front_land[...])
    back_ref[...] = jnp.where(gx == nx - 1, 0.0, back_land[...])
    left_ref[...] = jnp.where(gy == 0, 0.0, left_land[...])
    right_ref[...] = jnp.where(gy == ny - 1, 0.0, right_land[...])


def halos(density):
    depth, rows, cols = density.shape
    vmem = pltpu.MemorySpace.VMEM
    plane = jax.ShapeDtypeStruct((rows, cols), jnp.float32)
    column = jax.ShapeDtypeStruct((rows, depth), jnp.float32)
    return pl.pallas_call(
        halo_kernel,
        out_shape=(plane, plane, column, column),
        in_specs=[pl.BlockSpec(memory_space=pl.ANY)],
        out_specs=tuple(pl.BlockSpec(memory_space=vmem) for _ in range(4)),
        scratch_shapes=[
            pltpu.VMEM((depth, rows, cols), jnp.float32),
            pltpu.VMEM((rows, depth), jnp.float32),
            pltpu.VMEM((rows, depth), jnp.float32),
            (
                pltpu.VMEM((rows, cols), jnp.float32),
                pltpu.VMEM((rows, cols), jnp.float32),
                pltpu.VMEM((rows, depth), jnp.float32),
                pltpu.VMEM((rows, depth), jnp.float32),
            ),
            pltpu.SemaphoreType.DMA((4,)),
            pltpu.SemaphoreType.DMA((4,)),
            pltpu.SemaphoreType.DMA,
        ],
        compiler_params=pltpu.CompilerParams(collective_id=1, has_side_effects=True),
    )(density)


def local(density, absorb):
    front, back, left, right = halos(density)
    n = lax.axis_size("gx")
    gathered = march(density, front, back, left, right, absorb, n)
    return finish(gathered, density.shape[1] // n, density.shape[2])


def solution(mesh):
    placed = (P("gx", None, "gy"), P(None, "gy"))
    return jax.shard_map(
        local,
        mesh=mesh,
        in_specs=placed,
        out_specs=(P(None, "gx", "gy"), P("gx", "gy")),
        check_vma=False,
    )
```

```python
import functools

import jax
import jax.numpy as jnp
from jax import lax
from jax.experimental import pallas as pl
from jax.experimental.pallas import tpu as pltpu
from jax.sharding import PartitionSpec as P

SLOPES = (2.0, -1.5, 0.8)
OFFSETS = (0.0, 0.5, -0.3)
HALF_SLOPES = tuple(0.5 * v for v in SLOPES)
HALF_OFFSETS = tuple(0.5 * v for v in OFFSETS)
LOG2_E = 1.4426950408889634
MESH_ID = pl.DeviceIdType.MESH


def march_kernel(last, n, dens_hbm, front_ref, back_ref, left_ref, right_ref, absorb_ref,
                 colour_ref, out_ref, part, mixed, recv_pair, recv,
                 send_pair, got_pair, send_sems, recv_sems, local_sem, dens_ref, load_sems):
    rows, cols = dens_ref.shape[1], dens_ref.shape[2]
    shape = (rows, 128)
    lane = lax.broadcasted_iota(jnp.int32, shape, 1)
    row = lax.broadcasted_iota(jnp.int32, shape, 0)
    first_lane, last_lane = lane == 0, lane == 127
    top_row, bottom_row = row == 0, row == rows - 1
    halves = cols // 128
    me = lax.axis_index("gx")
    col = lax.axis_index("gy")
    barrier = pltpu.get_barrier_semaphore()

    pairs = n // 2
    parity = lax.rem(me, 2)
    chip = me // 2
    sems = (send_pair, got_pair, send_sems, recv_sems, local_sem)

    def greet(i, carry):
        peer = 2 * lax.rem(chip + i, pairs) + parity
        pl.semaphore_signal(barrier, inc=1, device_id=(peer, col), device_id_type=MESH_ID)
        return carry

    pl.semaphore_signal(barrier, inc=1, device_id=(me + 1 - 2 * parity, col), device_id_type=MESH_ID)
    lax.fori_loop(1, pairs, greet, 0)
    pieces = load_sems.shape[0]
    piece = (last + 1) // pieces
    loads = [
        pltpu.make_async_copy(
            dens_hbm.at[pl.ds(c * piece, piece)], dens_ref.at[pl.ds(c * piece, piece)], load_sems.at[c]
        )
        for c in range(pieces)
    ]
    for load in loads:
        load.start()
    for h in range(halves):
        lanes = slice(h * 128, (h + 1) * 128)
        left_lanes = slice((h - 1) * 128, h * 128) if h > 0 else None
        right_lanes = slice((h + 1) * 128, (h + 2) * 128) if h + 1 < halves else None
        absorb = absorb_ref[:, lanes]
        fade = absorb * (-LOG2_E)

        def plane(ref_plane):
            return ref_plane[:, lanes]

        def step(x, carry):
            seen, total, t0, t1, t2, softsum = carry
            centre_plane = dens_ref.at[x]
            d = centre_plane[:, lanes]
            behind = jnp.where(x == 0, front_ref[:, lanes], dens_ref[jnp.maximum(x - 1, 0), :, lanes])
            ahead = jnp.where(x == last, back_ref[:, lanes], dens_ref[jnp.minimum(x + 1, last), :, lanes])
            span = left_ref.shape[1]
            halo_left = pltpu.roll(left_ref[...], lax.rem(span - x, span), 1)
            halo_right = pltpu.roll(right_ref[...], lax.rem(span + 127 - x, span), 1)
            from_left = pltpu.roll(d, 1, 1)
            from_right = pltpu.roll(d, 127, 1)
            if left_lanes is None:
                edge_left = halo_left
            else:
                edge_left = pltpu.roll(centre_plane[:, left_lanes], 1, 1)
            if right_lanes is None:
                edge_right = halo_right
            else:
                edge_right = pltpu.roll(centre_plane[:, right_lanes], 127, 1)
            left = jnp.where(first_lane, edge_left, from_left)
            right = jnp.where(last_lane, edge_right, from_right)
            above = jnp.where(top_row, 0.0, pltpu.roll(d, 1, 0))
            below = jnp.where(bottom_row, 0.0, pltpu.roll(d, rows - 1, 0))
            step_depth = ahead - behind
            step_row = below - above
            step_col = right - left
            facing = 0.18 * step_depth + 0.24 * step_row + 0.225 * step_col
            length2 = 0.25 * (step_depth * step_depth + step_row * step_row + step_col * step_col) + 1.0
            lighting = 0.25 + jnp.maximum(facing, 0.0) * lax.rsqrt(length2)
            soft = jnp.log(1.0 + jnp.exp(d))
            passed = jnp.exp2(fade * soft)
            seen_after = seen * passed
            weight = (seen - seen_after) * lighting
            return (
                seen_after,
                total + weight,
                t0 + weight * jnp.tanh(HALF_SLOPES[0] * d + HALF_OFFSETS[0]),
                t1 + weight * jnp.tanh(HALF_SLOPES[1] * d + HALF_OFFSETS[1]),
                t2 + weight * jnp.tanh(HALF_SLOPES[2] * d + HALF_OFFSETS[2]),
                softsum + soft,
            )

        zero = jnp.zeros(shape, jnp.float32)
        one = jnp.ones(shape, jnp.float32)
        carry = (one, zero, zero, zero, zero, zero)
        if h == 0:
            loads[0].wait()
            for c in range(pieces):
                if c + 1 < pieces:
                    loads[c + 1].wait()
                carry = lax.fori_loop(c * piece, (c + 1) * piece, step, carry, unroll=min(16, piece))
        else:
            carry = lax.fori_loop(0, last + 1, step, carry, unroll=16)
        _, total, t0, t1, t2, softsum = carry
        for k, value in enumerate((t0, t1, t2)):
            out_ref[k, :, lanes] = 0.5 * (total + value)
        out_ref[3, :, lanes] = absorb * softsum

    share = rows // n
    pairs = n // 2
    for z in range(rows):
        owner = z // share
        slot = (owner % 2) * pairs + owner // 2
        for k in range(4):
            for h in range(halves):
                r = ((z % share) * 4 + k) * halves + h
                part[slot, r:r + 1, :] = out_ref[k, z:z + 1, h * 128:(h + 1) * 128]
    exchange_and_combine(n, share, halves, me, col, barrier, part, mixed, recv_pair, recv,
                         sems, colour_ref)


def merge(front, back, share, halves):
    def rows_of(k):
        return [(r * 4 + k) * halves + h for r in range(share) for h in range(halves)]

    seen = jnp.exp(-jnp.concatenate([front[i:i + 1] for i in rows_of(3)], axis=0))
    pieces = [None] * (share * 4 * halves)
    for k in range(4):
        idx = rows_of(k)
        f = jnp.concatenate([front[i:i + 1] for i in idx], axis=0)
        b = jnp.concatenate([back[i:i + 1] for i in idx], axis=0)
        merged = f + b if k == 3 else f + seen * b
        for j, i in enumerate(idx):
            pieces[i] = merged[j:j + 1]
    return jnp.concatenate(pieces, axis=0)


def exchange_and_combine(n, share, halves, me, col, barrier, part, mixed, recv_pair, recv,
                         sems, colour_ref):
    pairs = n // 2
    parity = lax.rem(me, 2)
    partner = me + 1 - 2 * parity
    chip = me // 2
    send_pair, got_pair, send_sems, recv_sems, local_sem = sems
    pl.semaphore_wait(barrier, pairs)

    swap = pltpu.make_async_remote_copy(
        src_ref=part.at[pl.ds((1 - parity) * pairs, pairs)],
        dst_ref=recv_pair,
        send_sem=send_pair,
        recv_sem=got_pair,
        device_id=(partner, col),
        device_id_type=MESH_ID,
    )
    swap.start()
    swap.wait()

    def combine_pair(j, carry):
        mine = part[parity * pairs + j]
        theirs = recv_pair[j]
        first = parity == 0
        front = jnp.where(first, mine, theirs)
        back = jnp.where(first, theirs, mine)
        mixed[j] = merge(front, back, share, halves)
        return carry

    lax.fori_loop(0, pairs, combine_pair, 0)

    def link(j, slot):
        return pltpu.make_async_remote_copy(
            src_ref=mixed.at[j],
            dst_ref=recv.at[slot],
            send_sem=send_sems.at[j],
            recv_sem=recv_sems.at[slot],
            device_id=(2 * j + parity, col),
            device_id_type=MESH_ID,
        )

    def send(i, carry):
        link(lax.rem(chip + i, pairs), chip).start()
        return carry

    lax.fori_loop(1, pairs, send, 0)
    own = pltpu.make_async_copy(mixed.at[chip], recv.at[chip], local_sem)
    own.start()
    own.wait()

    def finish(i, carry):
        j = lax.rem(chip + i, pairs)
        link(j, j).wait_send()
        link(j, j).wait_recv()
        return carry

    lax.fori_loop(1, pairs, finish, 0)
    colour_ref[...] = recv[...]


def finish_kernel(share, halves, recv_ref, colour_ref, transmit_ref):
    pairs = recv_ref.shape[0]
    cols = colour_ref.shape[-1]
    zero = jnp.zeros((share * halves, 128), jnp.float32)

    def value(block, k):
        pieces = [block[(r * 4 + k) * halves:(r * 4 + k + 1) * halves] for r in range(share)]
        return pieces[0] if share == 1 else jnp.concatenate(pieces, axis=0)

    def accumulate(d, carry):
        front, c0, c1, c2 = carry
        block = recv_ref[d]
        seen = jnp.exp(-front)
        return (
            front + value(block, 3),
            c0 + value(block, 0) * seen,
            c1 + value(block, 1) * seen,
            c2 + value(block, 2) * seen,
        )

    front, c0, c1, c2 = lax.fori_loop(0, pairs, accumulate, (zero, zero, zero, zero))
    for k, c in enumerate((c0, c1, c2)):
        colour_ref[k] = c.reshape(share, cols)
    transmit_ref[...] = jnp.exp(-front).reshape(share, cols)


def finish(gathered, share, cols):
    vmem = pltpu.MemorySpace.VMEM
    return pl.pallas_call(
        functools.partial(finish_kernel, share, cols // 128),
        out_shape=(
            jax.ShapeDtypeStruct((3, share, cols), jnp.float32),
            jax.ShapeDtypeStruct((share, cols), jnp.float32),
        ),
        in_specs=[pl.BlockSpec(memory_space=vmem)],
        out_specs=(pl.BlockSpec(memory_space=vmem), pl.BlockSpec(memory_space=vmem)),
    )(gathered)


def march(density, front, back, left, right, absorb, n):
    depth, rows, cols = density.shape
    share = rows // n
    tiles = (n, share * 4 * cols // 128, 128)
    half_tiles = (n // 2,) + tiles[1:]
    vmem = pltpu.MemorySpace.VMEM
    return pl.pallas_call(
        functools.partial(march_kernel, depth - 1, n),
        out_shape=jax.ShapeDtypeStruct(half_tiles, jnp.float32),
        in_specs=[pl.BlockSpec(memory_space=pl.ANY)] + [pl.BlockSpec(memory_space=vmem)] * 5,
        out_specs=pl.BlockSpec(memory_space=vmem),
        scratch_shapes=[
            pltpu.VMEM((4, rows, cols), jnp.float32),
            pltpu.VMEM(tiles, jnp.float32),
            pltpu.VMEM(half_tiles, jnp.float32),
            pltpu.VMEM(half_tiles, jnp.float32),
            pltpu.VMEM(half_tiles, jnp.float32),
            pltpu.SemaphoreType.DMA,
            pltpu.SemaphoreType.DMA,
            pltpu.SemaphoreType.DMA((n // 2,)),
            pltpu.SemaphoreType.DMA((n // 2,)),
            pltpu.SemaphoreType.DMA,
            pltpu.VMEM((depth, rows, cols), jnp.float32),
            pltpu.SemaphoreType.DMA((8 if depth % 8 == 0 else 1,)),
        ],
        compiler_params=pltpu.CompilerParams(collective_id=0, has_side_effects=True),
    )(density, front, back, left, right, absorb)


def halo_kernel(dens_ref, front_ref, back_ref, left_ref, right_ref,
                first_col, last_col, lands, send_sems, recv_sems):
    depth, rows, cols = dens_ref.shape
    nx, ny = lax.axis_size("gx"), lax.axis_size("gy")
    gx, gy = lax.axis_index("gx"), lax.axis_index("gy")
    ahead_x, behind_x = lax.rem(gx + 1, nx), lax.rem(gx + nx - 1, nx)
    ahead_y, behind_y = lax.rem(gy + 1, ny), lax.rem(gy + ny - 1, ny)
    barrier = pltpu.get_barrier_semaphore()
    for peer in ((ahead_x, gy), (behind_x, gy), (gx, ahead_y), (gx, behind_y)):
        pl.semaphore_signal(barrier, inc=1, device_id=peer, device_id_type=MESH_ID)
    for z in range(rows):
        low = jnp.transpose(dens_ref[:, z, 0:128])
        high = jnp.transpose(dens_ref[:, z, cols - 128:cols])
        first_col[z:z + 1, :] = low[0:1, :]
        last_col[z:z + 1, :] = high[127:128, :]
    pl.semaphore_wait(barrier, 4)
    front_land, back_land, left_land, right_land = lands
    copies = [
        (dens_ref.at[depth - 1], front_land, (ahead_x, gy)),
        (dens_ref.at[0], back_land, (behind_x, gy)),
        (last_col, left_land, (gx, ahead_y)),
        (first_col, right_land, (gx, behind_y)),
    ]
    started = []
    for i, (src, dst, peer) in enumerate(copies):
        copy = pltpu.make_async_remote_copy(
            src_ref=src, dst_ref=dst, send_sem=send_sems.at[i], recv_sem=recv_sems.at[i],
            device_id=peer, device_id_type=MESH_ID,
        )
        copy.start()
        started.append(copy)
    for copy in started:
        copy.wait()
    front_ref[...] = jnp.where(gx == 0, 0.0, front_land[...])
    back_ref[...] = jnp.where(gx == nx - 1, 0.0, back_land[...])
    left_ref[...] = jnp.where(gy == 0, 0.0, left_land[...])
    right_ref[...] = jnp.where(gy == ny - 1, 0.0, right_land[...])


def halos(density):
    depth, rows, cols = density.shape
    vmem = pltpu.MemorySpace.VMEM
    plane = jax.ShapeDtypeStruct((rows, cols), jnp.float32)
    column = jax.ShapeDtypeStruct((rows, depth), jnp.float32)
    return pl.pallas_call(
        halo_kernel,
        out_shape=(plane, plane, column, column),
        in_specs=[pl.BlockSpec(memory_space=vmem)],
        out_specs=tuple(pl.BlockSpec(memory_space=vmem) for _ in range(4)),
        scratch_shapes=[
            pltpu.VMEM((rows, depth), jnp.float32),
            pltpu.VMEM((rows, depth), jnp.float32),
            (
                pltpu.VMEM((rows, cols), jnp.float32),
                pltpu.VMEM((rows, cols), jnp.float32),
                pltpu.VMEM((rows, depth), jnp.float32),
                pltpu.VMEM((rows, depth), jnp.float32),
            ),
            pltpu.SemaphoreType.DMA((4,)),
            pltpu.SemaphoreType.DMA((4,)),
        ],
        compiler_params=pltpu.CompilerParams(collective_id=1, has_side_effects=True),
    )(density)


def local(density, absorb):
    front, back, left, right = halos(density)
    n = lax.axis_size("gx")
    gathered = march(density, front, back, left, right, absorb, n)
    return finish(gathered, density.shape[1] // n, density.shape[2])


def solution(mesh):
    placed = (P("gx", None, "gy"), P(None, "gy"))
    return jax.shard_map(
        local,
        mesh=mesh,
        in_specs=placed,
        out_specs=(P(None, "gx", "gy"), P("gx", "gy")),
        check_vma=False,
    )
```

```python
import functools

import jax
import jax.numpy as jnp
from jax import lax
from jax.experimental import pallas as pl
from jax.experimental.pallas import tpu as pltpu
from jax.sharding import PartitionSpec as P

SLOPES = (2.0, -1.5, 0.8)
OFFSETS = (0.0, 0.5, -0.3)
HALF_SLOPES = tuple(0.5 * v for v in SLOPES)
HALF_OFFSETS = tuple(0.5 * v for v in OFFSETS)
LOG2_E = 1.4426950408889634
MESH_ID = pl.DeviceIdType.MESH


def march_kernel(last, n, dens_hbm, front_ref, back_ref, left_ref, right_ref, absorb_ref,
                 colour_ref, out_ref, part, mixed, recv_pair, recv,
                 send_pair, got_pair, send_sems, recv_sems, local_sem, dens_ref, load_sems):
    rows, cols = dens_ref.shape[1], dens_ref.shape[2]
    shape = (rows, 128)
    lane = lax.broadcasted_iota(jnp.int32, shape, 1)
    row = lax.broadcasted_iota(jnp.int32, shape, 0)
    first_lane, last_lane = lane == 0, lane == 127
    top_row, bottom_row = row == 0, row == rows - 1
    halves = cols // 128
    me = lax.axis_index("gx")
    col = lax.axis_index("gy")
    barrier = pltpu.get_barrier_semaphore()

    pairs = n // 2
    parity = lax.rem(me, 2)
    chip = me // 2
    sems = (send_pair, got_pair, send_sems, recv_sems, local_sem)

    def greet(i, carry):
        peer = 2 * lax.rem(chip + i, pairs) + parity
        pl.semaphore_signal(barrier, inc=1, device_id=(peer, col), device_id_type=MESH_ID)
        return carry

    pl.semaphore_signal(barrier, inc=1, device_id=(me + 1 - 2 * parity, col), device_id_type=MESH_ID)
    lax.fori_loop(1, pairs, greet, 0)
    pieces = load_sems.shape[0]
    piece = (last + 1) // pieces
    loads = [
        pltpu.make_async_copy(
            dens_hbm.at[pl.ds(c * piece, piece)], dens_ref.at[pl.ds(c * piece, piece)], load_sems.at[c]
        )
        for c in range(pieces)
    ]
    for load in loads:
        load.start()
    for h in range(halves):
        lanes = slice(h * 128, (h + 1) * 128)
        left_lanes = slice((h - 1) * 128, h * 128) if h > 0 else None
        right_lanes = slice((h + 1) * 128, (h + 2) * 128) if h + 1 < halves else None
        absorb = absorb_ref[:, lanes]
        fade = absorb * (-LOG2_E)

        def plane(ref_plane):
            return ref_plane[:, lanes]

        def step(x, carry):
            seen, total, t0, t1, t2, softsum = carry
            centre_plane = dens_ref.at[x]
            d = centre_plane[:, lanes]
            behind = jnp.where(x == 0, front_ref[:, lanes], dens_ref[jnp.maximum(x - 1, 0), :, lanes])
            ahead = jnp.where(x == last, back_ref[:, lanes], dens_ref[jnp.minimum(x + 1, last), :, lanes])
            span = left_ref.shape[1]
            halo_left = pltpu.roll(left_ref[...], lax.rem(span - x, span), 1)
            halo_right = pltpu.roll(right_ref[...], lax.rem(span + 127 - x, span), 1)
            from_left = pltpu.roll(d, 1, 1)
            from_right = pltpu.roll(d, 127, 1)
            if left_lanes is None:
                edge_left = halo_left
            else:
                edge_left = pltpu.roll(centre_plane[:, left_lanes], 1, 1)
            if right_lanes is None:
                edge_right = halo_right
            else:
                edge_right = pltpu.roll(centre_plane[:, right_lanes], 127, 1)
            left = jnp.where(first_lane, edge_left, from_left)
            right = jnp.where(last_lane, edge_right, from_right)
            above = jnp.where(top_row, 0.0, pltpu.roll(d, 1, 0))
            below = jnp.where(bottom_row, 0.0, pltpu.roll(d, rows - 1, 0))
            step_depth = ahead - behind
            step_row = below - above
            step_col = right - left
            facing = 0.18 * step_depth + 0.24 * step_row + 0.225 * step_col
            length2 = 0.25 * (step_depth * step_depth + step_row * step_row + step_col * step_col) + 1.0
            lighting = 0.25 + jnp.maximum(facing, 0.0) * lax.rsqrt(length2)
            soft = jnp.log(1.0 + jnp.exp(d))
            passed = jnp.exp2(fade * soft)
            seen_after = seen * passed
            weight = (seen - seen_after) * lighting
            return (
                seen_after,
                total + weight,
                t0 + weight * jnp.tanh(HALF_SLOPES[0] * d + HALF_OFFSETS[0]),
                t1 + weight * jnp.tanh(HALF_SLOPES[1] * d + HALF_OFFSETS[1]),
                t2 + weight * jnp.tanh(HALF_SLOPES[2] * d + HALF_OFFSETS[2]),
                softsum + soft,
            )

        zero = jnp.zeros(shape, jnp.float32)
        one = jnp.ones(shape, jnp.float32)
        carry = (one, zero, zero, zero, zero, zero)
        if h == 0:
            loads[0].wait()
            for c in range(pieces):
                if c + 1 < pieces:
                    loads[c + 1].wait()
                carry = lax.fori_loop(c * piece, (c + 1) * piece, step, carry, unroll=min(16, piece))
        else:
            carry = lax.fori_loop(0, last + 1, step, carry, unroll=16)
        _, total, t0, t1, t2, softsum = carry
        for k, value in enumerate((t0, t1, t2)):
            out_ref[k, :, lanes] = 0.5 * (total + value)
        out_ref[3, :, lanes] = absorb * softsum

    share = rows // n
    pairs = n // 2
    for z in range(rows):
        owner = z // share
        slot = (owner % 2) * pairs + owner // 2
        for k in range(4):
            for h in range(halves):
                r = ((z % share) * 4 + k) * halves + h
                part[slot, r:r + 1, :] = out_ref[k, z:z + 1, h * 128:(h + 1) * 128]
    exchange_and_combine(n, share, halves, me, col, barrier, part, mixed, recv_pair, recv,
                         sems, colour_ref)


def merge(front, back, share, halves):
    def rows_of(k):
        return [(r * 4 + k) * halves + h for r in range(share) for h in range(halves)]

    seen = jnp.exp(-jnp.concatenate([front[i:i + 1] for i in rows_of(3)], axis=0))
    pieces = [None] * (share * 4 * halves)
    for k in range(4):
        idx = rows_of(k)
        f = jnp.concatenate([front[i:i + 1] for i in idx], axis=0)
        b = jnp.concatenate([back[i:i + 1] for i in idx], axis=0)
        merged = f + b if k == 3 else f + seen * b
        for j, i in enumerate(idx):
            pieces[i] = merged[j:j + 1]
    return jnp.concatenate(pieces, axis=0)


def exchange_and_combine(n, share, halves, me, col, barrier, part, mixed, recv_pair, recv,
                         sems, colour_ref):
    pairs = n // 2
    parity = lax.rem(me, 2)
    partner = me + 1 - 2 * parity
    chip = me // 2
    send_pair, got_pair, send_sems, recv_sems, local_sem = sems
    pl.semaphore_wait(barrier, pairs)

    swap = pltpu.make_async_remote_copy(
        src_ref=part.at[pl.ds((1 - parity) * pairs, pairs)],
        dst_ref=recv_pair,
        send_sem=send_pair,
        recv_sem=got_pair,
        device_id=(partner, col),
        device_id_type=MESH_ID,
    )
    swap.start()
    swap.wait()

    def combine_pair(j, carry):
        mine = part[parity * pairs + j]
        theirs = recv_pair[j]
        first = parity == 0
        front = jnp.where(first, mine, theirs)
        back = jnp.where(first, theirs, mine)
        mixed[j] = merge(front, back, share, halves)
        return carry

    lax.fori_loop(0, pairs, combine_pair, 0)

    def link(j, slot):
        return pltpu.make_async_remote_copy(
            src_ref=mixed.at[j],
            dst_ref=recv.at[slot],
            send_sem=send_sems.at[j],
            recv_sem=recv_sems.at[slot],
            device_id=(2 * j + parity, col),
            device_id_type=MESH_ID,
        )

    def send(i, carry):
        link(lax.rem(chip + i, pairs), chip).start()
        return carry

    lax.fori_loop(1, pairs, send, 0)
    own = pltpu.make_async_copy(mixed.at[chip], recv.at[chip], local_sem)
    own.start()
    own.wait()

    def finish(i, carry):
        j = lax.rem(chip + i, pairs)
        link(j, j).wait_send()
        link(j, j).wait_recv()
        return carry

    lax.fori_loop(1, pairs, finish, 0)
    colour_ref[...] = recv[...]


def finish_kernel(share, halves, recv_ref, colour_ref, transmit_ref):
    pairs = recv_ref.shape[0]
    cols = colour_ref.shape[-1]
    zero = jnp.zeros((share * halves, 128), jnp.float32)

    def value(block, k):
        pieces = [block[(r * 4 + k) * halves:(r * 4 + k + 1) * halves] for r in range(share)]
        return pieces[0] if share == 1 else jnp.concatenate(pieces, axis=0)

    def accumulate(d, carry):
        front, c0, c1, c2 = carry
        block = recv_ref[d]
        seen = jnp.exp(-front)
        return (
            front + value(block, 3),
            c0 + value(block, 0) * seen,
            c1 + value(block, 1) * seen,
            c2 + value(block, 2) * seen,
        )

    front, c0, c1, c2 = lax.fori_loop(0, pairs, accumulate, (zero, zero, zero, zero))
    for k, c in enumerate((c0, c1, c2)):
        colour_ref[k] = c.reshape(share, cols)
    transmit_ref[...] = jnp.exp(-front).reshape(share, cols)


def finish(gathered, share, cols):
    vmem = pltpu.MemorySpace.VMEM
    return pl.pallas_call(
        functools.partial(finish_kernel, share, cols // 128),
        out_shape=(
            jax.ShapeDtypeStruct((3, share, cols), jnp.float32),
            jax.ShapeDtypeStruct((share, cols), jnp.float32),
        ),
        in_specs=[pl.BlockSpec(memory_space=vmem)],
        out_specs=(pl.BlockSpec(memory_space=vmem), pl.BlockSpec(memory_space=vmem)),
    )(gathered)


def march(density, front, back, left, right, absorb, n):
    depth, rows, cols = density.shape
    share = rows // n
    tiles = (n, share * 4 * cols // 128, 128)
    half_tiles = (n // 2,) + tiles[1:]
    vmem = pltpu.MemorySpace.VMEM
    return pl.pallas_call(
        functools.partial(march_kernel, depth - 1, n),
        out_shape=jax.ShapeDtypeStruct(half_tiles, jnp.float32),
        in_specs=[pl.BlockSpec(memory_space=pl.ANY)] + [pl.BlockSpec(memory_space=vmem)] * 5,
        out_specs=pl.BlockSpec(memory_space=vmem),
        scratch_shapes=[
            pltpu.VMEM((4, rows, cols), jnp.float32),
            pltpu.VMEM(tiles, jnp.float32),
            pltpu.VMEM(half_tiles, jnp.float32),
            pltpu.VMEM(half_tiles, jnp.float32),
            pltpu.VMEM(half_tiles, jnp.float32),
            pltpu.SemaphoreType.DMA,
            pltpu.SemaphoreType.DMA,
            pltpu.SemaphoreType.DMA((n // 2,)),
            pltpu.SemaphoreType.DMA((n // 2,)),
            pltpu.SemaphoreType.DMA,
            pltpu.VMEM((depth, rows, cols), jnp.float32),
            pltpu.SemaphoreType.DMA((8 if depth % 8 == 0 else 1,)),
        ],
        compiler_params=pltpu.CompilerParams(collective_id=0, has_side_effects=True),
    )(density, front, back, left, right, absorb)


def halo_kernel(dens_hbm, front_ref, back_ref, left_ref, right_ref,
                dens_ref, first_col, last_col, lands, send_sems, recv_sems, load_sems):
    depth, rows, cols = dens_ref.shape
    nx, ny = lax.axis_size("gx"), lax.axis_size("gy")
    gx, gy = lax.axis_index("gx"), lax.axis_index("gy")
    ahead_x, behind_x = lax.rem(gx + 1, nx), lax.rem(gx + nx - 1, nx)
    ahead_y, behind_y = lax.rem(gy + 1, ny), lax.rem(gy + ny - 1, ny)
    barrier = pltpu.get_barrier_semaphore()
    for peer in ((ahead_x, gy), (behind_x, gy), (gx, ahead_y), (gx, behind_y)):
        pl.semaphore_signal(barrier, inc=1, device_id=peer, device_id_type=MESH_ID)
    group = rows // load_sems.shape[0]
    loads = [
        pltpu.make_async_copy(
            dens_hbm.at[:, pl.ds(g * group, group)], dens_ref.at[:, pl.ds(g * group, group)], load_sems.at[g]
        )
        for g in range(load_sems.shape[0])
    ]
    for load in loads:
        load.start()
    for z in range(rows):
        if z % group == 0:
            loads[z // group].wait()
        low = jnp.transpose(dens_ref[:, z, 0:128])
        high = jnp.transpose(dens_ref[:, z, cols - 128:cols])
        first_col[z:z + 1, :] = low[0:1, :]
        last_col[z:z + 1, :] = high[127:128, :]
    pl.semaphore_wait(barrier, 4)
    front_land, back_land, left_land, right_land = lands
    copies = [
        (dens_hbm.at[depth - 1], front_land, (ahead_x, gy)),
        (dens_hbm.at[0], back_land, (behind_x, gy)),
        (last_col, left_land, (gx, ahead_y)),
        (first_col, right_land, (gx, behind_y)),
    ]
    started = []
    for i, (src, dst, peer) in enumerate(copies):
        copy = pltpu.make_async_remote_copy(
            src_ref=src, dst_ref=dst, send_sem=send_sems.at[i], recv_sem=recv_sems.at[i],
            device_id=peer, device_id_type=MESH_ID,
        )
        copy.start()
        started.append(copy)
    for copy in started:
        copy.wait()
    front_ref[...] = jnp.where(gx == 0, 0.0, front_land[...])
    back_ref[...] = jnp.where(gx == nx - 1, 0.0, back_land[...])
    left_ref[...] = jnp.where(gy == 0, 0.0, left_land[...])
    right_ref[...] = jnp.where(gy == ny - 1, 0.0, right_land[...])


def halos(density):
    depth, rows, cols = density.shape
    vmem = pltpu.MemorySpace.VMEM
    plane = jax.ShapeDtypeStruct((rows, cols), jnp.float32)
    column = jax.ShapeDtypeStruct((rows, depth), jnp.float32)
    return pl.pallas_call(
        halo_kernel,
        out_shape=(plane, plane, column, column),
        in_specs=[pl.BlockSpec(memory_space=pl.ANY)],
        out_specs=tuple(pl.BlockSpec(memory_space=vmem) for _ in range(4)),
        scratch_shapes=[
            pltpu.VMEM((depth, rows, cols), jnp.float32),
            pltpu.VMEM((rows, depth), jnp.float32),
            pltpu.VMEM((rows, depth), jnp.float32),
            (
                pltpu.VMEM((rows, cols), jnp.float32),
                pltpu.VMEM((rows, cols), jnp.float32),
                pltpu.VMEM((rows, depth), jnp.float32),
                pltpu.VMEM((rows, depth), jnp.float32),
            ),
            pltpu.SemaphoreType.DMA((4,)),
            pltpu.SemaphoreType.DMA((4,)),
            pltpu.SemaphoreType.DMA((rows // 8 if rows % 8 == 0 else 1,)),
        ],
        compiler_params=pltpu.CompilerParams(collective_id=1, has_side_effects=True),
    )(density)


def local(density, absorb):
    front, back, left, right = halos(density)
    n = lax.axis_size("gx")
    gathered = march(density, front, back, left, right, absorb, n)
    return finish(gathered, density.shape[1] // n, density.shape[2])


def solution(mesh):
    placed = (P("gx", None, "gy"), P(None, "gy"))
    return jax.shard_map(
        local,
        mesh=mesh,
        in_specs=placed,
        out_specs=(P(None, "gx", "gy"), P("gx", "gy")),
        check_vma=False,
    )
```

```python
import functools

import jax
import jax.numpy as jnp
from jax import lax
from jax.experimental import pallas as pl
from jax.experimental.pallas import tpu as pltpu
from jax.sharding import PartitionSpec as P

SLOPES = (2.0, -1.5, 0.8)
OFFSETS = (0.0, 0.5, -0.3)
HALF_SLOPES = tuple(0.5 * v for v in SLOPES)
HALF_OFFSETS = tuple(0.5 * v for v in OFFSETS)
LOG2_E = 1.4426950408889634
MESH_ID = pl.DeviceIdType.MESH


def march_kernel(last, n, dens_hbm, front_ref, back_ref, left_ref, right_ref, absorb_ref,
                 colour_ref, out_ref, part, mixed, recv_pair, recv,
                 send_pair, got_pair, send_sems, recv_sems, local_sem, dens_ref, load_sems):
    rows, cols = dens_ref.shape[1], dens_ref.shape[2]
    shape = (rows, 128)
    lane = lax.broadcasted_iota(jnp.int32, shape, 1)
    row = lax.broadcasted_iota(jnp.int32, shape, 0)
    first_lane, last_lane = lane == 0, lane == 127
    top_row, bottom_row = row == 0, row == rows - 1
    halves = cols // 128
    me = lax.axis_index("gx")
    col = lax.axis_index("gy")
    barrier = pltpu.get_barrier_semaphore()

    pairs = n // 2
    parity = lax.rem(me, 2)
    chip = me // 2
    sems = (send_pair, got_pair, send_sems, recv_sems, local_sem)

    def greet(i, carry):
        peer = 2 * lax.rem(chip + i, pairs) + parity
        pl.semaphore_signal(barrier, inc=1, device_id=(peer, col), device_id_type=MESH_ID)
        return carry

    pl.semaphore_signal(barrier, inc=1, device_id=(me + 1 - 2 * parity, col), device_id_type=MESH_ID)
    lax.fori_loop(1, pairs, greet, 0)
    pieces = load_sems.shape[0]
    piece = (last + 1) // pieces
    loads = [
        pltpu.make_async_copy(
            dens_hbm.at[pl.ds(c * piece, piece)], dens_ref.at[pl.ds(c * piece, piece)], load_sems.at[c]
        )
        for c in range(pieces)
    ]
    for load in loads:
        load.start()
    for h in range(halves):
        lanes = slice(h * 128, (h + 1) * 128)
        left_lanes = slice((h - 1) * 128, h * 128) if h > 0 else None
        right_lanes = slice((h + 1) * 128, (h + 2) * 128) if h + 1 < halves else None
        absorb = absorb_ref[:, lanes]
        fade = absorb * (-LOG2_E)

        def plane(ref_plane):
            return ref_plane[:, lanes]

        def step(x, carry):
            seen, total, t0, t1, t2, softsum = carry
            centre_plane = dens_ref.at[x]
            d = centre_plane[:, lanes]
            behind = jnp.where(x == 0, front_ref[:, lanes], dens_ref[jnp.maximum(x - 1, 0), :, lanes])
            ahead = jnp.where(x == last, back_ref[:, lanes], dens_ref[jnp.minimum(x + 1, last), :, lanes])
            span = left_ref.shape[1]
            halo_left = pltpu.roll(left_ref[...], lax.rem(span - x, span), 1)
            halo_right = pltpu.roll(right_ref[...], lax.rem(span + 127 - x, span), 1)
            from_left = pltpu.roll(d, 1, 1)
            from_right = pltpu.roll(d, 127, 1)
            if left_lanes is None:
                edge_left = halo_left
            else:
                edge_left = pltpu.roll(centre_plane[:, left_lanes], 1, 1)
            if right_lanes is None:
                edge_right = halo_right
            else:
                edge_right = pltpu.roll(centre_plane[:, right_lanes], 127, 1)
            left = jnp.where(first_lane, edge_left, from_left)
            right = jnp.where(last_lane, edge_right, from_right)
            above = jnp.where(top_row, 0.0, pltpu.roll(d, 1, 0))
            below = jnp.where(bottom_row, 0.0, pltpu.roll(d, rows - 1, 0))
            step_depth = ahead - behind
            step_row = below - above
            step_col = right - left
            facing = 0.18 * step_depth + 0.24 * step_row + 0.225 * step_col
            length2 = 0.25 * (step_depth * step_depth + step_row * step_row + step_col * step_col) + 1.0
            lighting = 0.25 + jnp.maximum(facing, 0.0) * lax.rsqrt(length2)
            soft = jnp.log(1.0 + jnp.exp(d))
            passed = jnp.exp2(fade * soft)
            seen_after = seen * passed
            weight = (seen - seen_after) * lighting
            return (
                seen_after,
                total + weight,
                t0 + weight * jnp.tanh(HALF_SLOPES[0] * d + HALF_OFFSETS[0]),
                t1 + weight * jnp.tanh(HALF_SLOPES[1] * d + HALF_OFFSETS[1]),
                t2 + weight * jnp.tanh(HALF_SLOPES[2] * d + HALF_OFFSETS[2]),
                softsum + soft,
            )

        zero = jnp.zeros(shape, jnp.float32)
        one = jnp.ones(shape, jnp.float32)
        carry = (one, zero, zero, zero, zero, zero)
        if h == 0:
            loads[0].wait()
            for c in range(pieces):
                if c + 1 < pieces:
                    loads[c + 1].wait()
                carry = lax.fori_loop(c * piece, (c + 1) * piece, step, carry, unroll=piece)
        else:
            carry = lax.fori_loop(0, last + 1, step, carry, unroll=32)
        _, total, t0, t1, t2, softsum = carry
        for k, value in enumerate((t0, t1, t2)):
            out_ref[k, :, lanes] = 0.5 * (total + value)
        out_ref[3, :, lanes] = absorb * softsum

    share = rows // n
    pairs = n // 2
    for z in range(rows):
        owner = z // share
        slot = (owner % 2) * pairs + owner // 2
        for k in range(4):
            for h in range(halves):
                r = ((z % share) * 4 + k) * halves + h
                part[slot, r:r + 1, :] = out_ref[k, z:z + 1, h * 128:(h + 1) * 128]
    exchange_and_combine(n, share, halves, me, col, barrier, part, mixed, recv_pair, recv,
                         sems, colour_ref)


def merge(front, back, share, halves):
    def rows_of(k):
        return [(r * 4 + k) * halves + h for r in range(share) for h in range(halves)]

    seen = jnp.exp(-jnp.concatenate([front[i:i + 1] for i in rows_of(3)], axis=0))
    pieces = [None] * (share * 4 * halves)
    for k in range(4):
        idx = rows_of(k)
        f = jnp.concatenate([front[i:i + 1] for i in idx], axis=0)
        b = jnp.concatenate([back[i:i + 1] for i in idx], axis=0)
        merged = f + b if k == 3 else f + seen * b
        for j, i in enumerate(idx):
            pieces[i] = merged[j:j + 1]
    return jnp.concatenate(pieces, axis=0)


def exchange_and_combine(n, share, halves, me, col, barrier, part, mixed, recv_pair, recv,
                         sems, colour_ref):
    pairs = n // 2
    parity = lax.rem(me, 2)
    partner = me + 1 - 2 * parity
    chip = me // 2
    send_pair, got_pair, send_sems, recv_sems, local_sem = sems
    pl.semaphore_wait(barrier, pairs)

    swap = pltpu.make_async_remote_copy(
        src_ref=part.at[pl.ds((1 - parity) * pairs, pairs)],
        dst_ref=recv_pair,
        send_sem=send_pair,
        recv_sem=got_pair,
        device_id=(partner, col),
        device_id_type=MESH_ID,
    )
    swap.start()
    swap.wait()

    def combine_pair(j, carry):
        mine = part[parity * pairs + j]
        theirs = recv_pair[j]
        first = parity == 0
        front = jnp.where(first, mine, theirs)
        back = jnp.where(first, theirs, mine)
        mixed[j] = merge(front, back, share, halves)
        return carry

    lax.fori_loop(0, pairs, combine_pair, 0)

    def link(j, slot):
        return pltpu.make_async_remote_copy(
            src_ref=mixed.at[j],
            dst_ref=recv.at[slot],
            send_sem=send_sems.at[j],
            recv_sem=recv_sems.at[slot],
            device_id=(2 * j + parity, col),
            device_id_type=MESH_ID,
        )

    def send(i, carry):
        link(lax.rem(chip + i, pairs), chip).start()
        return carry

    lax.fori_loop(1, pairs, send, 0)
    own = pltpu.make_async_copy(mixed.at[chip], recv.at[chip], local_sem)
    own.start()
    own.wait()

    def finish(i, carry):
        j = lax.rem(chip + i, pairs)
        link(j, j).wait_send()
        link(j, j).wait_recv()
        return carry

    lax.fori_loop(1, pairs, finish, 0)
    colour_ref[...] = recv[...]


def finish_kernel(share, halves, recv_ref, colour_ref, transmit_ref):
    pairs = recv_ref.shape[0]
    cols = colour_ref.shape[-1]
    zero = jnp.zeros((share * halves, 128), jnp.float32)

    def value(block, k):
        pieces = [block[(r * 4 + k) * halves:(r * 4 + k + 1) * halves] for r in range(share)]
        return pieces[0] if share == 1 else jnp.concatenate(pieces, axis=0)

    def accumulate(d, carry):
        front, c0, c1, c2 = carry
        block = recv_ref[d]
        seen = jnp.exp(-front)
        return (
            front + value(block, 3),
            c0 + value(block, 0) * seen,
            c1 + value(block, 1) * seen,
            c2 + value(block, 2) * seen,
        )

    front, c0, c1, c2 = lax.fori_loop(0, pairs, accumulate, (zero, zero, zero, zero))
    for k, c in enumerate((c0, c1, c2)):
        colour_ref[k] = c.reshape(share, cols)
    transmit_ref[...] = jnp.exp(-front).reshape(share, cols)


def finish(gathered, share, cols):
    vmem = pltpu.MemorySpace.VMEM
    return pl.pallas_call(
        functools.partial(finish_kernel, share, cols // 128),
        out_shape=(
            jax.ShapeDtypeStruct((3, share, cols), jnp.float32),
            jax.ShapeDtypeStruct((share, cols), jnp.float32),
        ),
        in_specs=[pl.BlockSpec(memory_space=vmem)],
        out_specs=(pl.BlockSpec(memory_space=vmem), pl.BlockSpec(memory_space=vmem)),
    )(gathered)


def march(density, front, back, left, right, absorb, n):
    depth, rows, cols = density.shape
    share = rows // n
    tiles = (n, share * 4 * cols // 128, 128)
    half_tiles = (n // 2,) + tiles[1:]
    vmem = pltpu.MemorySpace.VMEM
    return pl.pallas_call(
        functools.partial(march_kernel, depth - 1, n),
        out_shape=jax.ShapeDtypeStruct(half_tiles, jnp.float32),
        in_specs=[pl.BlockSpec(memory_space=pl.ANY)] + [pl.BlockSpec(memory_space=vmem)] * 5,
        out_specs=pl.BlockSpec(memory_space=vmem),
        scratch_shapes=[
            pltpu.VMEM((4, rows, cols), jnp.float32),
            pltpu.VMEM(tiles, jnp.float32),
            pltpu.VMEM(half_tiles, jnp.float32),
            pltpu.VMEM(half_tiles, jnp.float32),
            pltpu.VMEM(half_tiles, jnp.float32),
            pltpu.SemaphoreType.DMA,
            pltpu.SemaphoreType.DMA,
            pltpu.SemaphoreType.DMA((n // 2,)),
            pltpu.SemaphoreType.DMA((n // 2,)),
            pltpu.SemaphoreType.DMA,
            pltpu.VMEM((depth, rows, cols), jnp.float32),
            pltpu.SemaphoreType.DMA((8 if depth % 8 == 0 else 1,)),
        ],
        compiler_params=pltpu.CompilerParams(collective_id=0, has_side_effects=True),
    )(density, front, back, left, right, absorb)


def halo_kernel(dens_hbm, front_ref, back_ref, left_ref, right_ref,
                dens_ref, first_col, last_col, lands, send_sems, recv_sems, load_sems):
    depth, rows, cols = dens_ref.shape
    nx, ny = lax.axis_size("gx"), lax.axis_size("gy")
    gx, gy = lax.axis_index("gx"), lax.axis_index("gy")
    ahead_x, behind_x = lax.rem(gx + 1, nx), lax.rem(gx + nx - 1, nx)
    ahead_y, behind_y = lax.rem(gy + 1, ny), lax.rem(gy + ny - 1, ny)
    barrier = pltpu.get_barrier_semaphore()
    for peer in ((ahead_x, gy), (behind_x, gy), (gx, ahead_y), (gx, behind_y)):
        pl.semaphore_signal(barrier, inc=1, device_id=peer, device_id_type=MESH_ID)
    group = rows // load_sems.shape[0]
    loads = [
        pltpu.make_async_copy(
            dens_hbm.at[:, pl.ds(g * group, group)], dens_ref.at[:, pl.ds(g * group, group)], load_sems.at[g]
        )
        for g in range(load_sems.shape[0])
    ]
    for load in loads:
        load.start()
    for z in range(rows):
        if z % group == 0:
            loads[z // group].wait()
        low = jnp.transpose(dens_ref[:, z, 0:128])
        high = jnp.transpose(dens_ref[:, z, cols - 128:cols])
        first_col[z:z + 1, :] = low[0:1, :]
        last_col[z:z + 1, :] = high[127:128, :]
    pl.semaphore_wait(barrier, 4)
    front_land, back_land, left_land, right_land = lands
    copies = [
        (dens_hbm.at[depth - 1], front_land, (ahead_x, gy)),
        (dens_hbm.at[0], back_land, (behind_x, gy)),
        (last_col, left_land, (gx, ahead_y)),
        (first_col, right_land, (gx, behind_y)),
    ]
    started = []
    for i, (src, dst, peer) in enumerate(copies):
        copy = pltpu.make_async_remote_copy(
            src_ref=src, dst_ref=dst, send_sem=send_sems.at[i], recv_sem=recv_sems.at[i],
            device_id=peer, device_id_type=MESH_ID,
        )
        copy.start()
        started.append(copy)
    for copy in started:
        copy.wait()
    front_ref[...] = jnp.where(gx == 0, 0.0, front_land[...])
    back_ref[...] = jnp.where(gx == nx - 1, 0.0, back_land[...])
    left_ref[...] = jnp.where(gy == 0, 0.0, left_land[...])
    right_ref[...] = jnp.where(gy == ny - 1, 0.0, right_land[...])


def halos(density):
    depth, rows, cols = density.shape
    vmem = pltpu.MemorySpace.VMEM
    plane = jax.ShapeDtypeStruct((rows, cols), jnp.float32)
    column = jax.ShapeDtypeStruct((rows, depth), jnp.float32)
    return pl.pallas_call(
        halo_kernel,
        out_shape=(plane, plane, column, column),
        in_specs=[pl.BlockSpec(memory_space=pl.ANY)],
        out_specs=tuple(pl.BlockSpec(memory_space=vmem) for _ in range(4)),
        scratch_shapes=[
            pltpu.VMEM((depth, rows, cols), jnp.float32),
            pltpu.VMEM((rows, depth), jnp.float32),
            pltpu.VMEM((rows, depth), jnp.float32),
            (
                pltpu.VMEM((rows, cols), jnp.float32),
                pltpu.VMEM((rows, cols), jnp.float32),
                pltpu.VMEM((rows, depth), jnp.float32),
                pltpu.VMEM((rows, depth), jnp.float32),
            ),
            pltpu.SemaphoreType.DMA((4,)),
            pltpu.SemaphoreType.DMA((4,)),
            pltpu.SemaphoreType.DMA((rows // 8 if rows % 8 == 0 else 1,)),
        ],
        compiler_params=pltpu.CompilerParams(collective_id=1, has_side_effects=True),
    )(density)


def local(density, absorb):
    front, back, left, right = halos(density)
    n = lax.axis_size("gx")
    gathered = march(density, front, back, left, right, absorb, n)
    return finish(gathered, density.shape[1] // n, density.shape[2])


def solution(mesh):
    placed = (P("gx", None, "gy"), P(None, "gy"))
    return jax.shard_map(
        local,
        mesh=mesh,
        in_specs=placed,
        out_specs=(P(None, "gx", "gy"), P("gx", "gy")),
        check_vma=False,
    )
```

```python
import functools

import jax
import jax.numpy as jnp
from jax import lax
from jax.experimental import pallas as pl
from jax.experimental.pallas import tpu as pltpu
from jax.sharding import PartitionSpec as P

SLOPES = (2.0, -1.5, 0.8)
OFFSETS = (0.0, 0.5, -0.3)
HALF_SLOPES = tuple(0.5 * v for v in SLOPES)
HALF_OFFSETS = tuple(0.5 * v for v in OFFSETS)
LOG2_E = 1.4426950408889634
MESH_ID = pl.DeviceIdType.MESH


def march_kernel(last, n, dens_hbm, front_ref, back_ref, left_ref, right_ref, absorb_ref,
                 colour_ref, out_ref, part, mixed, recv_pair, recv,
                 send_pair, got_pair, send_sems, recv_sems, local_sem, dens_ref, load_sems):
    rows, cols = dens_ref.shape[1], dens_ref.shape[2]
    shape = (rows, 128)
    lane = lax.broadcasted_iota(jnp.int32, shape, 1)
    row = lax.broadcasted_iota(jnp.int32, shape, 0)
    first_lane, last_lane = lane == 0, lane == 127
    top_row, bottom_row = row == 0, row == rows - 1
    halves = cols // 128
    me = lax.axis_index("gx")
    col = lax.axis_index("gy")
    barrier = pltpu.get_barrier_semaphore()

    pairs = n // 2
    parity = lax.rem(me, 2)
    chip = me // 2
    sems = (send_pair, got_pair, send_sems, recv_sems, local_sem)

    def greet(i, carry):
        peer = 2 * lax.rem(chip + i, pairs) + parity
        pl.semaphore_signal(barrier, inc=1, device_id=(peer, col), device_id_type=MESH_ID)
        return carry

    pl.semaphore_signal(barrier, inc=1, device_id=(me + 1 - 2 * parity, col), device_id_type=MESH_ID)
    lax.fori_loop(1, pairs, greet, 0)
    pieces = load_sems.shape[0]
    piece = (last + 1) // pieces
    loads = [
        pltpu.make_async_copy(
            dens_hbm.at[pl.ds(c * piece, piece)], dens_ref.at[pl.ds(c * piece, piece)], load_sems.at[c]
        )
        for c in range(pieces)
    ]
    for load in loads:
        load.start()
    for h in range(halves):
        lanes = slice(h * 128, (h + 1) * 128)
        left_lanes = slice((h - 1) * 128, h * 128) if h > 0 else None
        right_lanes = slice((h + 1) * 128, (h + 2) * 128) if h + 1 < halves else None
        absorb = absorb_ref[:, lanes]
        fade = absorb * (-LOG2_E)

        def plane(ref_plane):
            return ref_plane[:, lanes]

        def step(x, carry):
            seen, total, t0, t1, t2, softsum = carry
            centre_plane = dens_ref.at[x]
            d = centre_plane[:, lanes]
            behind = jnp.where(x == 0, front_ref[:, lanes], dens_ref[jnp.maximum(x - 1, 0), :, lanes])
            ahead = jnp.where(x == last, back_ref[:, lanes], dens_ref[jnp.minimum(x + 1, last), :, lanes])
            span = left_ref.shape[1]
            halo_left = pltpu.roll(left_ref[...], lax.rem(span - x, span), 1)
            halo_right = pltpu.roll(right_ref[...], lax.rem(span + 127 - x, span), 1)
            from_left = pltpu.roll(d, 1, 1)
            from_right = pltpu.roll(d, 127, 1)
            if left_lanes is None:
                edge_left = halo_left
            else:
                edge_left = pltpu.roll(centre_plane[:, left_lanes], 1, 1)
            if right_lanes is None:
                edge_right = halo_right
            else:
                edge_right = pltpu.roll(centre_plane[:, right_lanes], 127, 1)
            left = jnp.where(first_lane, edge_left, from_left)
            right = jnp.where(last_lane, edge_right, from_right)
            above = jnp.where(top_row, 0.0, pltpu.roll(d, 1, 0))
            below = jnp.where(bottom_row, 0.0, pltpu.roll(d, rows - 1, 0))
            step_depth = ahead - behind
            step_row = below - above
            step_col = right - left
            facing = 0.18 * step_depth + 0.24 * step_row + 0.225 * step_col
            length2 = 0.25 * (step_depth * step_depth + step_row * step_row + step_col * step_col) + 1.0
            lighting = 0.25 + jnp.maximum(facing, 0.0) * lax.rsqrt(length2)
            soft = jnp.log(1.0 + jnp.exp(d))
            passed = jnp.exp2(fade * soft)
            seen_after = seen * passed
            weight = (seen - seen_after) * lighting
            return (
                seen_after,
                total + weight,
                t0 + weight * jnp.tanh(HALF_SLOPES[0] * d + HALF_OFFSETS[0]),
                t1 + weight * jnp.tanh(HALF_SLOPES[1] * d + HALF_OFFSETS[1]),
                t2 + weight * jnp.tanh(HALF_SLOPES[2] * d + HALF_OFFSETS[2]),
                softsum + soft,
            )

        zero = jnp.zeros(shape, jnp.float32)
        one = jnp.ones(shape, jnp.float32)
        carry = (one, zero, zero, zero, zero, zero)
        if h == 0:
            loads[0].wait()
            for c in range(pieces):
                if c + 1 < pieces:
                    loads[c + 1].wait()
                carry = lax.fori_loop(c * piece, (c + 1) * piece, step, carry, unroll=min(16, piece))
        else:
            carry = lax.fori_loop(0, last + 1, step, carry, unroll=16)
        _, total, t0, t1, t2, softsum = carry
        for k, value in enumerate((t0, t1, t2)):
            out_ref[k, :, lanes] = 0.5 * (total + value)
        out_ref[3, :, lanes] = absorb * softsum

    share = rows // n
    pairs = n // 2
    for z in range(rows):
        owner = z // share
        slot = (owner % 2) * pairs + owner // 2
        for k in range(4):
            for h in range(halves):
                r = ((z % share) * 4 + k) * halves + h
                part[slot, r:r + 1, :] = out_ref[k, z:z + 1, h * 128:(h + 1) * 128]
    exchange_and_combine(n, share, halves, me, col, barrier, part, mixed, recv_pair, recv,
                         sems, colour_ref)


def merge(front, back, share, halves):
    def rows_of(k):
        return [(r * 4 + k) * halves + h for r in range(share) for h in range(halves)]

    seen = jnp.exp(-jnp.concatenate([front[i:i + 1] for i in rows_of(3)], axis=0))
    pieces = [None] * (share * 4 * halves)
    for k in range(4):
        idx = rows_of(k)
        f = jnp.concatenate([front[i:i + 1] for i in idx], axis=0)
        b = jnp.concatenate([back[i:i + 1] for i in idx], axis=0)
        merged = f + b if k == 3 else f + seen * b
        for j, i in enumerate(idx):
            pieces[i] = merged[j:j + 1]
    return jnp.concatenate(pieces, axis=0)


def exchange_and_combine(n, share, halves, me, col, barrier, part, mixed, recv_pair, recv,
                         sems, colour_ref):
    pairs = n // 2
    parity = lax.rem(me, 2)
    partner = me + 1 - 2 * parity
    chip = me // 2
    send_pair, got_pair, send_sems, recv_sems, local_sem = sems
    pl.semaphore_wait(barrier, pairs)

    swap = pltpu.make_async_remote_copy(
        src_ref=part.at[pl.ds((1 - parity) * pairs, pairs)],
        dst_ref=recv_pair,
        send_sem=send_pair,
        recv_sem=got_pair,
        device_id=(partner, col),
        device_id_type=MESH_ID,
    )
    swap.start()
    swap.wait()

    def combine_pair(j, carry):
        mine = part[parity * pairs + j]
        theirs = recv_pair[j]
        first = parity == 0
        front = jnp.where(first, mine, theirs)
        back = jnp.where(first, theirs, mine)
        mixed[j] = merge(front, back, share, halves)
        return carry

    lax.fori_loop(0, pairs, combine_pair, 0, unroll=True)

    def link(j, slot):
        return pltpu.make_async_remote_copy(
            src_ref=mixed.at[j],
            dst_ref=recv.at[slot],
            send_sem=send_sems.at[j],
            recv_sem=recv_sems.at[slot],
            device_id=(2 * j + parity, col),
            device_id_type=MESH_ID,
        )

    def send(i, carry):
        link(lax.rem(chip + i, pairs), chip).start()
        return carry

    lax.fori_loop(1, pairs, send, 0)
    own = pltpu.make_async_copy(mixed.at[chip], recv.at[chip], local_sem)
    own.start()
    own.wait()

    def finish(i, carry):
        j = lax.rem(chip + i, pairs)
        link(j, j).wait_send()
        link(j, j).wait_recv()
        return carry

    lax.fori_loop(1, pairs, finish, 0)
    colour_ref[...] = recv[...]


def finish_kernel(share, halves, recv_ref, colour_ref, transmit_ref):
    pairs = recv_ref.shape[0]
    cols = colour_ref.shape[-1]
    zero = jnp.zeros((share * halves, 128), jnp.float32)

    def value(block, k):
        pieces = [block[(r * 4 + k) * halves:(r * 4 + k + 1) * halves] for r in range(share)]
        return pieces[0] if share == 1 else jnp.concatenate(pieces, axis=0)

    def accumulate(d, carry):
        front, c0, c1, c2 = carry
        block = recv_ref[d]
        seen = jnp.exp(-front)
        return (
            front + value(block, 3),
            c0 + value(block, 0) * seen,
            c1 + value(block, 1) * seen,
            c2 + value(block, 2) * seen,
        )

    front, c0, c1, c2 = lax.fori_loop(0, pairs, accumulate, (zero, zero, zero, zero), unroll=True)
    for k, c in enumerate((c0, c1, c2)):
        colour_ref[k] = c.reshape(share, cols)
    transmit_ref[...] = jnp.exp(-front).reshape(share, cols)


def finish(gathered, share, cols):
    vmem = pltpu.MemorySpace.VMEM
    return pl.pallas_call(
        functools.partial(finish_kernel, share, cols // 128),
        out_shape=(
            jax.ShapeDtypeStruct((3, share, cols), jnp.float32),
            jax.ShapeDtypeStruct((share, cols), jnp.float32),
        ),
        in_specs=[pl.BlockSpec(memory_space=vmem)],
        out_specs=(pl.BlockSpec(memory_space=vmem), pl.BlockSpec(memory_space=vmem)),
    )(gathered)


def march(density, front, back, left, right, absorb, n):
    depth, rows, cols = density.shape
    share = rows // n
    tiles = (n, share * 4 * cols // 128, 128)
    half_tiles = (n // 2,) + tiles[1:]
    vmem = pltpu.MemorySpace.VMEM
    return pl.pallas_call(
        functools.partial(march_kernel, depth - 1, n),
        out_shape=jax.ShapeDtypeStruct(half_tiles, jnp.float32),
        in_specs=[pl.BlockSpec(memory_space=pl.ANY)] + [pl.BlockSpec(memory_space=vmem)] * 5,
        out_specs=pl.BlockSpec(memory_space=vmem),
        scratch_shapes=[
            pltpu.VMEM((4, rows, cols), jnp.float32),
            pltpu.VMEM(tiles, jnp.float32),
            pltpu.VMEM(half_tiles, jnp.float32),
            pltpu.VMEM(half_tiles, jnp.float32),
            pltpu.VMEM(half_tiles, jnp.float32),
            pltpu.SemaphoreType.DMA,
            pltpu.SemaphoreType.DMA,
            pltpu.SemaphoreType.DMA((n // 2,)),
            pltpu.SemaphoreType.DMA((n // 2,)),
            pltpu.SemaphoreType.DMA,
            pltpu.VMEM((depth, rows, cols), jnp.float32),
            pltpu.SemaphoreType.DMA((8 if depth % 8 == 0 else 1,)),
        ],
        compiler_params=pltpu.CompilerParams(collective_id=0, has_side_effects=True),
    )(density, front, back, left, right, absorb)


def halo_kernel(dens_hbm, front_ref, back_ref, left_ref, right_ref,
                dens_ref, first_col, last_col, lands, send_sems, recv_sems, load_sems):
    depth, rows, cols = dens_ref.shape
    nx, ny = lax.axis_size("gx"), lax.axis_size("gy")
    gx, gy = lax.axis_index("gx"), lax.axis_index("gy")
    ahead_x, behind_x = lax.rem(gx + 1, nx), lax.rem(gx + nx - 1, nx)
    ahead_y, behind_y = lax.rem(gy + 1, ny), lax.rem(gy + ny - 1, ny)
    barrier = pltpu.get_barrier_semaphore()
    for peer in ((ahead_x, gy), (behind_x, gy), (gx, ahead_y), (gx, behind_y)):
        pl.semaphore_signal(barrier, inc=1, device_id=peer, device_id_type=MESH_ID)
    group = rows // load_sems.shape[0]
    loads = [
        pltpu.make_async_copy(
            dens_hbm.at[:, pl.ds(g * group, group)], dens_ref.at[:, pl.ds(g * group, group)], load_sems.at[g]
        )
        for g in range(load_sems.shape[0])
    ]
    for load in loads:
        load.start()
    for z in range(rows):
        if z % group == 0:
            loads[z // group].wait()
        low = jnp.transpose(dens_ref[:, z, 0:128])
        high = jnp.transpose(dens_ref[:, z, cols - 128:cols])
        first_col[z:z + 1, :] = low[0:1, :]
        last_col[z:z + 1, :] = high[127:128, :]
    pl.semaphore_wait(barrier, 4)
    front_land, back_land, left_land, right_land = lands
    copies = [
        (dens_hbm.at[depth - 1], front_land, (ahead_x, gy)),
        (dens_hbm.at[0], back_land, (behind_x, gy)),
        (last_col, left_land, (gx, ahead_y)),
        (first_col, right_land, (gx, behind_y)),
    ]
    started = []
    for i, (src, dst, peer) in enumerate(copies):
        copy = pltpu.make_async_remote_copy(
            src_ref=src, dst_ref=dst, send_sem=send_sems.at[i], recv_sem=recv_sems.at[i],
            device_id=peer, device_id_type=MESH_ID,
        )
        copy.start()
        started.append(copy)
    for copy in started:
        copy.wait()
    front_ref[...] = jnp.where(gx == 0, 0.0, front_land[...])
    back_ref[...] = jnp.where(gx == nx - 1, 0.0, back_land[...])
    left_ref[...] = jnp.where(gy == 0, 0.0, left_land[...])
    right_ref[...] = jnp.where(gy == ny - 1, 0.0, right_land[...])


def halos(density):
    depth, rows, cols = density.shape
    vmem = pltpu.MemorySpace.VMEM
    plane = jax.ShapeDtypeStruct((rows, cols), jnp.float32)
    column = jax.ShapeDtypeStruct((rows, depth), jnp.float32)
    return pl.pallas_call(
        halo_kernel,
        out_shape=(plane, plane, column, column),
        in_specs=[pl.BlockSpec(memory_space=pl.ANY)],
        out_specs=tuple(pl.BlockSpec(memory_space=vmem) for _ in range(4)),
        scratch_shapes=[
            pltpu.VMEM((depth, rows, cols), jnp.float32),
            pltpu.VMEM((rows, depth), jnp.float32),
            pltpu.VMEM((rows, depth), jnp.float32),
            (
                pltpu.VMEM((rows, cols), jnp.float32),
                pltpu.VMEM((rows, cols), jnp.float32),
                pltpu.VMEM((rows, depth), jnp.float32),
                pltpu.VMEM((rows, depth), jnp.float32),
            ),
            pltpu.SemaphoreType.DMA((4,)),
            pltpu.SemaphoreType.DMA((4,)),
            pltpu.SemaphoreType.DMA((rows // 8 if rows % 8 == 0 else 1,)),
        ],
        compiler_params=pltpu.CompilerParams(collective_id=1, has_side_effects=True),
    )(density)


def local(density, absorb):
    front, back, left, right = halos(density)
    n = lax.axis_size("gx")
    gathered = march(density, front, back, left, right, absorb, n)
    return finish(gathered, density.shape[1] // n, density.shape[2])


def solution(mesh):
    placed = (P("gx", None, "gy"), P(None, "gy"))
    return jax.shard_map(
        local,
        mesh=mesh,
        in_specs=placed,
        out_specs=(P(None, "gx", "gy"), P("gx", "gy")),
        check_vma=False,
    )
```
